32 devices in a mesh: dp: 8 (over z, core), ctx: 4 (over y, x).
Axes of the slice: x: 2, y: 2, z: 4, core: 2. Of those that a mesh axis runs over, the one named last changes fastest.
Arguments:
- video: bfloat16 [64, 32, 64, 128], P('dp', 'ctx'), parts along dimension 0, may hold values from -6 to 6
- conv_weight: bfloat16 [3, 3, 3, 128, 256], replicated, may hold values from -0.109375 to 0.109375
- latent_weight: bfloat16 [256, 16], replicated, may hold values from -0.375 to 0.375
- embed_weight: bfloat16 [64, 3072], replicated, may hold values from -0.75 to 0.75
- modulation: float32 [32, 3072], P('dp'), parts along dimension 0, may hold values from -3 to 3
- qkv_weight: bfloat16 [3072, 3, 2048], P(None, None, 'ctx'), may hold values from -0.109375 to 0.109375
- qk_gain: float32 [2, 128], replicated, may hold values from 0.5 to 2
- text: bfloat16 [2048, 3072], P('dp'), parts along dimension 0, may hold values from -6 to 6
- text_weight: bfloat16 [3072, 2, 2048], P(None, None, 'ctx'), may hold values from -0.109375 to 0.109375
Outputs:
- attended: bfloat16 [8192, 2048], P(('dp', 'ctx')), parts along dimension 0
The draws below stay inside these ranges and needn't reach their ends.
There are 8 independent parts, one for each index of `dp`. The reference program is written for one: setup_inputs(seed, part) draws one part's arguments, and reference() takes and returns one part's arrays. A program takes and returns all parts, laid end to end along the dimension named above; an argument that names none is the same for every part. Nothing has to cross between parts.
All inputs are finite; a program needn't handle non-finite values.
Results may differ from the reference program's by a relative error of at most 0.0074.
Values may be sent and summed in bfloat16 or wider, within the bound.
No kernel may reach another device: no remote copies, remote signals or barrier semaphores. Data moves between devices by JAX's collectives and lax.ppermute only.
A program may use at most 128 MiB of HBM per device.

```python
import math
import jax
import jax.numpy as jnp
from jax import lax

C_IN = 128
C_MID = 256
LAT = 16
D = 3072
HEADS = 16
HS = 128
TXT = 256
FR = 8
W = 64
H = 32
PI = 64
TOKENS = 1024
HD = 2048


def levels(own_key, dims, pieces, low, high):
    level = 1.0
    for axis_at, parts in pieces:
        steps = jax.random.uniform(jax.random.fold_in(jax.random.fold_in(own_key, 6), axis_at), (parts,), jnp.float32, low / len(pieces), high / len(pieces))
        level = level * jnp.repeat(jnp.exp(steps), dims[axis_at] // parts).reshape((-1,) + (1,) * (len(dims) - 1 - axis_at))
    return level


def scatter_about(rng, shape, scale, reach, pieces=(), held_as=jnp.bfloat16):
    factor_of = levels(rng, shape, pieces, -0.22, 0.18) if pieces else 1.0
    values = jax.random.normal(rng, shape, jnp.float32) * scale * factor_of
    return jnp.minimum(jnp.maximum(values, -reach), reach).astype(held_as)


def setup_inputs(seed: int = 0, part: int = 0) -> dict:
    splits = jax.random.split(jax.random.key(seed), 10)
    part_splits = jax.random.split(jax.random.fold_in(splits[9], part), 10)
    video = scatter_about(part_splits[0], (FR, H, W, C_IN), 1.0, 6.0, ((1, 4),))
    conv_weight = scatter_about(splits[1], (3, 3, 3, C_IN, C_MID), (27 * C_IN) ** -0.5, 0.109375)
    latent_weight = scatter_about(splits[2], (C_MID, LAT), C_MID ** -0.5, 0.375)
    embed_weight = scatter_about(splits[3], (PI, D), PI ** -0.5, 0.75)
    modulation = scatter_about(part_splits[4], (4, D), 0.5, 3.0, (), jnp.float32)
    qkv_weight = scatter_about(splits[5], (D, 3, HD), D ** -0.5, 0.109375, ((2, 4),))
    qk_gain = jnp.clip(jnp.exp(jax.random.uniform(splits[6], (2, HS), jnp.float32, math.log(0.5), math.log(2.0))), 0.5, 2.0)
    text = scatter_about(part_splits[7], (TXT, D), 1.0, 6.0)
    text_weight = scatter_about(splits[8], (D, 2, HD), D ** -0.5, 0.109375, ((2, 4),))
    return dict(video=video, conv_weight=conv_weight, latent_weight=latent_weight, embed_weight=embed_weight, modulation=modulation, qkv_weight=qkv_weight, qk_gain=qk_gain, text=text, text_weight=text_weight)


def layer_norm(values):
    centred = values - lax.optimization_barrier(jnp.mean(values, -1, keepdims=True))
    return centred * lax.rsqrt(lax.optimization_barrier(jnp.mean(centred * centred, -1, keepdims=True)) + 1e-06)

def head_norm(values, gain):
    return values * lax.rsqrt(lax.optimization_barrier(jnp.mean(values * values, -1, keepdims=True)) + 1e-06) * gain

def patchify(latent):
    frames, rows, cols, chans = latent.shape
    shaped = latent.reshape(frames, rows // 2, 2, cols // 2, 2, chans)
    return shaped.transpose(0, 1, 3, 2, 4, 5).reshape(frames * (rows // 2) * (cols // 2), 4 * chans)

def reference(video, conv_weight, latent_weight, embed_weight, modulation, qkv_weight, qk_gain, text, text_weight):
    padded = jnp.pad(video, ((0, 0), (1, 0), (1, 0), (0, 0)))
    padded = jnp.concatenate([padded[:1], padded[:1], padded], 0)
    conv = lax.conv_general_dilated(padded[None], conv_weight, (1, 2, 2), 'VALID', dimension_numbers=('NDHWC', 'DHWIO', 'NDHWC'), preferred_element_type=jnp.float32)[0]
    activated = jax.nn.silu(conv).astype(jnp.bfloat16)
    latent = jnp.dot(activated, latent_weight, preferred_element_type=jnp.float32).astype(jnp.bfloat16)
    patches = patchify(latent)
    embedded = jnp.dot(patches, embed_weight, preferred_element_type=jnp.float32)
    stream = (layer_norm(embedded) * (1.0 + modulation[1]) + modulation[0]).astype(jnp.bfloat16)
    text_stream = (layer_norm(text.astype(jnp.float32)) * (1.0 + modulation[3]) + modulation[2]).astype(jnp.bfloat16)
    projected = jnp.dot(stream, qkv_weight.reshape(D, 3 * HD), preferred_element_type=jnp.float32)
    projected = projected.reshape(TOKENS, 3, HEADS, HS)
    queries = head_norm(projected[:, 0], qk_gain[0]).astype(jnp.bfloat16)
    keys = head_norm(projected[:, 1], qk_gain[1]).astype(jnp.bfloat16)
    values = projected[:, 2].astype(jnp.bfloat16)
    text_projected = jnp.dot(text_stream, text_weight.reshape(D, 2 * HD), preferred_element_type=jnp.float32)
    text_projected = text_projected.reshape(TXT, 2, HEADS, HS)
    text_keys = head_norm(text_projected[:, 0], qk_gain[1]).astype(jnp.bfloat16)
    text_values = text_projected[:, 1].astype(jnp.bfloat16)
    all_keys = jnp.concatenate([text_keys, keys], 0).transpose(1, 0, 2)
    all_values = jnp.concatenate([text_values, values], 0).transpose(1, 0, 2)
    scale = 1.0 / math.sqrt(HS)

    def one_head(operands):
        query_head, key_head, value_head = operands
        logits = jnp.dot(query_head, key_head.T, preferred_element_type=jnp.float32) * scale
        expd = jnp.exp(logits - lax.optimization_barrier(jnp.max(logits, -1, keepdims=True)))
        weights = (expd / lax.optimization_barrier(jnp.sum(expd, -1, keepdims=True))).astype(jnp.bfloat16)
        return jnp.dot(weights, value_head, preferred_element_type=jnp.float32).astype(jnp.bfloat16)
    heads_out = lax.map(one_head, (queries.transpose(1, 0, 2), all_keys, all_values))
    return heads_out.transpose(1, 0, 2).reshape(TOKENS, HD)
```

```python
import math

import jax
import jax.numpy as jnp
from jax import lax
from jax.experimental import pallas as pl
from jax.experimental.pallas import tpu as pltpu
from jax.sharding import PartitionSpec as P

HS = 128
EPS = 1e-06
F32 = jnp.float32
BF16 = jnp.bfloat16
VMEM = pltpu.VMEM
VMEM_LIMIT = 56 * 1024 * 1024


def vmem_spec():
    return pl.BlockSpec(memory_space=pltpu.VMEM)


def hbm_spec():
    return pl.BlockSpec(memory_space=pl.ANY)


def smem_spec():
    return pl.BlockSpec(memory_space=pltpu.SMEM)


def params():
    return pltpu.CompilerParams(vmem_limit_bytes=VMEM_LIMIT)


def cost(flops, bytes_accessed, transcendentals=0):
    return pl.CostEstimate(
        flops=int(flops), bytes_accessed=int(bytes_accessed), transcendentals=int(transcendentals)
    )


def nbytes(*arrays):
    return sum(math.prod(a.shape) * a.dtype.itemsize for a in arrays)


def split(x):
    hi = x.astype(BF16)
    return hi, (x - hi.astype(F32)).astype(BF16)


def dot(a, b):
    return jnp.dot(a, b, preferred_element_type=F32)


def dot_nt(a, b):
    return lax.dot_general(a, b, (((1,), (1,)), ((), ())), preferred_element_type=F32)


def fold_kernel(chunks, e_ref, mod_ref, w_hbm, rhs0_ref, rhs1_ref, shift_ref, gram_ref, w_buf, lhs_ref, acc_ref, sem):
    parts, depth, width = w_hbm.shape
    rows = depth // chunks

    def copy(c):
        at = pl.ds(c * rows, rows)
        return pltpu.make_async_copy(w_hbm.at[:, at], w_buf.at[:, at], sem.at[c])

    for c in range(chunks):
        copy(c).start()
    pi = e_ref.shape[0]
    e = e_ref[...].astype(F32)
    centred = e - jnp.mean(e, -1, keepdims=True)
    hi, lo = split(centred * (1.0 + mod_ref[1:2, :]))
    lhs_ref[0:pi, :] = hi
    lhs_ref[pi : 2 * pi, :] = lo
    shift_hi, shift_lo = split(mod_ref[0:1, :])
    lhs_ref[2 * pi :, :] = jnp.concatenate(
        [shift_hi.astype(F32), shift_lo.astype(F32), jnp.zeros((14, depth), F32)], 0
    ).astype(BF16)
    chi, clo = split(jnp.concatenate([centred, centred], 0))
    gram = dot_nt(chi, chi) + dot_nt(chi, clo) + dot_nt(clo, chi)
    row = lax.broadcasted_iota(jnp.int32, gram.shape, 0) // pi
    col = lax.broadcasted_iota(jnp.int32, gram.shape, 1) // pi
    ghi, glo = split(jnp.where(row == col, gram * (1.0 / depth), 0.0))
    gram_ref[...] = jnp.concatenate([ghi, glo], 0)
    for c in range(chunks):
        copy(c).wait()
        lhs = lhs_ref[:, c * rows : (c + 1) * rows]
        for p in range(parts):
            at = slice(p * width, (p + 1) * width)
            term = dot(lhs, w_buf[p, c * rows : (c + 1) * rows, :])
            if c == 0:
                acc_ref[:, at] = term
            else:
                acc_ref[:, at] += term
    total = acc_ref[...]
    hi, lo = split(total[:pi] + total[pi : 2 * pi])
    none = jnp.zeros_like(hi)
    rhs0_ref[...] = jnp.concatenate([hi, none, lo, none], 0)
    rhs1_ref[...] = jnp.concatenate([none, hi, none, lo], 0)
    shift_ref[...] = total[2 * pi : 2 * pi + 1] + total[2 * pi + 1 : 2 * pi + 2]


def fold(embed_weight, modulation, weight):
    parts, depth, width = weight.shape
    pi = embed_weight.shape[0]
    cols = parts * width
    chunks = 6
    return pl.pallas_call(
        lambda *refs: fold_kernel(chunks, *refs),
        out_shape=(
            jax.ShapeDtypeStruct((4 * pi, cols), BF16),
            jax.ShapeDtypeStruct((4 * pi, cols), BF16),
            jax.ShapeDtypeStruct((1, cols), F32),
            jax.ShapeDtypeStruct((4 * pi, 2 * pi), BF16),
        ),
        in_specs=[vmem_spec(), vmem_spec(), hbm_spec()],
        out_specs=(vmem_spec(),) * 4,
        scratch_shapes=[
            VMEM((parts, depth, width), BF16),
            VMEM((2 * pi + 16, depth), BF16),
            VMEM((2 * pi + 16, cols), F32),
            pltpu.SemaphoreType.DMA((chunks,)),
        ],
        compiler_params=params(),
        cost_estimate=cost(2 * 144 * depth * cols, nbytes(weight, embed_weight, modulation)),
        name="fold",
    )(embed_weight, modulation, weight)


def text_kernel(chunks, text_ref, mod_ref, gain_ref, w_hbm, key_ref, value_ref, w_buf, stream_ref, acc_ref, sem):
    depth, parts, width = w_hbm.shape
    rows = depth // chunks

    def copy(c):
        at = pl.ds(c * rows, rows)
        return pltpu.make_async_copy(w_hbm.at[at], w_buf.at[at], sem.at[c])

    for c in range(chunks):
        copy(c).start()
    text = text_ref[...].astype(F32)
    centred = text - jnp.mean(text, -1, keepdims=True)
    normed = centred * lax.rsqrt(jnp.mean(centred * centred, -1, keepdims=True) + EPS)
    stream_ref[...] = (normed * (1.0 + mod_ref[3:4, :]) + mod_ref[2:3, :]).astype(BF16)
    step = 128
    row = lax.broadcasted_iota(jnp.int32, (2 * step, 2 * step), 0)
    col = lax.broadcasted_iota(jnp.int32, (2 * step, 2 * step), 1)
    pick = jnp.where(col == 2 * (row % step) + row // step, 1.0, 0.0).astype(BF16)
    flat = w_buf.reshape(depth * parts, width)
    for c in range(chunks):
        copy(c).wait()
        pieces = ([], [])
        for s in range(rows // step):
            at = 2 * (c * rows + s * step)
            both = dot(pick, flat[at : at + 2 * step, :]).astype(BF16)
            pieces[0].append(both[:step])
            pieces[1].append(both[step:])
        stream = stream_ref[:, c * rows : (c + 1) * rows]
        for p in range(2):
            term = dot(stream, jnp.concatenate(pieces[p], 0))
            if c == 0:
                acc_ref[p] = term
            else:
                acc_ref[p] += term
    for h in range(width // HS):
        at = slice(h * HS, (h + 1) * HS)
        key = acc_ref[0, :, at]
        scale = lax.rsqrt(jnp.mean(key * key, -1, keepdims=True) + EPS)
        key_ref[h] = (key * scale * gain_ref[1:2, :]).astype(BF16)
        value_ref[h] = acc_ref[1, :, at].astype(BF16)


def text_side(text, modulation, gain, weight):
    depth, parts, width = weight.shape
    count = text.shape[0]
    heads = width // HS
    chunks = 6
    return pl.pallas_call(
        lambda *refs: text_kernel(chunks, *refs),
        out_shape=(jax.ShapeDtypeStruct((heads, count, HS), BF16),) * 2,
        in_specs=[vmem_spec(), vmem_spec(), vmem_spec(), hbm_spec()],
        out_specs=(vmem_spec(),) * 2,
        scratch_shapes=[
            VMEM((depth, parts, width), BF16),
            VMEM((count, depth), BF16),
            VMEM((parts, count, width), F32),
            pltpu.SemaphoreType.DMA((chunks,)),
        ],
        compiler_params=params(),
        cost_estimate=cost(4 * count * depth * parts * width, nbytes(weight, text, modulation)),
        name="text_side",
    )(text, modulation, gain, weight)


def conv_kernel(video_ref, halo_ref, weight_ref, latent_ref, out_ref, wide_ref, even_ref, odd_ref, left_ref, spread_ref):
    frames, rows, cols, chans = video_ref.shape
    block = cols + 8
    half = cols // 2
    quarter = cols // 4
    for r in range(rows + 1):
        for f in range(frames):
            base = (r * frames + f) * block
            pixels = halo_ref[f, 0] if r == 0 else video_ref[f, r - 1]
            wide_ref[base : base + 8, :] = jnp.zeros((8, chans), F32)
            wide_ref[base + 8 : base + block, :] = pixels.astype(F32)
            at = [wide_ref[pl.ds(base + 7 + o, quarter, stride=4), :] for o in range(5)]
            even = jnp.concatenate([at[1], at[3]], 0).astype(BF16)
            odd = jnp.concatenate([at[2], at[4]], 0).astype(BF16)
            left = jnp.concatenate([at[0], at[2]], 0).astype(BF16)
            for t in (range(3) if f == 0 else (f + 2,)):
                even_ref[r, t] = even
                odd_ref[r, t] = odd
                left_ref[r, t] = left
    lat, mid = latent_ref.shape
    tall = rows // 2
    spread_ref[...] = jnp.zeros_like(spread_ref)
    for s in range(2 * tall):
        spread_ref[s * lat : (s + 1) * lat, s * mid : (s + 1) * mid] = latent_ref[...]
    pieces = []
    for j in range(tall):
        taps = []
        for kt in range(3):
            for kr in range(3):
                for ref in (left_ref, even_ref, odd_ref):
                    taps.append(ref[2 * j + kr, kt : kt + frames].reshape(frames * half, chans))
        conv = dot(jnp.concatenate(taps, 1), weight_ref[...])
        act = (conv * (1.0 / (1.0 + jnp.exp(-conv)))).astype(BF16)
        for b in range(2):
            pieces.append(
                jnp.concatenate(
                    [act[f * half + b * quarter : f * half + (b + 1) * quarter] for f in range(frames)], 0
                )
            )
    out_ref[...] = dot_nt(jnp.concatenate(pieces, 1), spread_ref[...]).astype(BF16)


def conv_side(video, halo, conv_weight, latent_weight):
    frames, rows, cols, chans = video.shape
    mid = conv_weight.shape[-1]
    lat = latent_weight.shape[1]
    weight = conv_weight.reshape(-1, mid)
    latent = latent_weight.T
    half = cols // 2
    tall = rows // 2
    return pl.pallas_call(
        conv_kernel,
        out_shape=jax.ShapeDtypeStruct((frames * half // 2, 2 * tall * lat), BF16),
        in_specs=[vmem_spec()] * 4,
        out_specs=vmem_spec(),
        scratch_shapes=[VMEM(((rows + 1) * frames * (cols + 8), chans), F32)]
        + [VMEM((rows + 1, frames + 2, half, chans), BF16)] * 3
        + [VMEM((2 * tall * lat, 2 * tall * mid), BF16)],
        compiler_params=params(),
        cost_estimate=cost(2 * frames * tall * half * 27 * chans * mid, nbytes(video, halo, weight)),
        name="conv_side",
    )(video, halo, weight, latent)


def qkv_kernel(order, frames, *refs):
    n = len(order)
    me_ref = refs[0]
    patch_refs = refs[1 : 1 + n]
    rhs_refs = refs[1 + n : 3 + n]
    shift_ref, gram_ref, gain_ref, tkey_ref, tvalue_ref = refs[3 + n : 8 + n]
    query_refs = refs[8 + n : 8 + 2 * n]
    key_ref, value_ref, patch_scr = refs[8 + 2 * n :]
    me = me_ref[0]
    heads, count, _ = tkey_ref.shape
    rows = patch_refs[0].shape[0]
    for k, ref in zip(order, patch_refs):
        patch_scr[pl.ds(pl.multiple_of((me ^ k) * rows, rows), rows), :] = ref[...]
    for h in range(heads):
        key_ref[h, 0:count, :] = tkey_ref[h]
        value_ref[h, 0:count, :] = tvalue_ref[h]
    own = frames // n
    span = rows // n
    grain = span // own
    pieces = []
    for k in order:
        for s in range(n):
            at = pl.multiple_of((me ^ k) * span, span) + s * rows
            pieces.append(patch_scr[pl.ds(pl.multiple_of(at, span), span), :])
    x = jnp.concatenate(pieces, 0)
    xx = jnp.concatenate([x, x], 1)
    quad = dot(xx, gram_ref[...]) * x.astype(F32)
    lane = lax.broadcasted_iota(jnp.int32, quad.shape, 1)
    low = lane < quad.shape[1] // 2
    width = heads * HS
    gain_q = gain_ref[0:1, :] * (math.log2(math.e) / math.sqrt(HS))
    gain_k = gain_ref[1:2, :]
    for i in range(2):
        var = jnp.sum(jnp.where(low if i == 0 else ~low, quad, 0.0), -1, keepdims=True)
        rstd = lax.rsqrt(jnp.maximum(var, 0.0) + EPS)
        for p in range(3):
            for h0 in range(0, heads, 2):
                at = slice(p * width + h0 * HS, p * width + (h0 + 2) * HS)
                pair = dot(xx, rhs_refs[i][:, at]) * rstd + shift_ref[:, at]
                for h in (h0, h0 + 1):
                    v = pair[:, (h - h0) * HS : (h - h0 + 1) * HS]
                    if p < 2:
                        v = v * lax.rsqrt(jnp.mean(v * v, -1, keepdims=True) + EPS)
                        v = v * (gain_q if p == 0 else gain_k)
                    v = v.astype(BF16)
                    for k in range(n):
                        block = v[k * rows : (k + 1) * rows]
                        if p == 0:
                            for s in range(n):
                                for f in range(own):
                                    to = f * (n * 2 * grain) + (s * 2 + i) * grain
                                    come = s * span + f * grain
                                    query_refs[k][h, to : to + grain, :] = block[come : come + grain]
                        else:
                            ref = key_ref if p == 1 else value_ref
                            to = count + (2 * k + i) * rows
                            ref[h, to : to + rows, :] = block


def qkv_side(order, frames, me, patches, rhs0, rhs1, shift, gram, gain, tkey, tvalue):
    n = len(order)
    heads, count, _ = tkey.shape
    rows = patches[0].shape[0]
    total = count + 2 * n * rows
    outs = pl.pallas_call(
        lambda *refs: qkv_kernel(order, frames, *refs),
        out_shape=(jax.ShapeDtypeStruct((heads, 2 * rows, HS), BF16),) * n
        + (jax.ShapeDtypeStruct((heads, total, HS), BF16),) * 2,
        in_specs=[smem_spec()] + [vmem_spec()] * (n + 7),
        out_specs=(vmem_spec(),) * (n + 2),
        scratch_shapes=[VMEM((n * rows, rows), BF16)],
        compiler_params=params(),
        cost_estimate=cost(2 * 2 * n * rows * 256 * 3 * heads * HS, 4 * nbytes(rhs0)),
        name="qkv_side",
    )(me, *patches, rhs0, rhs1, shift, gram, gain, tkey, tvalue)
    return outs[:n], outs[n], outs[n + 1]


def attend_kernel(query_ref, key_ref, value_ref, out_ref):
    heads, total, _ = key_ref.shape
    step = 256
    for h in range(heads):
        query = query_ref[h]
        acc = None
        for c in range(0, total, step):
            logits = dot_nt(query, key_ref[h, c : c + step, :])
            weights = jnp.exp2(logits)
            fold_sum = weights[:, :HS] + weights[:, HS:]
            term = dot(weights.astype(BF16), value_ref[h, c : c + step, :])
            if acc is None:
                acc, norm = term, fold_sum
            else:
                acc, norm = acc + term, norm + fold_sum
        norm = jnp.sum(norm, -1, keepdims=True)
        out_ref[:, h * HS : (h + 1) * HS] = (acc / norm).astype(BF16)


def attend(query, key, value):
    heads, rows, _ = query.shape
    total = key.shape[1]
    return pl.pallas_call(
        attend_kernel,
        out_shape=jax.ShapeDtypeStruct((rows, heads * HS), BF16),
        in_specs=[vmem_spec()] * 3,
        out_specs=vmem_spec(),
        compiler_params=params(),
        cost_estimate=cost(
            4 * heads * rows * total * HS, nbytes(query, key, value), heads * rows * total
        ),
        name="attend",
    )(query, key, value)


def gather_kernel(order, me_ref, *refs):
    n = len(order)
    out_ref, sem = refs[n:]
    width = refs[0].shape[1]
    copies = []
    for j, k in enumerate(order):
        at = pl.multiple_of((me_ref[0] ^ k) * width, width)
        copies.append(pltpu.make_async_copy(refs[j], out_ref.at[:, pl.ds(at, width)], sem.at[j]))
    for c in copies:
        c.start()
    for c in copies:
        c.wait()


def side_by_side(order, me, blocks):
    n = len(order)
    rows, width = blocks[0].shape
    return pl.pallas_call(
        lambda *refs: gather_kernel(order, *refs),
        out_shape=jax.ShapeDtypeStruct((rows, n * width), BF16),
        in_specs=[smem_spec()] + [hbm_spec()] * n,
        out_specs=hbm_spec(),
        scratch_shapes=[pltpu.SemaphoreType.DMA((n,))],
        cost_estimate=cost(0, 2 * n * nbytes(blocks[0])),
        name="side_by_side",
    )(me, *blocks)


def shards(video, conv_weight, latent_weight, embed_weight, modulation, qkv_weight, qk_gain, text, text_weight):
    n = lax.axis_size("ctx")
    frames = video.shape[0]
    me = lax.axis_index("ctx").astype(jnp.int32).reshape(1)

    def swap(x, k):
        return lax.ppermute(x, "ctx", [(i, i ^ k) for i in range(n)])

    halo = lax.ppermute(video[:, -1:], "ctx", [(i, i + 1) for i in range(n - 1)])
    rhs0, rhs1, shift, gram = fold(embed_weight, modulation, qkv_weight.transpose(1, 0, 2))
    patches = conv_side(video, halo, conv_weight, latent_weight)
    order = tuple(range(n - 1, -1, -1))
    received = [swap(patches, k) if k else patches for k in order]
    tkey, tvalue = text_side(text, modulation, qk_gain, text_weight)
    queries, key, value = qkv_side(
        order, frames, me, received, rhs0, rhs1, shift, gram, qk_gain, tkey, tvalue
    )
    blocks = []
    for query, k in zip(queries, order):
        block = attend(query, key, value)
        blocks.append(swap(block, k) if k else block)
    return side_by_side(order, me, blocks)


def solution(mesh):
    in_specs = (
        P("dp", "ctx", None, None),
        P(),
        P(),
        P(),
        P("dp", None),
        P(None, None, "ctx"),
        P(),
        P("dp", None),
        P(None, None, "ctx"),
    )
    out_specs = P(("dp", "ctx"), None)
    return jax.shard_map(shards, mesh=mesh, in_specs=in_specs, out_specs=out_specs, check_vma=False)
```

```python
import math

import jax
import jax.numpy as jnp
from jax import lax
from jax.experimental import pallas as pl
from jax.experimental.pallas import tpu as pltpu
from jax.sharding import PartitionSpec as P

HS = 128
EPS = 1e-06
F32 = jnp.float32
BF16 = jnp.bfloat16
VMEM = pltpu.VMEM
MIB = 1024 * 1024


def vmem_spec():
    return pl.BlockSpec(memory_space=pltpu.VMEM)


def hbm_spec():
    return pl.BlockSpec(memory_space=pltpu.HBM)


def smem_spec():
    return pl.BlockSpec(memory_space=pltpu.SMEM)


def params(mib):
    return pltpu.CompilerParams(vmem_limit_bytes=mib * MIB)


def cost(flops, bytes_accessed, transcendentals=0):
    return pl.CostEstimate(
        flops=int(flops), bytes_accessed=int(bytes_accessed), transcendentals=int(transcendentals)
    )


def nbytes(*arrays):
    return sum(math.prod(a.shape) * a.dtype.itemsize for a in arrays)


def split(x):
    hi = x.astype(BF16)
    return hi, (x - hi.astype(F32)).astype(BF16)


def dot(a, b):
    return jnp.dot(a, b, preferred_element_type=F32)


def dot_nt(a, b):
    return lax.dot_general(a, b, (((1,), (1,)), ((), ())), preferred_element_type=F32)


def fold_kernel(
    chunks,
    e_hbm,
    mod_hbm,
    w_hbm,
    text_hbm,
    video_hbm,
    conv_hbm,
    rhs0_ref,
    rhs1_ref,
    shift_ref,
    gram_ref,
    stream_ref,
    video_ref,
    conv_ref,
    e_ref,
    mod_ref,
    text_ref,
    w_buf,
    lhs_ref,
    acc_ref,
    sem,
    w_sem,
):
    parts, depth, width = w_hbm.shape
    rows = depth // chunks
    small = [
        pltpu.make_async_copy(src, dst, sem.at[i])
        for i, (src, dst) in enumerate(
            (
                (e_hbm, e_ref),
                (mod_hbm, mod_ref),
                (text_hbm, text_ref),
                (video_hbm, video_ref),
                (conv_hbm, conv_ref),
            )
        )
    ]

    def copy(c):
        at = pl.ds(c * rows, rows)
        return pltpu.make_async_copy(w_hbm.at[:, at], w_buf.at[:, at], w_sem.at[c])

    small[0].start()
    small[1].start()
    for c in range(chunks):
        copy(c).start()
    for c in small[2:]:
        c.start()
    small[0].wait()
    small[1].wait()
    pi = e_ref.shape[0]
    e = e_ref[...].astype(F32)
    centred = e - jnp.mean(e, -1, keepdims=True)
    hi, lo = split(centred * (1.0 + mod_ref[1:2, :]))
    lhs_ref[0:pi, :] = hi
    lhs_ref[pi : 2 * pi, :] = lo
    shift_hi, shift_lo = split(mod_ref[0:1, :])
    lhs_ref[2 * pi :, :] = jnp.concatenate(
        [shift_hi.astype(F32), shift_lo.astype(F32), jnp.zeros((14, depth), F32)], 0
    ).astype(BF16)
    chi, clo = split(jnp.concatenate([centred, centred], 0))
    gram = dot_nt(chi, chi) + dot_nt(chi, clo) + dot_nt(clo, chi)
    row = lax.broadcasted_iota(jnp.int32, gram.shape, 0) // pi
    col = lax.broadcasted_iota(jnp.int32, gram.shape, 1) // pi
    ghi, glo = split(jnp.where(row == col, gram * (1.0 / depth), 0.0))
    gram_ref[...] = jnp.concatenate([ghi, glo], 0)
    for c in range(chunks):
        copy(c).wait()
        lhs = lhs_ref[:, c * rows : (c + 1) * rows]
        for p in range(parts):
            at = slice(p * width, (p + 1) * width)
            term = dot(lhs, w_buf[p, c * rows : (c + 1) * rows, :])
            if c == 0:
                acc_ref[:, at] = term
            else:
                acc_ref[:, at] += term
    total = acc_ref[...]
    hi, lo = split(total[:pi] + total[pi : 2 * pi])
    none = jnp.zeros_like(hi)
    rhs0_ref[...] = jnp.concatenate([hi, none, lo, none], 0)
    rhs1_ref[...] = jnp.concatenate([none, hi, none, lo], 0)
    shift_ref[...] = total[2 * pi : 2 * pi + 1] + total[2 * pi + 1 : 2 * pi + 2]
    small[2].wait()
    text = text_ref[...].astype(F32)
    centred = text - jnp.mean(text, -1, keepdims=True)
    normed = centred * lax.rsqrt(jnp.mean(centred * centred, -1, keepdims=True) + EPS)
    stream_ref[...] = (normed * (1.0 + mod_ref[3:4, :]) + mod_ref[2:3, :]).astype(BF16)
    small[3].wait()
    small[4].wait()


def fold(embed_weight, modulation, weight, text, video, conv_weight):
    parts, depth, width = weight.shape
    pi = embed_weight.shape[0]
    cols = parts * width
    chunks = 6
    return pl.pallas_call(
        lambda *refs: fold_kernel(chunks, *refs),
        out_shape=(
            jax.ShapeDtypeStruct((4 * pi, cols), BF16),
            jax.ShapeDtypeStruct((4 * pi, cols), BF16),
            jax.ShapeDtypeStruct((1, cols), F32),
            jax.ShapeDtypeStruct((4 * pi, 2 * pi), BF16),
            jax.ShapeDtypeStruct(text.shape, BF16),
            jax.ShapeDtypeStruct(video.shape, BF16),
            jax.ShapeDtypeStruct(conv_weight.shape, BF16),
        ),
        in_specs=[hbm_spec()] * 6,
        out_specs=(vmem_spec(),) * 7,
        scratch_shapes=[
            VMEM(embed_weight.shape, BF16),
            VMEM(modulation.shape, F32),
            VMEM(text.shape, BF16),
            VMEM((parts, depth, width), BF16),
            VMEM((2 * pi + 16, depth), BF16),
            VMEM((2 * pi + 16, cols), F32),
            pltpu.SemaphoreType.DMA((5,)),
            pltpu.SemaphoreType.DMA((chunks,)),
        ],
        compiler_params=params(32),
        cost_estimate=cost(
            2 * 144 * depth * cols, nbytes(weight, embed_weight, modulation, text, video, conv_weight)
        ),
        name="fold",
    )(*[pltpu.with_memory_space_constraint(a, pltpu.HBM) for a in (embed_weight, modulation, weight, text, video, conv_weight)])


def text_kernel(stream_ref, gain_ref, w_ref, key_ref, value_ref, acc_ref):
    depth, parts, width = w_ref.shape
    step = 128
    group = 4
    row = lax.broadcasted_iota(jnp.int32, (2 * step, 2 * step), 0)
    col = lax.broadcasted_iota(jnp.int32, (2 * step, 2 * step), 1)
    pick = jnp.where(col == 2 * (row % step) + row // step, 1.0, 0.0).astype(BF16)
    flat = w_ref.reshape(depth * parts, width)
    for c in range(depth // (group * step)):
        pieces = ([], [])
        for s in range(group):
            at = 2 * (c * group + s) * step
            both = dot(pick, flat[at : at + 2 * step, :]).astype(BF16)
            pieces[0].append(both[:step])
            pieces[1].append(both[step:])
        stream = stream_ref[:, c * group * step : (c + 1) * group * step]
        for p in range(2):
            term = dot(stream, jnp.concatenate(pieces[p], 0))
            if c == 0:
                acc_ref[p] = term
            else:
                acc_ref[p] += term
    for h in range(width // HS):
        at = slice(h * HS, (h + 1) * HS)
        key = acc_ref[0, :, at]
        scale = lax.rsqrt(jnp.mean(key * key, -1, keepdims=True) + EPS)
        key_ref[h] = (key * scale * gain_ref[1:2, :]).astype(BF16)
        value_ref[h] = acc_ref[1, :, at].astype(BF16)


def text_side(stream, gain, weight):
    depth, parts, width = weight.shape
    count = stream.shape[0]
    heads = width // HS
    return pl.pallas_call(
        text_kernel,
        out_shape=(jax.ShapeDtypeStruct((heads, count, HS), BF16),) * 2,
        in_specs=[vmem_spec()] * 3,
        out_specs=(vmem_spec(),) * 2,
        scratch_shapes=[VMEM((parts, count, width), F32)],
        compiler_params=params(12),
        cost_estimate=cost(4 * count * depth * parts * width, nbytes(weight, stream)),
        name="text_side",
    )(stream, gain, weight)


def conv_kernel(
    chunks,
    video_ref,
    halo_ref,
    weight_ref,
    latent_ref,
    text_hbm,
    out_ref,
    text_ref,
    wide_ref,
    even_ref,
    odd_ref,
    left_ref,
    spread_ref,
    sem,
):
    deep = text_hbm.shape[0] // chunks
    ahead = [
        pltpu.make_async_copy(text_hbm.at[pl.ds(c * deep, deep)], text_ref.at[pl.ds(c * deep, deep)], sem.at[c])
        for c in range(chunks)
    ]
    for copy in ahead:
        copy.start()
    frames, rows, cols, chans = video_ref.shape
    block = cols + 8
    half = cols // 2
    quarter = cols // 4
    for r in range(rows + 1):
        for f in range(frames):
            base = (r * frames + f) * block
            pixels = halo_ref[f, 0] if r == 0 else video_ref[f, r - 1]
            wide_ref[base : base + 8, :] = jnp.zeros((8, chans), F32)
            wide_ref[base + 8 : base + block, :] = pixels.astype(F32)
            at = [wide_ref[pl.ds(base + 7 + o, quarter, stride=4), :] for o in range(5)]
            even = jnp.concatenate([at[1], at[3]], 0).astype(BF16)
            odd = jnp.concatenate([at[2], at[4]], 0).astype(BF16)
            left = jnp.concatenate([at[0], at[2]], 0).astype(BF16)
            for t in (range(3) if f == 0 else (f + 2,)):
                even_ref[r, t] = even
                odd_ref[r, t] = odd
                left_ref[r, t] = left
    lat, mid = latent_ref.shape
    tall = rows // 2
    spread_ref[...] = jnp.zeros_like(spread_ref)
    for s in range(2 * tall):
        spread_ref[s * lat : (s + 1) * lat, s * mid : (s + 1) * mid] = latent_ref[...]
    pieces = []
    for j in range(tall):
        taps = []
        for kt in range(3):
            for kr in range(3):
                for ref in (left_ref, even_ref, odd_ref):
                    taps.append(ref[2 * j + kr, kt : kt + frames].reshape(frames * half, chans))
        conv = dot(jnp.concatenate(taps, 1), weight_ref[...])
        act = (conv * (1.0 / (1.0 + jnp.exp(-conv)))).astype(BF16)
        for b in range(2):
            pieces.append(
                jnp.concatenate(
                    [act[f * half + b * quarter : f * half + (b + 1) * quarter] for f in range(frames)], 0
                )
            )
    out_ref[...] = dot_nt(jnp.concatenate(pieces, 1), spread_ref[...]).astype(BF16)
    for copy in ahead:
        copy.wait()


def conv_side(video, halo, weight, latent_weight, text_weight):
    frames, rows, cols, chans = video.shape
    mid = weight.shape[-1]
    lat = latent_weight.shape[1]
    latent = latent_weight.T
    half = cols // 2
    tall = rows // 2
    chunks = 4
    return pl.pallas_call(
        lambda *refs: conv_kernel(chunks, *refs),
        out_shape=(
            jax.ShapeDtypeStruct((frames * half // 2, 2 * tall * lat), BF16),
            jax.ShapeDtypeStruct(text_weight.shape, BF16),
        ),
        in_specs=[vmem_spec()] * 4 + [hbm_spec()],
        out_specs=(vmem_spec(),) * 2,
        scratch_shapes=[VMEM(((rows + 1) * frames * (cols + 8), chans), F32)]
        + [VMEM((rows + 1, frames + 2, half, chans), BF16)] * 3
        + [VMEM((2 * tall * lat, 2 * tall * mid), BF16), pltpu.SemaphoreType.DMA((chunks,))],
        compiler_params=params(24),
        cost_estimate=cost(
            2 * frames * tall * half * 27 * chans * mid, nbytes(video, halo, weight, text_weight)
        ),
        name="conv_side",
    )(video, halo, weight, latent, pltpu.with_memory_space_constraint(text_weight, pltpu.HBM))


def qkv_kernel(order, frames, *refs):
    n = len(order)
    me_ref = refs[0]
    patch_refs = refs[1 : 1 + n]
    rhs_refs = refs[1 + n : 3 + n]
    shift_ref, gram_ref, gain_ref, tkey_ref, tvalue_ref = refs[3 + n : 8 + n]
    query_refs = refs[8 + n : 8 + 2 * n]
    key_ref, value_ref, patch_scr = refs[8 + 2 * n :]
    me = me_ref[0]
    heads, count, _ = tkey_ref.shape
    rows = patch_refs[0].shape[0]
    for k, ref in zip(order, patch_refs):
        patch_scr[pl.ds(pl.multiple_of((me ^ k) * rows, rows), rows), :] = ref[...]
    for h in range(heads):
        key_ref[h, 0:count, :] = tkey_ref[h]
        value_ref[h, 0:count, :] = tvalue_ref[h]
    own = frames // n
    span = rows // n
    grain = span // own
    pieces = []
    for k in order:
        for s in range(n):
            at = pl.multiple_of((me ^ k) * span, span) + s * rows
            pieces.append(patch_scr[pl.ds(pl.multiple_of(at, span), span), :])
    x = jnp.concatenate(pieces, 0)
    xx = jnp.concatenate([x, x], 1)
    quad = dot(xx, gram_ref[...]) * x.astype(F32)
    lane = lax.broadcasted_iota(jnp.int32, quad.shape, 1)
    low = lane < quad.shape[1] // 2
    width = heads * HS
    gain_q = gain_ref[0:1, :] * (math.log2(math.e) / math.sqrt(HS))
    gain_k = gain_ref[1:2, :]
    for i in range(2):
        var = jnp.sum(jnp.where(low if i == 0 else ~low, quad, 0.0), -1, keepdims=True)
        rstd = lax.rsqrt(jnp.maximum(var, 0.0) + EPS)
        for p in range(3):
            for h0 in range(0, heads, 2):
                at = slice(p * width + h0 * HS, p * width + (h0 + 2) * HS)
                pair = dot(xx, rhs_refs[i][:, at]) * rstd + shift_ref[:, at]
                for h in (h0, h0 + 1):
                    v = pair[:, (h - h0) * HS : (h - h0 + 1) * HS]
                    if p < 2:
                        v = v * lax.rsqrt(jnp.mean(v * v, -1, keepdims=True) + EPS)
                        v = v * (gain_q if p == 0 else gain_k)
                    v = v.astype(BF16)
                    for k in range(n):
                        block = v[k * rows : (k + 1) * rows]
                        if p == 0:
                            for s in range(n):
                                for f in range(own):
                                    to = f * (n * 2 * grain) + (s * 2 + i) * grain
                                    come = s * span + f * grain
                                    query_refs[k][h, to : to + grain, :] = block[come : come + grain]
                        else:
                            ref = key_ref if p == 1 else value_ref
                            to = count + (2 * k + i) * rows
                            ref[h, to : to + rows, :] = block


def qkv_side(order, frames, me, patches, rhs0, rhs1, shift, gram, gain, tkey, tvalue):
    n = len(order)
    heads, count, _ = tkey.shape
    rows = patches[0].shape[0]
    total = count + 2 * n * rows
    outs = pl.pallas_call(
        lambda *refs: qkv_kernel(order, frames, *refs),
        out_shape=(jax.ShapeDtypeStruct((heads, 2 * rows, HS), BF16),) * n
        + (jax.ShapeDtypeStruct((heads, total, HS), BF16),) * 2,
        in_specs=[smem_spec()] + [vmem_spec()] * (n + 7),
        out_specs=(vmem_spec(),) * (n + 2),
        scratch_shapes=[VMEM((n * rows, rows), BF16)],
        compiler_params=params(16),
        cost_estimate=cost(2 * 2 * n * rows * 256 * 3 * heads * HS, 4 * nbytes(rhs0)),
        name="qkv_side",
    )(me, *patches, rhs0, rhs1, shift, gram, gain, tkey, tvalue)
    return outs[:n], outs[n], outs[n + 1]


def attend_kernel(query_ref, key_ref, value_ref, out_ref):
    heads, total, _ = key_ref.shape
    for h in range(heads):
        weights = jnp.exp2(dot_nt(query_ref[h], key_ref[h]))
        norm = weights[:, :HS]
        for c in range(HS, total, HS):
            norm = norm + weights[:, c : c + HS]
        norm = jnp.sum(norm, -1, keepdims=True)
        attended = dot(weights.astype(BF16), value_ref[h])
        out_ref[:, h * HS : (h + 1) * HS] = (attended / norm).astype(BF16)


def attend(query, key, value):
    heads, rows, _ = query.shape
    total = key.shape[1]
    return pl.pallas_call(
        attend_kernel,
        out_shape=jax.ShapeDtypeStruct((rows, heads * HS), BF16),
        in_specs=[vmem_spec()] * 3,
        out_specs=vmem_spec(),
        compiler_params=params(8),
        cost_estimate=cost(heads * rows * HS, nbytes(query)),
        name="attend",
    )(query, key, value)


def gather_kernel(order, me_ref, *refs):
    n = len(order)
    out_ref, sem = refs[n:]
    width = refs[0].shape[1]
    copies = []
    for j, k in enumerate(order):
        at = pl.multiple_of((me_ref[0] ^ k) * width, width)
        copies.append(pltpu.make_async_copy(refs[j], out_ref.at[:, pl.ds(at, width)], sem.at[j]))
    for c in copies:
        c.start()
    for c in copies:
        c.wait()


def side_by_side(order, me, blocks):
    n = len(order)
    rows, width = blocks[0].shape
    return pl.pallas_call(
        lambda *refs: gather_kernel(order, *refs),
        out_shape=jax.ShapeDtypeStruct((rows, n * width), BF16),
        in_specs=[smem_spec()] + [vmem_spec()] * n,
        out_specs=hbm_spec(),
        scratch_shapes=[pltpu.SemaphoreType.DMA((n,))],
        compiler_params=params(4),
        cost_estimate=cost(0, 2 * n * nbytes(blocks[0])),
        name="side_by_side",
    )(me, *blocks)


def shards(video, conv_weight, latent_weight, embed_weight, modulation, qkv_weight, qk_gain, text, text_weight):
    n = lax.axis_size("ctx")
    frames = video.shape[0]
    me = lax.axis_index("ctx").astype(jnp.int32).reshape(1)

    def swap(x, k):
        return lax.ppermute(x, "ctx", [(i, i ^ k) for i in range(n)])

    halo = lax.ppermute(video[:, -1:], "ctx", [(i, i + 1) for i in range(n - 1)])
    rhs0, rhs1, shift, gram, stream, tile, taps = fold(
        embed_weight,
        modulation,
        qkv_weight.transpose(1, 0, 2),
        text,
        video,
        conv_weight.reshape(-1, conv_weight.shape[-1]),
    )
    patches, text_near = conv_side(tile, halo, taps, latent_weight, text_weight)
    order = tuple(range(n - 1, -1, -1))
    received = [swap(patches, k) if k else patches for k in order]
    tkey, tvalue = text_side(stream, qk_gain, text_near)
    queries, key, value = qkv_side(
        order, frames, me, received, rhs0, rhs1, shift, gram, qk_gain, tkey, tvalue
    )
    blocks = []
    for query, k in zip(queries, order):
        block = attend(query, key, value)
        blocks.append(swap(block, k) if k else block)
    return side_by_side(order, me, blocks)


def solution(mesh):
    in_specs = (
        P("dp", "ctx", None, None),
        P(),
        P(),
        P(),
        P("dp", None),
        P(None, None, "ctx"),
        P(),
        P("dp", None),
        P(None, None, "ctx"),
    )
    out_specs = P(("dp", "ctx"), None)
    return jax.shard_map(shards, mesh=mesh, in_specs=in_specs, out_specs=out_specs, check_vma=False)
```

```python
import math

import jax
import jax.numpy as jnp
from jax import lax
from jax.experimental import pallas as pl
from jax.experimental.pallas import tpu as pltpu
from jax.sharding import PartitionSpec as P

HS = 128
EPS = 1e-06
F32 = jnp.float32
BF16 = jnp.bfloat16
VMEM = pltpu.VMEM
MIB = 1024 * 1024


def vmem_spec():
    return pl.BlockSpec(memory_space=pltpu.VMEM)


def hbm_spec():
    return pl.BlockSpec(memory_space=pltpu.HBM)


def smem_spec():
    return pl.BlockSpec(memory_space=pltpu.SMEM)


def params(mib):
    return pltpu.CompilerParams(vmem_limit_bytes=mib * MIB)


def cost(flops, bytes_accessed, transcendentals=0):
    return pl.CostEstimate(
        flops=int(flops), bytes_accessed=int(bytes_accessed), transcendentals=int(transcendentals)
    )


def nbytes(*arrays):
    return sum(math.prod(a.shape) * a.dtype.itemsize for a in arrays)


def split(x):
    hi = x.astype(BF16)
    return hi, (x - hi.astype(F32)).astype(BF16)


def dot(a, b):
    return jnp.dot(a, b, preferred_element_type=F32)


def dot_nt(a, b):
    return lax.dot_general(a, b, (((1,), (1,)), ((), ())), preferred_element_type=F32)


def fold_kernel(
    chunks,
    e_hbm,
    mod_hbm,
    w_hbm,
    text_hbm,
    video_hbm,
    conv_hbm,
    rhs0_ref,
    rhs1_ref,
    shift_ref,
    gram_ref,
    stream_ref,
    video_ref,
    conv_ref,
    e_ref,
    mod_ref,
    text_ref,
    w_buf,
    lhs_ref,
    acc_ref,
    sem,
    w_sem,
):
    parts, depth, width = w_hbm.shape
    rows = depth // chunks
    small = [
        pltpu.make_async_copy(src, dst, sem.at[i])
        for i, (src, dst) in enumerate(
            (
                (e_hbm, e_ref),
                (mod_hbm, mod_ref),
                (text_hbm, text_ref),
                (video_hbm, video_ref),
                (conv_hbm, conv_ref),
            )
        )
    ]

    def copy(c):
        at = pl.ds(c * rows, rows)
        return pltpu.make_async_copy(w_hbm.at[:, at], w_buf.at[:, at], w_sem.at[c])

    small[0].start()
    small[1].start()
    for c in range(chunks):
        copy(c).start()
    for c in small[2:]:
        c.start()
    small[0].wait()
    small[1].wait()
    pi = e_ref.shape[0]
    e = e_ref[...].astype(F32)
    centred = e - jnp.mean(e, -1, keepdims=True)
    hi, lo = split(centred * (1.0 + mod_ref[1:2, :]))
    lhs_ref[0:pi, :] = hi
    lhs_ref[pi : 2 * pi, :] = lo
    shift_hi, shift_lo = split(mod_ref[0:1, :])
    lhs_ref[2 * pi :, :] = jnp.concatenate(
        [shift_hi.astype(F32), shift_lo.astype(F32), jnp.zeros((14, depth), F32)], 0
    ).astype(BF16)
    both = jnp.concatenate(split(centred), 0)
    gram = dot_nt(both, both)
    lane = lax.broadcasted_iota(jnp.int32, (pi, 2 * pi), 1)
    gram = gram[:pi] + jnp.where(lane < pi, gram[pi:], 0.0)
    gram = gram + pltpu.roll(gram, pi, 1)
    gram = jnp.concatenate([gram, gram], 0)
    row = lax.broadcasted_iota(jnp.int32, gram.shape, 0) // pi
    col = lax.broadcasted_iota(jnp.int32, gram.shape, 1) // pi
    ghi, glo = split(jnp.where(row == col, gram * (1.0 / depth), 0.0))
    gram_ref[...] = jnp.concatenate([ghi, glo], 0)
    for c in range(chunks):
        copy(c).wait()
        lhs = lhs_ref[:, c * rows : (c + 1) * rows]
        for p in range(parts):
            at = slice(p * width, (p + 1) * width)
            term = dot(lhs, w_buf[p, c * rows : (c + 1) * rows, :])
            if c == 0:
                acc_ref[:, at] = term
            else:
                acc_ref[:, at] += term
    total = acc_ref[...]
    hi, lo = split(total[:pi] + total[pi : 2 * pi])
    none = jnp.zeros_like(hi)
    rhs0_ref[...] = jnp.concatenate([hi, none, lo, none], 0)
    rhs1_ref[...] = jnp.concatenate([none, hi, none, lo], 0)
    shift_ref[...] = total[2 * pi : 2 * pi + 1] + total[2 * pi + 1 : 2 * pi + 2]
    small[2].wait()
    text = text_ref[...].astype(F32)
    centred = text - jnp.mean(text, -1, keepdims=True)
    normed = centred * lax.rsqrt(jnp.mean(centred * centred, -1, keepdims=True) + EPS)
    stream_ref[...] = (normed * (1.0 + mod_ref[3:4, :]) + mod_ref[2:3, :]).astype(BF16)
    small[3].wait()
    small[4].wait()


def fold(embed_weight, modulation, weight, text, video, conv_weight):
    parts, depth, width = weight.shape
    pi = embed_weight.shape[0]
    cols = parts * width
    chunks = 6
    return pl.pallas_call(
        lambda *refs: fold_kernel(chunks, *refs),
        out_shape=(
            jax.ShapeDtypeStruct((4 * pi, cols), BF16),
            jax.ShapeDtypeStruct((4 * pi, cols), BF16),
            jax.ShapeDtypeStruct((1, cols), F32),
            jax.ShapeDtypeStruct((4 * pi, 2 * pi), BF16),
            jax.ShapeDtypeStruct(text.shape, BF16),
            jax.ShapeDtypeStruct(video.shape, BF16),
            jax.ShapeDtypeStruct(conv_weight.shape, BF16),
        ),
        in_specs=[hbm_spec()] * 6,
        out_specs=(vmem_spec(),) * 7,
        scratch_shapes=[
            VMEM(embed_weight.shape, BF16),
            VMEM(modulation.shape, F32),
            VMEM(text.shape, BF16),
            VMEM((parts, depth, width), BF16),
            VMEM((2 * pi + 16, depth), BF16),
            VMEM((2 * pi + 16, cols), F32),
            pltpu.SemaphoreType.DMA((5,)),
            pltpu.SemaphoreType.DMA((chunks,)),
        ],
        compiler_params=params(32),
        cost_estimate=cost(
            2 * 144 * depth * cols, nbytes(weight, embed_weight, modulation, text, video, conv_weight)
        ),
        name="fold",
    )(*[pltpu.with_memory_space_constraint(a, pltpu.HBM) for a in (embed_weight, modulation, weight, text, video, conv_weight)])


def text_kernel(stream_ref, gain_ref, w_ref, key_ref, value_ref, acc_ref):
    depth, parts, width = w_ref.shape
    step = 128
    group = 4
    row = lax.broadcasted_iota(jnp.int32, (2 * step, 2 * step), 0)
    col = lax.broadcasted_iota(jnp.int32, (2 * step, 2 * step), 1)
    pick = jnp.where(col == 2 * (row % step) + row // step, 1.0, 0.0).astype(BF16)
    flat = w_ref.reshape(depth * parts, width)
    for c in range(depth // (group * step)):
        pieces = ([], [])
        for s in range(group):
            at = 2 * (c * group + s) * step
            both = dot(pick, flat[at : at + 2 * step, :]).astype(BF16)
            pieces[0].append(both[:step])
            pieces[1].append(both[step:])
        stream = stream_ref[:, c * group * step : (c + 1) * group * step]
        for p in range(2):
            term = dot(stream, jnp.concatenate(pieces[p], 0))
            if c == 0:
                acc_ref[p] = term
            else:
                acc_ref[p] += term
    for h in range(width // HS):
        at = slice(h * HS, (h + 1) * HS)
        key = acc_ref[0, :, at]
        scale = lax.rsqrt(jnp.mean(key * key, -1, keepdims=True) + EPS)
        key_ref[h] = (key * scale * gain_ref[1:2, :]).astype(BF16)
        value_ref[h] = acc_ref[1, :, at].astype(BF16)


def text_side(stream, gain, weight):
    depth, parts, width = weight.shape
    count = stream.shape[0]
    heads = width // HS
    return pl.pallas_call(
        text_kernel,
        out_shape=(jax.ShapeDtypeStruct((heads, count, HS), BF16),) * 2,
        in_specs=[vmem_spec()] * 3,
        out_specs=(vmem_spec(),) * 2,
        scratch_shapes=[VMEM((parts, count, width), F32)],
        compiler_params=params(12),
        cost_estimate=cost(4 * count * depth * parts * width, nbytes(weight, stream)),
        name="text_side",
    )(stream, gain, weight)


def conv_kernel(
    chunks,
    video_ref,
    halo_ref,
    weight_ref,
    latent_ref,
    text_hbm,
    out_ref,
    text_ref,
    wide_ref,
    even_ref,
    odd_ref,
    left_ref,
    spread_ref,
    sem,
):
    deep = text_hbm.shape[0] // chunks
    ahead = [
        pltpu.make_async_copy(text_hbm.at[pl.ds(c * deep, deep)], text_ref.at[pl.ds(c * deep, deep)], sem.at[c])
        for c in range(chunks)
    ]
    for copy in ahead:
        copy.start()
    frames, rows, cols, chans = video_ref.shape
    block = cols + 8
    half = cols // 2
    quarter = cols // 4
    for r in range(rows + 1):
        for f in range(frames):
            base = (r * frames + f) * block
            pixels = halo_ref[f, 0] if r == 0 else video_ref[f, r - 1]
            wide_ref[base : base + 8, :] = jnp.zeros((8, chans), F32)
            wide_ref[base + 8 : base + block, :] = pixels.astype(F32)
            at = [wide_ref[pl.ds(base + 7 + o, quarter, stride=4), :] for o in range(5)]
            even = jnp.concatenate([at[1], at[3]], 0).astype(BF16)
            odd = jnp.concatenate([at[2], at[4]], 0).astype(BF16)
            left = jnp.concatenate([at[0], at[2]], 0).astype(BF16)
            for t in (range(3) if f == 0 else (f + 2,)):
                even_ref[r, t] = even
                odd_ref[r, t] = odd
                left_ref[r, t] = left
    lat, mid = latent_ref.shape
    tall = rows // 2
    spread_ref[...] = jnp.zeros_like(spread_ref)
    for s in range(2 * tall):
        spread_ref[s * lat : (s + 1) * lat, s * mid : (s + 1) * mid] = latent_ref[...]
    pieces = []
    for j in range(tall):
        taps = []
        for kt in range(3):
            for kr in range(3):
                for ref in (left_ref, even_ref, odd_ref):
                    taps.append(ref[2 * j + kr, kt : kt + frames].reshape(frames * half, chans))
        conv = dot(jnp.concatenate(taps, 1), weight_ref[...])
        act = (conv * (1.0 / (1.0 + jnp.exp(-conv)))).astype(BF16)
        for b in range(2):
            pieces.append(
                jnp.concatenate(
                    [act[f * half + b * quarter : f * half + (b + 1) * quarter] for f in range(frames)], 0
                )
            )
    out_ref[...] = dot_nt(jnp.concatenate(pieces, 1), spread_ref[...]).astype(BF16)
    for copy in ahead:
        copy.wait()


def conv_side(video, halo, weight, latent_weight, text_weight):
    frames, rows, cols, chans = video.shape
    mid = weight.shape[-1]
    lat = latent_weight.shape[1]
    latent = latent_weight.T
    half = cols // 2
    tall = rows // 2
    chunks = 4
    return pl.pallas_call(
        lambda *refs: conv_kernel(chunks, *refs),
        out_shape=(
            jax.ShapeDtypeStruct((frames * half // 2, 2 * tall * lat), BF16),
            jax.ShapeDtypeStruct(text_weight.shape, BF16),
        ),
        in_specs=[vmem_spec()] * 4 + [hbm_spec()],
        out_specs=(vmem_spec(),) * 2,
        scratch_shapes=[VMEM(((rows + 1) * frames * (cols + 8), chans), F32)]
        + [VMEM((rows + 1, frames + 2, half, chans), BF16)] * 3
        + [VMEM((2 * tall * lat, 2 * tall * mid), BF16), pltpu.SemaphoreType.DMA((chunks,))],
        compiler_params=params(24),
        cost_estimate=cost(
            2 * frames * tall * half * 27 * chans * mid, nbytes(video, halo, weight, text_weight)
        ),
        name="conv_side",
    )(video, halo, weight, latent, pltpu.with_memory_space_constraint(text_weight, pltpu.HBM))


def head_norm(v, gain):
    return (v * lax.rsqrt(jnp.mean(v * v, -1, keepdims=True) + EPS) * gain).astype(BF16)


def token_scales(x, xx, gram_ref):
    quad = dot(xx, gram_ref[...]) * x.astype(F32)
    lane = lax.broadcasted_iota(jnp.int32, quad.shape, 1)
    low = lane < quad.shape[1] // 2
    scales = []
    for i in range(2):
        var = jnp.sum(jnp.where(low if i == 0 else ~low, quad, 0.0), -1, keepdims=True)
        scales.append(lax.rsqrt(jnp.maximum(var, 0.0) + EPS))
    return scales


def block_queries(n, own, x, xx, scales, rhs_refs, shift_ref, gain_ref, query_ref):
    heads = query_ref.shape[0]
    span = x.shape[0] // n
    grain = span // own
    gain = gain_ref[0:1, :] * (math.log2(math.e) / math.sqrt(HS))
    for i in range(2):
        at = slice(0, heads * HS)
        projected = dot(xx, rhs_refs[i][:, at]) * scales[i] + shift_ref[:, at]
        for h in range(heads):
            v = head_norm(projected[:, h * HS : (h + 1) * HS], gain)
            for s in range(n):
                for f in range(own):
                    to = f * (n * 2 * grain) + (s * 2 + i) * grain
                    come = s * span + f * grain
                    query_ref[h, to : to + grain, :] = v[come : come + grain]


def attention(query_ref, key_ref, value_ref, out_ref):
    heads, total, _ = key_ref.shape
    for h in range(heads):
        weights = jnp.exp2(dot_nt(query_ref[h], key_ref[h]))
        norm = weights[:, :HS]
        for c in range(HS, total, HS):
            norm = norm + weights[:, c : c + HS]
        norm = jnp.sum(norm, -1, keepdims=True)
        attended = dot(weights.astype(BF16), value_ref[h])
        out_ref[:, h * HS : (h + 1) * HS] = (attended / norm).astype(BF16)


def first_kernel(order, frames, *refs):
    n = len(order)
    me_ref = refs[0]
    patch_refs = refs[1 : 1 + n]
    rhs_refs = refs[1 + n : 3 + n]
    shift_ref, gram_ref, gain_ref, tkey_ref, tvalue_ref = refs[3 + n : 8 + n]
    out_ref, x_ref, key_ref, value_ref, patch_scr, query_ref = refs[8 + n :]
    me = me_ref[0]
    heads, count, _ = tkey_ref.shape
    rows = patch_refs[0].shape[0]
    for k, ref in zip(order, patch_refs):
        patch_scr[pl.ds(pl.multiple_of((me ^ k) * rows, rows), rows), :] = ref[...]
    for h in range(heads):
        key_ref[h, 0:count, :] = tkey_ref[h]
        value_ref[h, 0:count, :] = tvalue_ref[h]
    own = frames // n
    span = rows // n
    for j, k in enumerate(order):
        for s in range(n):
            at = pl.multiple_of((me ^ k) * span, span) + s * rows
            x_ref[j * rows + s * span : j * rows + (s + 1) * span, :] = patch_scr[
                pl.ds(pl.multiple_of(at, span), span), :
            ]
    x = x_ref[...]
    xx = jnp.concatenate([x, x], 1)
    scales = token_scales(x, xx, gram_ref)
    width = heads * HS
    for i in range(2):
        for p in (1, 2):
            for h0 in range(0, heads, 2):
                at = slice(p * width + h0 * HS, p * width + (h0 + 2) * HS)
                pair = dot(xx, rhs_refs[i][:, at]) * scales[i] + shift_ref[:, at]
                for h in (h0, h0 + 1):
                    v = pair[:, (h - h0) * HS : (h - h0 + 1) * HS]
                    to = slice(count + i * n * rows, count + (i + 1) * n * rows)
                    if p == 1:
                        key_ref[h, to, :] = head_norm(v, gain_ref[1:2, :])
                    else:
                        value_ref[h, to, :] = v.astype(BF16)
    block_queries(
        n, own, x[:rows], xx[:rows], [v[:rows] for v in scales], rhs_refs, shift_ref, gain_ref, query_ref
    )
    attention(query_ref, key_ref, value_ref, out_ref)


def first_block(order, frames, me, patches, rhs0, rhs1, shift, gram, gain, tkey, tvalue):
    n = len(order)
    heads, count, _ = tkey.shape
    rows = patches[0].shape[0]
    total = count + 2 * n * rows
    return pl.pallas_call(
        lambda *refs: first_kernel(order, frames, *refs),
        out_shape=(
            jax.ShapeDtypeStruct((2 * rows, heads * HS), BF16),
            jax.ShapeDtypeStruct((n * rows, rows), BF16),
            jax.ShapeDtypeStruct((heads, total, HS), BF16),
            jax.ShapeDtypeStruct((heads, total, HS), BF16),
        ),
        in_specs=[smem_spec()] + [vmem_spec()] * (n + 7),
        out_specs=(vmem_spec(),) * 4,
        scratch_shapes=[VMEM((n * rows, rows), BF16), VMEM((heads, 2 * rows, HS), BF16)],
        compiler_params=params(16),
        cost_estimate=cost(2 * 2 * n * rows * 256 * 3 * heads * HS, 4 * nbytes(rhs0)),
        name="first_block",
    )(me, *patches, rhs0, rhs1, shift, gram, gain, tkey, tvalue)


def attend_kernel(
    n, own, j, x_ref, rhs0_ref, rhs1_ref, shift_ref, gram_ref, gain_ref, key_ref, value_ref, out_ref, query_ref
):
    rows = x_ref.shape[1]
    x = x_ref[j * rows : (j + 1) * rows, :]
    xx = jnp.concatenate([x, x], 1)
    scales = token_scales(x, xx, gram_ref)
    block_queries(n, own, x, xx, scales, (rhs0_ref, rhs1_ref), shift_ref, gain_ref, query_ref)
    attention(query_ref, key_ref, value_ref, out_ref)


def attend(n, frames, j, x, rhs0, rhs1, shift, gram, gain, key, value):
    heads = key.shape[0]
    rows = x.shape[1]
    return pl.pallas_call(
        lambda *refs: attend_kernel(n, frames // n, j, *refs),
        out_shape=jax.ShapeDtypeStruct((2 * rows, heads * HS), BF16),
        in_specs=[vmem_spec()] * 8,
        out_specs=vmem_spec(),
        scratch_shapes=[VMEM((heads, 2 * rows, HS), BF16)],
        compiler_params=params(12),
        cost_estimate=cost(heads * rows * HS, 2 * nbytes(x)),
        name="attend",
    )(x, rhs0, rhs1, shift, gram, gain, key, value)


def place(block, me, k, out_ref, sem):
    width = block.shape[1]
    at = pl.multiple_of((me ^ k) * width, width)
    return pltpu.make_async_copy(block, out_ref.at[:, pl.ds(at, width)], sem)


def own_kernel(
    n,
    own,
    far,
    me_ref,
    far_ref,
    x_ref,
    rhs0_ref,
    rhs1_ref,
    shift_ref,
    gram_ref,
    gain_ref,
    key_ref,
    value_ref,
    out_ref,
    query_ref,
    block_ref,
    sem,
):
    first = place(far_ref, me_ref[0], far, out_ref, sem.at[0])
    first.start()
    attend_kernel(
        n,
        own,
        n - 1,
        x_ref,
        rhs0_ref,
        rhs1_ref,
        shift_ref,
        gram_ref,
        gain_ref,
        key_ref,
        value_ref,
        block_ref,
        query_ref,
    )
    second = place(block_ref, me_ref[0], 0, out_ref, sem.at[1])
    second.start()
    first.wait()
    second.wait()


def own_block(n, frames, far, me, far_block, x, rhs0, rhs1, shift, gram, gain, key, value):
    heads = key.shape[0]
    rows = x.shape[1]
    width = heads * HS
    return pl.pallas_call(
        lambda *refs: own_kernel(n, frames // n, far, *refs),
        out_shape=jax.ShapeDtypeStruct((2 * rows, n * width), BF16),
        in_specs=[smem_spec()] + [vmem_spec()] * 9,
        out_specs=hbm_spec(),
        scratch_shapes=[
            VMEM((heads, 2 * rows, HS), BF16),
            VMEM((2 * rows, width), BF16),
            pltpu.SemaphoreType.DMA((2,)),
        ],
        compiler_params=params(12),
        cost_estimate=cost(heads * rows * HS, 2 * nbytes(x)),
        name="own_block",
    )(me, far_block, x, rhs0, rhs1, shift, gram, gain, key, value)


def rest_kernel(order, me_ref, out_in_ref, *refs):
    n = len(order)
    out_ref, sem = refs[n:]
    copies = [place(refs[j], me_ref[0], k, out_ref, sem.at[j]) for j, k in enumerate(order)]
    for c in copies:
        c.start()
    for c in copies:
        c.wait()


def rest(order, me, out, blocks):
    n = len(order)
    return pl.pallas_call(
        lambda *refs: rest_kernel(order, *refs),
        out_shape=jax.ShapeDtypeStruct(out.shape, BF16),
        in_specs=[smem_spec(), hbm_spec()] + [vmem_spec()] * n,
        out_specs=hbm_spec(),
        scratch_shapes=[pltpu.SemaphoreType.DMA((n,))],
        input_output_aliases={1: 0},
        compiler_params=params(4),
        cost_estimate=cost(0, 2 * n * nbytes(blocks[0])),
        name="rest",
    )(me, out, *blocks)


def shards(video, conv_weight, latent_weight, embed_weight, modulation, qkv_weight, qk_gain, text, text_weight):
    n = lax.axis_size("ctx")
    frames = video.shape[0]
    me = lax.axis_index("ctx").astype(jnp.int32).reshape(1)

    def swap(x, k):
        return lax.ppermute(x, "ctx", [(i, i ^ k) for i in range(n)])

    halo = lax.ppermute(video[:, -1:], "ctx", [(i, i + 1) for i in range(n - 1)])
    rhs0, rhs1, shift, gram, stream, tile, taps = fold(
        embed_weight,
        modulation,
        qkv_weight.transpose(1, 0, 2),
        text,
        video,
        conv_weight.reshape(-1, conv_weight.shape[-1]),
    )
    patches, text_near = conv_side(tile, halo, taps, latent_weight, text_weight)
    order = tuple(range(n - 1, -1, -1))
    received = [swap(patches, k) if k else patches for k in order]
    tkey, tvalue = text_side(stream, qk_gain, text_near)
    block, x, key, value = first_block(
        order, frames, me, received, rhs0, rhs1, shift, gram, qk_gain, tkey, tvalue
    )
    far_block = swap(block, order[0])
    common = (x, rhs0, rhs1, shift, gram, qk_gain, key, value)
    blocks = [swap(attend(n, frames, j, *common), order[j]) for j in range(1, n - 1)]
    out = own_block(n, frames, order[0], me, far_block, *common)
    return rest(order[1 : n - 1], me, out, blocks)


def solution(mesh):
    in_specs = (
        P("dp", "ctx", None, None),
        P(),
        P(),
        P(),
        P("dp", None),
        P(None, None, "ctx"),
        P(),
        P("dp", None),
        P(None, None, "ctx"),
    )
    out_specs = P(("dp", "ctx"), None)
    return jax.shard_map(shards, mesh=mesh, in_specs=in_specs, out_specs=out_specs, check_vma=False)
```

```python
import math

import jax
import jax.numpy as jnp
from jax import lax
from jax.experimental import pallas as pl
from jax.experimental.pallas import tpu as pltpu
from jax.sharding import PartitionSpec as P

HS = 128
EPS = 1e-06
F32 = jnp.float32
BF16 = jnp.bfloat16
VMEM = pltpu.VMEM
MIB = 1024 * 1024


def vmem_spec():
    return pl.BlockSpec(memory_space=pltpu.VMEM)


def hbm_spec():
    return pl.BlockSpec(memory_space=pltpu.HBM)


def far(x):
    return pltpu.with_memory_space_constraint(x, pltpu.HBM)


def params(mib):
    return pltpu.CompilerParams(vmem_limit_bytes=mib * MIB)


def cost(flops, bytes_accessed, transcendentals=0):
    return pl.CostEstimate(
        flops=int(flops), bytes_accessed=int(bytes_accessed), transcendentals=int(transcendentals)
    )


def nbytes(*arrays):
    return sum(math.prod(a.shape) * a.dtype.itemsize for a in arrays)


def split(x):
    hi = x.astype(BF16)
    return hi, (x - hi.astype(F32)).astype(BF16)


def dot(a, b):
    return jnp.dot(a, b, preferred_element_type=F32)


def dot_nt(a, b):
    return lax.dot_general(a, b, (((1,), (1,)), ((), ())), preferred_element_type=F32)


def head_norm(v, gain):
    return (v * lax.rsqrt(jnp.mean(v * v, -1, keepdims=True) + EPS) * gain).astype(BF16)


def edge_kernel(video_hbm, text_hbm, mod_hbm, halo_ref, text_ref, mod_ref, sem):
    rows = video_hbm.shape[1]
    pairs = (
        (video_hbm.at[:, pl.ds(rows - 1, 1)], halo_ref),
        (mod_hbm, mod_ref),
        (text_hbm, text_ref),
    )
    copies = [pltpu.make_async_copy(src, dst, sem.at[i]) for i, (src, dst) in enumerate(pairs)]
    for c in copies:
        c.start()
    for c in copies:
        c.wait()


def edge(video, text, modulation):
    frames, _, cols, chans = video.shape
    return pl.pallas_call(
        edge_kernel,
        out_shape=(
            jax.ShapeDtypeStruct((frames, 1, cols, chans), BF16),
            jax.ShapeDtypeStruct(text.shape, BF16),
            jax.ShapeDtypeStruct(modulation.shape, F32),
        ),
        in_specs=[hbm_spec()] * 3,
        out_specs=(vmem_spec(),) * 3,
        scratch_shapes=[pltpu.SemaphoreType.DMA((3,))],
        compiler_params=params(4),
        cost_estimate=cost(0, 2 * nbytes(text, modulation)),
        name="edge",
    )(*[far(a) for a in (video, text, modulation)])


def text_kernel(
    chunks,
    text_ref,
    mod_ref,
    gain_ref,
    w_hbm,
    video_hbm,
    conv_hbm,
    e_hbm,
    key_ref,
    value_ref,
    video_ref,
    conv_ref,
    e_ref,
    w_ref,
    stream_ref,
    acc_ref,
    sem,
    w_sem,
):
    depth, parts, width = w_hbm.shape
    deep = depth // chunks
    copies = [
        pltpu.make_async_copy(w_hbm.at[pl.ds(c * deep, deep)], w_ref.at[pl.ds(c * deep, deep)], w_sem.at[c])
        for c in range(chunks)
    ]
    pairs = (
        (video_hbm, video_ref),
        (conv_hbm, conv_ref),
        (e_hbm, e_ref),
    )
    ahead = [pltpu.make_async_copy(src, dst, sem.at[i]) for i, (src, dst) in enumerate(pairs)]
    for c in copies:
        c.start()
    few = 16
    for r in range(0, text_ref.shape[0], few):
        text = text_ref[r : r + few, :].astype(F32)
        centred = text - jnp.mean(text, -1, keepdims=True)
        normed = centred * lax.rsqrt(jnp.mean(centred * centred, -1, keepdims=True) + EPS)
        stream_ref[r : r + few, :] = (normed * (1.0 + mod_ref[3:4, :]) + mod_ref[2:3, :]).astype(BF16)
    step = 128
    row = lax.broadcasted_iota(jnp.int32, (2 * step, 2 * step), 0)
    col = lax.broadcasted_iota(jnp.int32, (2 * step, 2 * step), 1)
    pick = jnp.where(col == 2 * (row % step) + row // step, 1.0, 0.0).astype(BF16)
    flat = w_ref.reshape(depth * parts, width)
    for c in range(chunks):
        copies[c].wait()
        if c == 0:
            for copy in ahead:
                copy.start()
        pieces = ([], [])
        for s in range(deep // step):
            at = 2 * (c * deep + s * step)
            both = dot(pick, flat[at : at + 2 * step, :]).astype(BF16)
            pieces[0].append(both[:step])
            pieces[1].append(both[step:])
        stream = stream_ref[:, c * deep : (c + 1) * deep]
        for p in range(2):
            term = dot(stream, jnp.concatenate(pieces[p], 0))
            if c == 0:
                acc_ref[p] = term
            else:
                acc_ref[p] += term
    for h in range(width // HS):
        at = slice(h * HS, (h + 1) * HS)
        key_ref[h] = head_norm(acc_ref[0, :, at], gain_ref[1:2, :])
        value_ref[h] = acc_ref[1, :, at].astype(BF16)
    for c in ahead:
        c.wait()


def text_side(text, modulation, gain, weight, video, conv_weight, embed_weight):
    depth, parts, width = weight.shape
    count = text.shape[0]
    heads = width // HS
    chunks = 3
    return pl.pallas_call(
        lambda *refs: text_kernel(chunks, *refs),
        out_shape=(
            jax.ShapeDtypeStruct((heads, count, HS), BF16),
            jax.ShapeDtypeStruct((heads, count, HS), BF16),
            jax.ShapeDtypeStruct(video.shape, BF16),
            jax.ShapeDtypeStruct(conv_weight.shape, BF16),
            jax.ShapeDtypeStruct(embed_weight.shape, BF16),
        ),
        in_specs=[vmem_spec()] * 3 + [hbm_spec()] * 4,
        out_specs=(vmem_spec(),) * 5,
        scratch_shapes=[
            VMEM((depth, parts, width), BF16),
            VMEM((count, depth), BF16),
            VMEM((parts, count, width), F32),
            pltpu.SemaphoreType.DMA((3,)),
            pltpu.SemaphoreType.DMA((chunks,)),
        ],
        compiler_params=params(24),
        cost_estimate=cost(4 * count * depth * parts * width, nbytes(weight, text, video, conv_weight)),
        name="text_side",
    )(text, modulation, gain, *[far(a) for a in (weight, video, conv_weight, embed_weight)])


def fold_kernel(
    e_ref,
    mod_ref,
    w0_ref,
    w_hbm,
    rhs0_ref,
    rhs1_ref,
    shift_ref,
    gram_ref,
    lhs_ref,
    both_ref,
    acc_ref,
    w1_ref,
    sem,
):
    parts, deep0, width = w0_ref.shape
    pi, depth = e_ref.shape
    copies = [
        pltpu.make_async_copy(w_hbm.at[p, pl.ds(deep0, depth - deep0)], w1_ref.at[p], sem.at[p])
        for p in range(parts)
    ]
    for c in copies:
        c.start()
    few = 16
    for r in range(0, pi, few):
        e = e_ref[r : r + few, :].astype(F32)
        centred = e - jnp.mean(e, -1, keepdims=True)
        hi, lo = split(centred * (1.0 + mod_ref[1:2, :]))
        lhs_ref[r : r + few, :] = hi
        lhs_ref[pi + r : pi + r + few, :] = lo
        hi, lo = split(centred)
        both_ref[r : r + few, :] = hi
        both_ref[pi + r : pi + r + few, :] = lo
    shift_hi, shift_lo = split(mod_ref[0:1, :])
    lhs_ref[2 * pi :, :] = jnp.concatenate(
        [shift_hi.astype(F32), shift_lo.astype(F32), jnp.zeros((14, depth), F32)], 0
    ).astype(BF16)
    gram = dot_nt(both_ref[...], both_ref[...])
    lane = lax.broadcasted_iota(jnp.int32, (pi, 2 * pi), 1)
    gram = gram[:pi] + jnp.where(lane < pi, gram[pi:], 0.0)
    gram = gram + pltpu.roll(gram, pi, 1)
    gram = jnp.concatenate([gram, gram], 0)
    row = lax.broadcasted_iota(jnp.int32, gram.shape, 0) // pi
    col = lax.broadcasted_iota(jnp.int32, gram.shape, 1) // pi
    ghi, glo = split(jnp.where(row == col, gram * (1.0 / depth), 0.0))
    gram_ref[...] = jnp.concatenate([ghi, glo], 0)
    for p in range(parts):
        at = slice(p * width, (p + 1) * width)
        acc_ref[:, at] = dot(lhs_ref[:, :deep0], w0_ref[p])
    for p in range(parts):
        at = slice(p * width, (p + 1) * width)
        copies[p].wait()
        acc_ref[:, at] += dot(lhs_ref[:, deep0:], w1_ref[p])
    total = acc_ref[...]
    hi, lo = split(total[:pi] + total[pi : 2 * pi])
    none = jnp.zeros_like(hi)
    rhs0_ref[...] = jnp.concatenate([hi, none, lo, none], 0)
    rhs1_ref[...] = jnp.concatenate([none, hi, none, lo], 0)
    shift_ref[...] = total[2 * pi : 2 * pi + 1] + total[2 * pi + 1 : 2 * pi + 2]


def fold(embed_weight, modulation, weight0, weight):
    parts, taken, width = weight0.shape
    pi, depth = embed_weight.shape
    cols = parts * width
    return pl.pallas_call(
        fold_kernel,
        out_shape=(
            jax.ShapeDtypeStruct((4 * pi, cols), BF16),
            jax.ShapeDtypeStruct((4 * pi, cols), BF16),
            jax.ShapeDtypeStruct((1, cols), F32),
            jax.ShapeDtypeStruct((4 * pi, 2 * pi), BF16),
        ),
        in_specs=[vmem_spec()] * 3 + [hbm_spec()],
        out_specs=(vmem_spec(),) * 4,
        scratch_shapes=[
            VMEM((2 * pi + 16, depth), BF16),
            VMEM((2 * pi, depth), BF16),
            VMEM((2 * pi + 16, cols), F32),
            VMEM((parts, depth - taken, width), BF16),
            pltpu.SemaphoreType.DMA((parts,)),
        ],
        compiler_params=params(12),
        cost_estimate=cost(2 * 144 * depth * cols, nbytes(weight, embed_weight, modulation)),
        name="fold",
    )(embed_weight, modulation, weight0, far(weight))


def conv_kernel(
    chunks,
    video_ref,
    halo_ref,
    weight_ref,
    latent_ref,
    qkv_hbm,
    out_ref,
    qkv_ref,
    wide_ref,
    even_ref,
    odd_ref,
    left_ref,
    spread_ref,
    sem,
):
    deep = qkv_ref.shape[1] // chunks
    ahead = [
        pltpu.make_async_copy(
            qkv_hbm.at[p, pl.ds(c * deep, deep)], qkv_ref.at[p, pl.ds(c * deep, deep)], sem.at[p, c]
        )
        for p in range(qkv_ref.shape[0])
        for c in range(chunks)
    ]
    for copy in ahead:
        copy.start()
    frames, rows, cols, chans = video_ref.shape
    block = cols + 8
    half = cols // 2
    quarter = cols // 4
    for r in range(rows + 1):
        for f in range(frames):
            base = (r * frames + f) * block
            pixels = halo_ref[f, 0] if r == 0 else video_ref[f, r - 1]
            wide_ref[base : base + 8, :] = jnp.zeros((8, chans), F32)
            wide_ref[base + 8 : base + block, :] = pixels.astype(F32)
            at = [wide_ref[pl.ds(base + 7 + o, quarter, stride=4), :] for o in range(5)]
            even = jnp.concatenate([at[1], at[3]], 0).astype(BF16)
            odd = jnp.concatenate([at[2], at[4]], 0).astype(BF16)
            left = jnp.concatenate([at[0], at[2]], 0).astype(BF16)
            for t in (range(3) if f == 0 else (f + 2,)):
                even_ref[r, t] = even
                odd_ref[r, t] = odd
                left_ref[r, t] = left
    lat, mid = latent_ref.shape
    tall = rows // 2
    spread_ref[...] = jnp.zeros_like(spread_ref)
    for s in range(2 * tall):
        spread_ref[s * lat : (s + 1) * lat, s * mid : (s + 1) * mid] = latent_ref[...]
    pieces = []
    for j in range(tall):
        taps = []
        for kt in range(3):
            for kr in range(3):
                for ref in (left_ref, even_ref, odd_ref):
                    taps.append(ref[2 * j + kr, kt : kt + frames].reshape(frames * half, chans))
        conv = dot(jnp.concatenate(taps, 1), weight_ref[...])
        act = (conv * (1.0 / (1.0 + jnp.exp(-conv)))).astype(BF16)
        for b in range(2):
            pieces.append(
                jnp.concatenate(
                    [act[f * half + b * quarter : f * half + (b + 1) * quarter] for f in range(frames)], 0
                )
            )
    out_ref[...] = dot_nt(jnp.concatenate(pieces, 1), spread_ref[...]).astype(BF16)
    for copy in ahead:
        copy.wait()


def conv_side(video, halo, weight, latent_weight, qkv_weight, taken):
    frames, rows, cols, chans = video.shape
    parts, depth, width = qkv_weight.shape
    mid = weight.shape[-1]
    lat = latent_weight.shape[1]
    latent = latent_weight.T
    half = cols // 2
    tall = rows // 2
    chunks = 1
    return pl.pallas_call(
        lambda *refs: conv_kernel(chunks, *refs),
        out_shape=(
            jax.ShapeDtypeStruct((frames * half // 2, 2 * tall * lat), BF16),
            jax.ShapeDtypeStruct((parts, taken, width), BF16),
        ),
        in_specs=[vmem_spec()] * 4 + [hbm_spec()],
        out_specs=(vmem_spec(),) * 2,
        scratch_shapes=[VMEM(((rows + 1) * frames * (cols + 8), chans), F32)]
        + [VMEM((rows + 1, frames + 2, half, chans), BF16)] * 3
        + [VMEM((2 * tall * lat, 2 * tall * mid), BF16), pltpu.SemaphoreType.DMA((parts, chunks))],
        compiler_params=params(24),
        cost_estimate=cost(
            2 * frames * tall * half * 27 * chans * mid, nbytes(video, halo, weight)
        ),
        name="conv_side",
    )(video, halo, weight, latent, far(qkv_weight))


def token_scales(x, xx, gram_ref):
    quad = dot(xx, gram_ref[...]) * x.astype(F32)
    lane = lax.broadcasted_iota(jnp.int32, quad.shape, 1)
    low = lane < quad.shape[1] // 2
    scales = []
    for i in range(2):
        var = jnp.sum(jnp.where(low if i == 0 else ~low, quad, 0.0), -1, keepdims=True)
        scales.append(lax.rsqrt(jnp.maximum(var, 0.0) + EPS))
    return scales


def block_queries(n, own, x, xx, scales, rhs_refs, shift_ref, gain_ref, query_ref):
    heads = query_ref.shape[0]
    span = x.shape[0] // n
    grain = span // own
    gain = gain_ref[0:1, :] * (math.log2(math.e) / math.sqrt(HS))
    for i in range(2):
        at = slice(0, heads * HS)
        projected = dot(xx, rhs_refs[i][:, at]) * scales[i] + shift_ref[:, at]
        for h in range(heads):
            v = head_norm(projected[:, h * HS : (h + 1) * HS], gain)
            for s in range(n):
                for f in range(own):
                    to = f * (n * 2 * grain) + (s * 2 + i) * grain
                    come = s * span + f * grain
                    query_ref[h, to : to + grain, :] = v[come : come + grain]


def attention(query_ref, key_ref, value_ref, out_ref):
    heads, total, _ = key_ref.shape
    for h in range(heads):
        weights = jnp.exp2(dot_nt(query_ref[h], key_ref[h]))
        norm = weights[:, :HS]
        for c in range(HS, total, HS):
            norm = norm + weights[:, c : c + HS]
        norm = jnp.sum(norm, -1, keepdims=True)
        attended = dot(weights.astype(BF16), value_ref[h])
        out_ref[:, h * HS : (h + 1) * HS] = (attended / norm).astype(BF16)


def first_kernel(order, frames, *refs):
    n = len(order)
    patch_refs = refs[:n]
    rhs0_ref, rhs1_ref, shift_ref, gram_ref, gain_ref, tkey_ref, tvalue_ref = refs[n : n + 7]
    out_ref, x_ref, key_ref, value_ref, patch_scr, query_ref = refs[n + 7 :]
    me = lax.axis_index("ctx")
    rhs_refs = (rhs0_ref, rhs1_ref)
    heads, count, _ = tkey_ref.shape
    rows = patch_refs[0].shape[1]
    for k, ref in zip(order, patch_refs):
        patch_scr[pl.ds(pl.multiple_of((me ^ k) * rows, rows), rows), :] = ref[...]
    key_ref[:, 0:count, :] = tkey_ref[...]
    value_ref[:, 0:count, :] = tvalue_ref[...]
    own = frames // n
    span = rows // n
    for j, k in enumerate(order):
        for s in range(n):
            at = pl.multiple_of((me ^ k) * span, span) + s * rows
            x_ref[j * rows + s * span : j * rows + (s + 1) * span, :] = patch_scr[
                pl.ds(pl.multiple_of(at, span), span), :
            ]
    x = x_ref[...]
    xx = jnp.concatenate([x, x], 1)
    scales = token_scales(x, xx, gram_ref)
    width = heads * HS
    for i in range(2):
        for p in (1, 2):
            for h0 in range(0, heads, 2):
                at = slice(p * width + h0 * HS, p * width + (h0 + 2) * HS)
                pair = dot(xx, rhs_refs[i][:, at]) * scales[i] + shift_ref[:, at]
                for h in (h0, h0 + 1):
                    v = pair[:, (h - h0) * HS : (h - h0 + 1) * HS]
                    to = slice(count + i * n * rows, count + (i + 1) * n * rows)
                    if p == 1:
                        key_ref[h, to, :] = head_norm(v, gain_ref[1:2, :])
                    else:
                        value_ref[h, to, :] = v.astype(BF16)
    block_queries(
        n, own, x[:rows], xx[:rows], [v[:rows] for v in scales], rhs_refs, shift_ref, gain_ref, query_ref
    )
    attention(query_ref, key_ref, value_ref, out_ref)


def first_block(order, frames, patches, rhs0, rhs1, shift, gram, gain, tkey, tvalue):
    n = len(order)
    heads, count, _ = tkey.shape
    rows = patches[0].shape[1]
    total = count + 2 * n * rows
    return pl.pallas_call(
        lambda *refs: first_kernel(order, frames, *refs),
        out_shape=(
            jax.ShapeDtypeStruct((2 * rows, heads * HS), BF16),
            jax.ShapeDtypeStruct((n * rows, rows), BF16),
            jax.ShapeDtypeStruct((heads, total, HS), BF16),
            jax.ShapeDtypeStruct((heads, total, HS), BF16),
        ),
        in_specs=[vmem_spec()] * (n + 7),
        out_specs=(vmem_spec(),) * 4,
        scratch_shapes=[VMEM((n * rows, rows), BF16), VMEM((heads, 2 * rows, HS), BF16)],
        compiler_params=params(16),
        cost_estimate=cost(2 * 2 * n * rows * 256 * 3 * heads * HS, 4 * nbytes(rhs0)),
        name="first_block",
    )(*patches, rhs0, rhs1, shift, gram, gain, tkey, tvalue)


def attend_kernel(
    n, own, j, x_ref, rhs0_ref, rhs1_ref, shift_ref, gram_ref, gain_ref, key_ref, value_ref, out_ref, query_ref
):
    rows = x_ref.shape[1]
    x = x_ref[j * rows : (j + 1) * rows, :]
    xx = jnp.concatenate([x, x], 1)
    scales = token_scales(x, xx, gram_ref)
    block_queries(n, own, x, xx, scales, (rhs0_ref, rhs1_ref), shift_ref, gain_ref, query_ref)
    attention(query_ref, key_ref, value_ref, out_ref)


def attend(n, frames, j, x, rhs0, rhs1, shift, gram, gain, key, value):
    heads = key.shape[0]
    rows = x.shape[1]
    return pl.pallas_call(
        lambda *refs: attend_kernel(n, frames // n, j, *refs),
        out_shape=jax.ShapeDtypeStruct((2 * rows, heads * HS), BF16),
        in_specs=[vmem_spec()] * 8,
        out_specs=vmem_spec(),
        scratch_shapes=[VMEM((heads, 2 * rows, HS), BF16)],
        compiler_params=params(12),
        cost_estimate=cost(heads * rows * HS, 2 * nbytes(x)),
        name="attend",
    )(x, rhs0, rhs1, shift, gram, gain, key, value)


def place(block, k, out_ref, sem):
    width = block.shape[1]
    at = pl.multiple_of((lax.axis_index("ctx") ^ k) * width, width)
    return pltpu.make_async_copy(block, out_ref.at[:, pl.ds(at, width)], sem)


def own_kernel(
    n,
    own,
    far,
    far_ref,
    x_ref,
    rhs0_ref,
    rhs1_ref,
    shift_ref,
    gram_ref,
    gain_ref,
    key_ref,
    value_ref,
    out_ref,
    query_ref,
    block_ref,
    sem,
):
    first = place(far_ref, far, out_ref, sem.at[0])
    first.start()
    attend_kernel(
        n,
        own,
        n - 1,
        x_ref,
        rhs0_ref,
        rhs1_ref,
        shift_ref,
        gram_ref,
        gain_ref,
        key_ref,
        value_ref,
        block_ref,
        query_ref,
    )
    second = place(block_ref, 0, out_ref, sem.at[1])
    second.start()
    first.wait()
    second.wait()


def own_block(n, frames, far, far_block, x, rhs0, rhs1, shift, gram, gain, key, value):
    heads = key.shape[0]
    rows = x.shape[1]
    width = heads * HS
    return pl.pallas_call(
        lambda *refs: own_kernel(n, frames // n, far, *refs),
        out_shape=jax.ShapeDtypeStruct((2 * rows, n * width), BF16),
        in_specs=[vmem_spec()] * 9,
        out_specs=hbm_spec(),
        scratch_shapes=[
            VMEM((heads, 2 * rows, HS), BF16),
            VMEM((2 * rows, width), BF16),
            pltpu.SemaphoreType.DMA((2,)),
        ],
        compiler_params=params(12),
        cost_estimate=cost(heads * rows * HS, 2 * nbytes(x)),
        name="own_block",
    )(far_block, x, rhs0, rhs1, shift, gram, gain, key, value)


def rest_kernel(order, out_in_ref, *refs):
    n = len(order)
    out_ref, sem = refs[n:]
    copies = [place(refs[j], k, out_ref, sem.at[j]) for j, k in enumerate(order)]
    for c in copies:
        c.start()
    for c in copies:
        c.wait()


def rest(order, out, blocks):
    n = len(order)
    return pl.pallas_call(
        lambda *refs: rest_kernel(order, *refs),
        out_shape=jax.ShapeDtypeStruct(out.shape, BF16),
        in_specs=[hbm_spec()] + [vmem_spec()] * n,
        out_specs=hbm_spec(),
        scratch_shapes=[pltpu.SemaphoreType.DMA((n,))],
        input_output_aliases={0: 0},
        compiler_params=params(4),
        cost_estimate=cost(0, 2 * n * nbytes(blocks[0])),
        name="rest",
    )(out, *blocks)


def shards(video, conv_weight, latent_weight, embed_weight, modulation, qkv_weight, qk_gain, text, text_weight):
    n = lax.axis_size("ctx")
    frames = video.shape[0]

    def swap(x, k):
        return lax.ppermute(x, "ctx", [(i, i ^ k) for i in range(n)])

    weight = qkv_weight.transpose(1, 0, 2)
    edge_row, text_near, mod_near = edge(video, text, modulation)
    halo = lax.ppermute(edge_row, "ctx", [(i, i + 1) for i in range(n - 1)])
    tkey, tvalue, tile, taps, e_near = text_side(
        text_near,
        mod_near,
        qk_gain,
        text_weight,
        video,
        conv_weight.reshape(-1, conv_weight.shape[-1]),
        embed_weight,
    )
    patches, weight_near = conv_side(tile, halo, taps, latent_weight, weight, weight.shape[1] * 2 // 3)
    order = tuple(range(n - 1, -1, -1))
    received = [swap(patches, k) if k else patches for k in order]
    rhs0, rhs1, shift, gram = fold(e_near, mod_near, weight_near, weight)
    block, x, key, value = first_block(
        order, frames, received, rhs0, rhs1, shift, gram, qk_gain, tkey, tvalue
    )
    far_block = swap(block, order[0])
    common = (x, rhs0, rhs1, shift, gram, qk_gain, key, value)
    blocks = [swap(attend(n, frames, j, *common), order[j]) for j in range(1, n - 1)]
    out = own_block(n, frames, order[0], far_block, *common)
    return rest(order[1 : n - 1], out, blocks)


def solution(mesh):
    in_specs = (
        P("dp", "ctx", None, None),
        P(),
        P(),
        P(),
        P("dp", None),
        P(None, None, "ctx"),
        P(),
        P("dp", None),
        P(None, None, "ctx"),
    )
    out_specs = P(("dp", "ctx"), None)
    return jax.shard_map(shards, mesh=mesh, in_specs=in_specs, out_specs=out_specs, check_vma=False)
```

```python
import math

import jax
import jax.numpy as jnp
from jax import lax
from jax.experimental import pallas as pl
from jax.experimental.pallas import tpu as pltpu
from jax.sharding import PartitionSpec as P

HS = 128
EPS = 1e-06
F32 = jnp.float32
BF16 = jnp.bfloat16
VMEM = pltpu.VMEM
MIB = 1024 * 1024


def vmem_spec():
    return pl.BlockSpec(memory_space=pltpu.VMEM)


def hbm_spec():
    return pl.BlockSpec(memory_space=pltpu.HBM)


def far(x):
    return pltpu.with_memory_space_constraint(x, pltpu.HBM)


def params(mib):
    return pltpu.CompilerParams(vmem_limit_bytes=mib * MIB)


def cost(flops, bytes_accessed, transcendentals=0):
    return pl.CostEstimate(
        flops=int(flops), bytes_accessed=int(bytes_accessed), transcendentals=int(transcendentals)
    )


def nbytes(*arrays):
    return sum(math.prod(a.shape) * a.dtype.itemsize for a in arrays)


def split(x):
    hi = x.astype(BF16)
    return hi, (x - hi.astype(F32)).astype(BF16)


def dot(a, b):
    return jnp.dot(a, b, preferred_element_type=F32)


def dot_nt(a, b):
    return lax.dot_general(a, b, (((1,), (1,)), ((), ())), preferred_element_type=F32)


def head_norm(v, gain):
    return (v * lax.rsqrt(jnp.mean(v * v, -1, keepdims=True) + EPS) * gain).astype(BF16)


def edge_kernel(video_hbm, text_hbm, mod_hbm, halo_ref, text_ref, mod_ref, sem):
    rows = video_hbm.shape[1]
    pairs = (
        (video_hbm.at[:, pl.ds(rows - 1, 1)], halo_ref),
        (mod_hbm, mod_ref),
        (text_hbm, text_ref),
    )
    copies = [pltpu.make_async_copy(src, dst, sem.at[i]) for i, (src, dst) in enumerate(pairs)]
    for c in copies:
        c.start()
    for c in copies:
        c.wait()


def edge(video, text, modulation):
    frames, _, cols, chans = video.shape
    return pl.pallas_call(
        edge_kernel,
        out_shape=(
            jax.ShapeDtypeStruct((frames, 1, cols, chans), BF16),
            jax.ShapeDtypeStruct(text.shape, BF16),
            jax.ShapeDtypeStruct(modulation.shape, F32),
        ),
        in_specs=[hbm_spec()] * 3,
        out_specs=(vmem_spec(),) * 3,
        scratch_shapes=[pltpu.SemaphoreType.DMA((3,))],
        compiler_params=params(4),
        cost_estimate=cost(0, 2 * nbytes(text, modulation)),
        name="edge",
    )(*[far(a) for a in (video, text, modulation)])


def add_text(stream, flat, acc_ref, fresh):
    step = 128
    row = lax.broadcasted_iota(jnp.int32, (2 * step, 2 * step), 0)
    col = lax.broadcasted_iota(jnp.int32, (2 * step, 2 * step), 1)
    pick = jnp.where(col == 2 * (row % step) + row // step, 1.0, 0.0).astype(BF16)
    pieces = ([], [])
    for at in range(0, flat.shape[0], 2 * step):
        both = dot(pick, flat[at : at + 2 * step, :]).astype(BF16)
        pieces[0].append(both[:step])
        pieces[1].append(both[step:])
    for p in range(2):
        term = dot(stream, jnp.concatenate(pieces[p], 0))
        if fresh:
            acc_ref[p] = term
        else:
            acc_ref[p] += term


def text_kernel(
    chunks,
    text_ref,
    mod_ref,
    w_hbm,
    video_hbm,
    conv_hbm,
    e_hbm,
    acc_ref,
    stream_ref,
    last_ref,
    video_ref,
    conv_ref,
    e_ref,
    w_ref,
    sem,
    w_sem,
):
    depth, parts, width = w_hbm.shape
    taken = w_ref.shape[0]
    deep = taken // chunks
    copies = [
        pltpu.make_async_copy(w_hbm.at[pl.ds(c * deep, deep)], w_ref.at[pl.ds(c * deep, deep)], w_sem.at[c])
        for c in range(chunks)
    ]
    pairs = (
        (video_hbm, video_ref),
        (conv_hbm, conv_ref),
        (e_hbm, e_ref),
        (w_hbm.at[pl.ds(taken, depth - taken)], last_ref),
    )
    ahead = [pltpu.make_async_copy(src, dst, sem.at[i]) for i, (src, dst) in enumerate(pairs)]
    for c in copies:
        c.start()
    few = 16
    for r in range(0, text_ref.shape[0], few):
        text = text_ref[r : r + few, :].astype(F32)
        centred = text - jnp.mean(text, -1, keepdims=True)
        normed = centred * lax.rsqrt(jnp.mean(centred * centred, -1, keepdims=True) + EPS)
        stream_ref[r : r + few, :] = (normed * (1.0 + mod_ref[3:4, :]) + mod_ref[2:3, :]).astype(BF16)
    flat = w_ref.reshape(taken * parts, width)
    for c in range(chunks):
        copies[c].wait()
        if c == 0:
            for copy in ahead:
                copy.start()
        at = slice(c * deep, (c + 1) * deep)
        add_text(stream_ref[:, at], flat.at[2 * c * deep : 2 * (c + 1) * deep], acc_ref, c == 0)
    for c in ahead:
        c.wait()


def text_side(text, modulation, weight, video, conv_weight, embed_weight):
    depth, parts, width = weight.shape
    count = text.shape[0]
    taken = depth * 2 // 3
    chunks = 2
    return pl.pallas_call(
        lambda *refs: text_kernel(chunks, *refs),
        out_shape=(
            jax.ShapeDtypeStruct((parts, count, width), F32),
            jax.ShapeDtypeStruct(text.shape, BF16),
            jax.ShapeDtypeStruct((depth - taken, parts, width), BF16),
            jax.ShapeDtypeStruct(video.shape, BF16),
            jax.ShapeDtypeStruct(conv_weight.shape, BF16),
            jax.ShapeDtypeStruct(embed_weight.shape, BF16),
        ),
        in_specs=[vmem_spec()] * 2 + [hbm_spec()] * 4,
        out_specs=(vmem_spec(),) * 6,
        scratch_shapes=[
            VMEM((taken, parts, width), BF16),
            pltpu.SemaphoreType.DMA((4,)),
            pltpu.SemaphoreType.DMA((chunks,)),
        ],
        compiler_params=params(20),
        cost_estimate=cost(4 * count * depth * parts * width, nbytes(weight, text, video, conv_weight)),
        name="text_side",
    )(text, modulation, *[far(a) for a in (weight, video, conv_weight, embed_weight)])


def fold_kernel(
    e_ref,
    mod_ref,
    gain_ref,
    w0_ref,
    part_ref,
    stream_ref,
    last_ref,
    w_hbm,
    rhs0_ref,
    rhs1_ref,
    shift_ref,
    gram_ref,
    key_ref,
    value_ref,
    lhs_ref,
    both_ref,
    acc_ref,
    sum_ref,
    w1_ref,
    sem,
):
    parts, deep0, width = w0_ref.shape
    pi, depth = e_ref.shape
    copies = [
        pltpu.make_async_copy(w_hbm.at[p, pl.ds(deep0, depth - deep0)], w1_ref.at[p], sem.at[p])
        for p in range(parts)
    ]
    for c in copies:
        c.start()
    last, _, _ = last_ref.shape
    add_text(stream_ref[:, depth - last :], last_ref.reshape(2 * last, width), sum_ref, True)
    for h in range(width // HS):
        at = slice(h * HS, (h + 1) * HS)
        key_ref[h] = head_norm(part_ref[0, :, at] + sum_ref[0, :, at], gain_ref[1:2, :])
        value_ref[h] = (part_ref[1, :, at] + sum_ref[1, :, at]).astype(BF16)
    few = 16
    for r in range(0, pi, few):
        e = e_ref[r : r + few, :].astype(F32)
        centred = e - jnp.mean(e, -1, keepdims=True)
        hi, lo = split(centred * (1.0 + mod_ref[1:2, :]))
        lhs_ref[r : r + few, :] = hi
        lhs_ref[pi + r : pi + r + few, :] = lo
        hi, lo = split(centred)
        both_ref[r : r + few, :] = hi
        both_ref[pi + r : pi + r + few, :] = lo
    shift_hi, shift_lo = split(mod_ref[0:1, :])
    lhs_ref[2 * pi :, :] = jnp.concatenate(
        [shift_hi.astype(F32), shift_lo.astype(F32), jnp.zeros((14, depth), F32)], 0
    ).astype(BF16)
    gram = dot_nt(both_ref[...], both_ref[...])
    lane = lax.broadcasted_iota(jnp.int32, (pi, 2 * pi), 1)
    gram = gram[:pi] + jnp.where(lane < pi, gram[pi:], 0.0)
    gram = gram + pltpu.roll(gram, pi, 1)
    gram = jnp.concatenate([gram, gram], 0)
    row = lax.broadcasted_iota(jnp.int32, gram.shape, 0) // pi
    col = lax.broadcasted_iota(jnp.int32, gram.shape, 1) // pi
    ghi, glo = split(jnp.where(row == col, gram * (1.0 / depth), 0.0))
    gram_ref[...] = jnp.concatenate([ghi, glo], 0)
    for p in range(parts):
        at = slice(p * width, (p + 1) * width)
        acc_ref[:, at] = dot(lhs_ref[:, :deep0], w0_ref[p])
    for p in range(parts):
        at = slice(p * width, (p + 1) * width)
        copies[p].wait()
        acc_ref[:, at] += dot(lhs_ref[:, deep0:], w1_ref[p])
    total = acc_ref[...]
    hi, lo = split(total[:pi] + total[pi : 2 * pi])
    none = jnp.zeros_like(hi)
    rhs0_ref[...] = jnp.concatenate([hi, none, lo, none], 0)
    rhs1_ref[...] = jnp.concatenate([none, hi, none, lo], 0)
    shift_ref[...] = total[2 * pi : 2 * pi + 1] + total[2 * pi + 1 : 2 * pi + 2]


def fold(embed_weight, modulation, gain, weight0, part, stream, last, weight):
    parts, taken, width = weight0.shape
    pi, depth = embed_weight.shape
    cols = parts * width
    count = stream.shape[0]
    heads = width // HS
    return pl.pallas_call(
        fold_kernel,
        out_shape=(
            jax.ShapeDtypeStruct((4 * pi, cols), BF16),
            jax.ShapeDtypeStruct((4 * pi, cols), BF16),
            jax.ShapeDtypeStruct((1, cols), F32),
            jax.ShapeDtypeStruct((4 * pi, 2 * pi), BF16),
            jax.ShapeDtypeStruct((heads, count, HS), BF16),
            jax.ShapeDtypeStruct((heads, count, HS), BF16),
        ),
        in_specs=[vmem_spec()] * 7 + [hbm_spec()],
        out_specs=(vmem_spec(),) * 6,
        scratch_shapes=[
            VMEM((2 * pi + 16, depth), BF16),
            VMEM((2 * pi, depth), BF16),
            VMEM((2 * pi + 16, cols), F32),
            VMEM(part.shape, F32),
            VMEM((parts, depth - taken, width), BF16),
            pltpu.SemaphoreType.DMA((parts,)),
        ],
        compiler_params=params(20),
        cost_estimate=cost(2 * 144 * depth * cols, nbytes(weight, embed_weight, modulation)),
        name="fold",
    )(embed_weight, modulation, gain, weight0, part, stream, last, far(weight))


def conv_kernel(
    chunks,
    video_ref,
    halo_ref,
    weight_ref,
    latent_ref,
    qkv_hbm,
    out_ref,
    qkv_ref,
    wide_ref,
    even_ref,
    odd_ref,
    left_ref,
    spread_ref,
    sem,
):
    deep = qkv_ref.shape[1] // chunks
    ahead = [
        pltpu.make_async_copy(
            qkv_hbm.at[p, pl.ds(c * deep, deep)], qkv_ref.at[p, pl.ds(c * deep, deep)], sem.at[p, c]
        )
        for p in range(qkv_ref.shape[0])
        for c in range(chunks)
    ]
    for copy in ahead:
        copy.start()
    frames, rows, cols, chans = video_ref.shape
    block = cols + 8
    half = cols // 2
    quarter = cols // 4
    for r in range(rows + 1):
        for f in range(frames):
            base = (r * frames + f) * block
            pixels = (halo_ref[f, 0] if r == 0 else video_ref[f, r - 1]).astype(F32)
            if r == 0:
                pixels = jnp.where(lax.axis_index("ctx") == 0, 0.0, pixels)
            wide_ref[base : base + 8, :] = jnp.zeros((8, chans), F32)
            wide_ref[base + 8 : base + block, :] = pixels
            at = [wide_ref[pl.ds(base + 7 + o, quarter, stride=4), :] for o in range(5)]
            even = jnp.concatenate([at[1], at[3]], 0).astype(BF16)
            odd = jnp.concatenate([at[2], at[4]], 0).astype(BF16)
            left = jnp.concatenate([at[0], at[2]], 0).astype(BF16)
            for t in (range(3) if f == 0 else (f + 2,)):
                even_ref[r, t] = even
                odd_ref[r, t] = odd
                left_ref[r, t] = left
    lat, mid = latent_ref.shape
    tall = rows // 2
    spread_ref[...] = jnp.zeros_like(spread_ref)
    for s in range(2 * tall):
        spread_ref[s * lat : (s + 1) * lat, s * mid : (s + 1) * mid] = latent_ref[...]
    pieces = []
    for j in range(tall):
        taps = []
        for kt in range(3):
            for kr in range(3):
                for ref in (left_ref, even_ref, odd_ref):
                    taps.append(ref[2 * j + kr, kt : kt + frames].reshape(frames * half, chans))
        conv = dot(jnp.concatenate(taps, 1), weight_ref[...])
        act = (conv * (1.0 / (1.0 + jnp.exp(-conv)))).astype(BF16)
        for b in range(2):
            pieces.append(
                jnp.concatenate(
                    [act[f * half + b * quarter : f * half + (b + 1) * quarter] for f in range(frames)], 0
                )
            )
    out_ref[...] = dot_nt(jnp.concatenate(pieces, 1), spread_ref[...]).astype(BF16)
    for copy in ahead:
        copy.wait()


def conv_side(video, halo, weight, latent_weight, qkv_weight, taken):
    frames, rows, cols, chans = video.shape
    parts, depth, width = qkv_weight.shape
    mid = weight.shape[-1]
    lat = latent_weight.shape[1]
    latent = latent_weight.T
    half = cols // 2
    tall = rows // 2
    chunks = 1
    return pl.pallas_call(
        lambda *refs: conv_kernel(chunks, *refs),
        out_shape=(
            jax.ShapeDtypeStruct((frames * half // 2, 2 * tall * lat), BF16),
            jax.ShapeDtypeStruct((parts, taken, width), BF16),
        ),
        in_specs=[vmem_spec()] * 4 + [hbm_spec()],
        out_specs=(vmem_spec(),) * 2,
        scratch_shapes=[VMEM(((rows + 1) * frames * (cols + 8), chans), F32)]
        + [VMEM((rows + 1, frames + 2, half, chans), BF16)] * 3
        + [VMEM((2 * tall * lat, 2 * tall * mid), BF16), pltpu.SemaphoreType.DMA((parts, chunks))],
        compiler_params=params(24),
        cost_estimate=cost(
            2 * frames * tall * half * 27 * chans * mid, nbytes(video, halo, weight)
        ),
        name="conv_side",
    )(video, halo, weight, latent, far(qkv_weight))


def token_scales(x, xx, gram_ref):
    quad = dot(xx, gram_ref[...]) * x.astype(F32)
    lane = lax.broadcasted_iota(jnp.int32, quad.shape, 1)
    low = lane < quad.shape[1] // 2
    scales = []
    for i in range(2):
        var = jnp.sum(jnp.where(low if i == 0 else ~low, quad, 0.0), -1, keepdims=True)
        scales.append(lax.rsqrt(jnp.maximum(var, 0.0) + EPS))
    return scales


def block_queries(n, own, x, xx, scales, rhs_refs, shift_ref, gain_ref, query_ref):
    heads = query_ref.shape[0]
    rows = x.shape[1]
    span = rows // n
    grain = span // own
    gain = gain_ref[0:1, :] * (math.log2(math.e) / math.sqrt(HS))
    for i in range(2):
        at = slice(0, heads * HS)
        projected = dot(xx, rhs_refs[i][:, at]) * scales[i] + shift_ref[:, at]
        for h in range(heads):
            v = head_norm(projected[:, h * HS : (h + 1) * HS], gain)
            for j in range(x.shape[0] // rows):
                for s in range(n):
                    for f in range(own):
                        to = 2 * j * rows + f * (n * 2 * grain) + (s * 2 + i) * grain
                        come = j * rows + s * span + f * grain
                        query_ref[h, to : to + grain, :] = v[come : come + grain]


def attention(query_ref, key_ref, value_ref, out_refs):
    heads, total, _ = key_ref.shape
    rows = query_ref.shape[1] // len(out_refs)
    for j in range(0, len(out_refs), 2):
        group = out_refs[j : j + 2]
        for h in range(heads):
            query = query_ref[h, j * rows : (j + len(group)) * rows, :]
            weights = jnp.exp2(dot_nt(query, key_ref[h]))
            norm = weights[:, :HS]
            for c in range(HS, total, HS):
                norm = norm + weights[:, c : c + HS]
            norm = jnp.sum(norm, -1, keepdims=True)
            attended = (dot(weights.astype(BF16), value_ref[h]) / norm).astype(BF16)
            for g, ref in enumerate(group):
                ref[:, h * HS : (h + 1) * HS] = attended[g * rows : (g + 1) * rows]


def first_kernel(order, frames, *refs):
    n = len(order)
    patch_refs = refs[:n]
    rhs0_ref, rhs1_ref, shift_ref, gram_ref, gain_ref, tkey_ref, tvalue_ref = refs[n : n + 7]
    out_ref, x_ref, key_ref, value_ref, patch_scr, query_ref = refs[n + 7 :]
    me = lax.axis_index("ctx")
    rhs_refs = (rhs0_ref, rhs1_ref)
    heads, count, _ = tkey_ref.shape
    rows = patch_refs[0].shape[1]
    for k, ref in zip(order, patch_refs):
        patch_scr[pl.ds(pl.multiple_of((me ^ k) * rows, rows), rows), :] = ref[...]
    key_ref[:, 0:count, :] = tkey_ref[...]
    value_ref[:, 0:count, :] = tvalue_ref[...]
    own = frames // n
    span = rows // n
    for j, k in enumerate(order):
        for s in range(n):
            at = pl.multiple_of((me ^ k) * span, span) + s * rows
            x_ref[j * rows + s * span : j * rows + (s + 1) * span, :] = patch_scr[
                pl.ds(pl.multiple_of(at, span), span), :
            ]
    x = x_ref[...]
    xx = jnp.concatenate([x, x], 1)
    scales = token_scales(x, xx, gram_ref)
    width = heads * HS
    for i in range(2):
        for p in (1, 2):
            for h0 in range(0, heads, 2):
                at = slice(p * width + h0 * HS, p * width + (h0 + 2) * HS)
                pair = dot(xx, rhs_refs[i][:, at]) * scales[i] + shift_ref[:, at]
                for h in (h0, h0 + 1):
                    v = pair[:, (h - h0) * HS : (h - h0 + 1) * HS]
                    to = slice(count + i * n * rows, count + (i + 1) * n * rows)
                    if p == 1:
                        key_ref[h, to, :] = head_norm(v, gain_ref[1:2, :])
                    else:
                        value_ref[h, to, :] = v.astype(BF16)
    block_queries(
        n, own, x[:rows], xx[:rows], [v[:rows] for v in scales], rhs_refs, shift_ref, gain_ref, query_ref
    )
    attention(query_ref, key_ref, value_ref, (out_ref,))


def first_block(order, frames, patches, rhs0, rhs1, shift, gram, gain, tkey, tvalue):
    n = len(order)
    heads, count, _ = tkey.shape
    rows = patches[0].shape[1]
    total = count + 2 * n * rows
    return pl.pallas_call(
        lambda *refs: first_kernel(order, frames, *refs),
        out_shape=(
            jax.ShapeDtypeStruct((2 * rows, heads * HS), BF16),
            jax.ShapeDtypeStruct((n * rows, rows), BF16),
            jax.ShapeDtypeStruct((heads, total, HS), BF16),
            jax.ShapeDtypeStruct((heads, total, HS), BF16),
        ),
        in_specs=[vmem_spec()] * (n + 7),
        out_specs=(vmem_spec(),) * 4,
        scratch_shapes=[VMEM((n * rows, rows), BF16), VMEM((heads, 2 * rows, HS), BF16)],
        compiler_params=params(16),
        cost_estimate=cost(2 * 2 * n * rows * 256 * 3 * heads * HS, 4 * nbytes(rhs0)),
        name="first_block",
    )(*patches, rhs0, rhs1, shift, gram, gain, tkey, tvalue)


def attend_kernel(
    n, own, first, x_ref, rhs0_ref, rhs1_ref, shift_ref, gram_ref, gain_ref, key_ref, value_ref, *refs
):
    out_refs, query_ref = refs[:-1], refs[-1]
    rows = x_ref.shape[1]
    x = x_ref[first * rows : (first + len(out_refs)) * rows, :]
    xx = jnp.concatenate([x, x], 1)
    scales = token_scales(x, xx, gram_ref)
    block_queries(n, own, x, xx, scales, (rhs0_ref, rhs1_ref), shift_ref, gain_ref, query_ref)
    attention(query_ref, key_ref, value_ref, out_refs)


def attend(n, frames, first, count, x, rhs0, rhs1, shift, gram, gain, key, value):
    heads = key.shape[0]
    rows = x.shape[1]
    return pl.pallas_call(
        lambda *refs: attend_kernel(n, frames // n, first, *refs),
        out_shape=(jax.ShapeDtypeStruct((2 * rows, heads * HS), BF16),) * count,
        in_specs=[vmem_spec()] * 8,
        out_specs=(vmem_spec(),) * count,
        scratch_shapes=[VMEM((heads, count * 2 * rows, HS), BF16)],
        compiler_params=params(20),
        cost_estimate=cost(heads * rows * HS, 2 * nbytes(x)),
        name="attend",
    )(x, rhs0, rhs1, shift, gram, gain, key, value)


def place(block, k, out_ref, sem):
    width = block.shape[1]
    at = pl.multiple_of((lax.axis_index("ctx") ^ k) * width, width)
    return pltpu.make_async_copy(block, out_ref.at[:, pl.ds(at, width)], sem)


def own_kernel(
    n,
    own,
    far,
    far_ref,
    x_ref,
    rhs0_ref,
    rhs1_ref,
    shift_ref,
    gram_ref,
    gain_ref,
    key_ref,
    value_ref,
    out_ref,
    query_ref,
    block_ref,
    sem,
):
    first = place(far_ref, far, out_ref, sem.at[0])
    first.start()
    attend_kernel(
        n,
        own,
        n - 1,
        x_ref,
        rhs0_ref,
        rhs1_ref,
        shift_ref,
        gram_ref,
        gain_ref,
        key_ref,
        value_ref,
        block_ref,
        query_ref,
    )
    second = place(block_ref, 0, out_ref, sem.at[1])
    second.start()
    first.wait()
    second.wait()


def own_block(n, frames, far, far_block, x, rhs0, rhs1, shift, gram, gain, key, value):
    heads = key.shape[0]
    rows = x.shape[1]
    width = heads * HS
    return pl.pallas_call(
        lambda *refs: own_kernel(n, frames // n, far, *refs),
        out_shape=jax.ShapeDtypeStruct((2 * rows, n * width), BF16),
        in_specs=[vmem_spec()] * 9,
        out_specs=hbm_spec(),
        scratch_shapes=[
            VMEM((heads, 2 * rows, HS), BF16),
            VMEM((2 * rows, width), BF16),
            pltpu.SemaphoreType.DMA((2,)),
        ],
        compiler_params=params(12),
        cost_estimate=cost(heads * rows * HS, 2 * nbytes(x)),
        name="own_block",
    )(far_block, x, rhs0, rhs1, shift, gram, gain, key, value)


def rest_kernel(order, out_in_ref, *refs):
    n = len(order)
    out_ref, sem = refs[n:]
    copies = [place(refs[j], k, out_ref, sem.at[j]) for j, k in enumerate(order)]
    for c in copies:
        c.start()
    for c in copies:
        c.wait()


def rest(order, out, blocks):
    n = len(order)
    return pl.pallas_call(
        lambda *refs: rest_kernel(order, *refs),
        out_shape=jax.ShapeDtypeStruct(out.shape, BF16),
        in_specs=[hbm_spec()] + [vmem_spec()] * n,
        out_specs=hbm_spec(),
        scratch_shapes=[pltpu.SemaphoreType.DMA((n,))],
        input_output_aliases={0: 0},
        compiler_params=params(4),
        cost_estimate=cost(0, 2 * n * nbytes(blocks[0])),
        name="rest",
    )(out, *blocks)


def shards(video, conv_weight, latent_weight, embed_weight, modulation, qkv_weight, qk_gain, text, text_weight):
    n = lax.axis_size("ctx")
    frames = video.shape[0]

    def swap(x, k):
        return lax.ppermute(x, "ctx", [(i, i ^ k) for i in range(n)])

    weight = qkv_weight.transpose(1, 0, 2)
    edge_row, text_near, mod_near = edge(video, text, modulation)
    halo = lax.ppermute(edge_row, "ctx", [(i, (i + 1) % n) for i in range(n)])
    part, stream, last, tile, taps, e_near = text_side(
        text_near,
        mod_near,
        text_weight,
        video,
        conv_weight.reshape(-1, conv_weight.shape[-1]),
        embed_weight,
    )
    patches, weight_near = conv_side(tile, halo, taps, latent_weight, weight, weight.shape[1] * 2 // 3)
    order = tuple(range(n - 1, -1, -1))
    received = [swap(patches, k) if k else patches for k in order]
    rhs0, rhs1, shift, gram, tkey, tvalue = fold(
        e_near, mod_near, qk_gain, weight_near, part, stream, last, weight
    )
    block, x, key, value = first_block(
        order, frames, received, rhs0, rhs1, shift, gram, qk_gain, tkey, tvalue
    )
    far_block = swap(block, order[0])
    common = (x, rhs0, rhs1, shift, gram, qk_gain, key, value)
    blocks = [swap(b, k) for b, k in zip(attend(n, frames, 1, n - 2, *common), order[1:])]
    out = own_block(n, frames, order[0], far_block, *common)
    return rest(order[1 : n - 1], out, blocks)


def solution(mesh):
    in_specs = (
        P("dp", "ctx", None, None),
        P(),
        P(),
        P(),
        P("dp", None),
        P(None, None, "ctx"),
        P(),
        P("dp", None),
        P(None, None, "ctx"),
    )
    out_specs = P(("dp", "ctx"), None)
    return jax.shard_map(shards, mesh=mesh, in_specs=in_specs, out_specs=out_specs, check_vma=False)
```

```python
import math

import jax
import jax.numpy as jnp
from jax import lax
from jax.experimental import pallas as pl
from jax.experimental.pallas import tpu as pltpu
from jax.sharding import PartitionSpec as P

HS = 128
EPS = 1e-06
F32 = jnp.float32
BF16 = jnp.bfloat16
VMEM = pltpu.VMEM
MIB = 1024 * 1024


def vmem_spec():
    return pl.BlockSpec(memory_space=pltpu.VMEM)


def hbm_spec():
    return pl.BlockSpec(memory_space=pltpu.HBM)


def far(x):
    return pltpu.with_memory_space_constraint(x, pltpu.HBM)


def params(mib):
    return pltpu.CompilerParams(vmem_limit_bytes=mib * MIB)


def cost(flops, bytes_accessed, transcendentals=0):
    return pl.CostEstimate(
        flops=int(flops), bytes_accessed=int(bytes_accessed), transcendentals=int(transcendentals)
    )


def nbytes(*arrays):
    return sum(math.prod(a.shape) * a.dtype.itemsize for a in arrays)


def split(x):
    hi = x.astype(BF16)
    return hi, (x - hi.astype(F32)).astype(BF16)


def dot(a, b):
    return jnp.dot(a, b, preferred_element_type=F32)


def dot_nt(a, b):
    return lax.dot_general(a, b, (((1,), (1,)), ((), ())), preferred_element_type=F32)


def head_norm(v, gain):
    return (v * lax.rsqrt(jnp.mean(v * v, -1, keepdims=True) + EPS) * gain).astype(BF16)


def edge_kernel(video_hbm, e_hbm, mod_hbm, halo_ref, e_ref, mod_ref, sem):
    rows = video_hbm.shape[1]
    pairs = (
        (video_hbm.at[:, pl.ds(rows - 1, 1)], halo_ref),
        (e_hbm, e_ref),
        (mod_hbm, mod_ref),
    )
    copies = [pltpu.make_async_copy(src, dst, sem.at[i]) for i, (src, dst) in enumerate(pairs)]
    for c in copies:
        c.start()
    for c in copies:
        c.wait()


def edge(video, embed_weight, modulation):
    frames, _, cols, chans = video.shape
    return pl.pallas_call(
        edge_kernel,
        out_shape=(
            jax.ShapeDtypeStruct((frames, 1, cols, chans), BF16),
            jax.ShapeDtypeStruct(embed_weight.shape, BF16),
            jax.ShapeDtypeStruct(modulation.shape, F32),
        ),
        in_specs=[hbm_spec()] * 3,
        out_specs=(vmem_spec(),) * 3,
        scratch_shapes=[pltpu.SemaphoreType.DMA((3,))],
        compiler_params=params(4),
        cost_estimate=cost(0, 2 * nbytes(embed_weight, modulation)),
        name="edge",
    )(*[far(a) for a in (video, embed_weight, modulation)])


def add_text(stream, flat, acc_ref, fresh):
    step = 128
    row = lax.broadcasted_iota(jnp.int32, (2 * step, 2 * step), 0)
    col = lax.broadcasted_iota(jnp.int32, (2 * step, 2 * step), 1)
    pick = jnp.where(col == 2 * (row % step) + row // step, 1.0, 0.0).astype(BF16)
    pieces = ([], [])
    for at in range(0, flat.shape[0], 2 * step):
        both = dot(pick, flat[at : at + 2 * step, :]).astype(BF16)
        pieces[0].append(both[:step])
        pieces[1].append(both[step:])
    for p in range(2):
        term = dot(stream, jnp.concatenate(pieces[p], 0))
        if fresh:
            acc_ref[p] = term
        else:
            acc_ref[p] += term


def embed_side(e_ref, mod_ref, lhs_ref, gram_ref, centred_ref):
    pi, depth = e_ref.shape
    few = 16
    for r in range(0, pi, few):
        e = e_ref[r : r + few, :].astype(F32)
        centred = e - jnp.mean(e, -1, keepdims=True)
        lhs_ref[r : r + few, :] = (centred * (1.0 + mod_ref[1:2, :])).astype(BF16)
        centred = centred.astype(BF16)
        centred_ref[r : r + few, :] = centred
        centred_ref[pi + r : pi + r + few, :] = centred
    shift_hi, shift_lo = split(mod_ref[0:1, :])
    lhs_ref[pi:, :] = jnp.concatenate(
        [shift_hi.astype(F32), shift_lo.astype(F32), jnp.zeros((few - 2, depth), F32)], 0
    ).astype(BF16)
    gram = dot_nt(centred_ref[...], centred_ref[...])
    row = lax.broadcasted_iota(jnp.int32, gram.shape, 0) // pi
    col = lax.broadcasted_iota(jnp.int32, gram.shape, 1) // pi
    ghi, glo = split(jnp.where(row == col, gram * (1.0 / depth), 0.0))
    gram_ref[...] = jnp.concatenate([ghi, glo], 0)


def text_kernel(
    chunks,
    e_ref,
    mod_ref,
    text_hbm,
    w_hbm,
    video_hbm,
    conv_hbm,
    lhs_ref,
    gram_ref,
    acc_ref,
    stream_ref,
    last_ref,
    video_ref,
    conv_ref,
    text_ref,
    centred_ref,
    w_ref,
    sem,
    w_sem,
):
    depth, parts, width = w_hbm.shape
    taken = w_ref.shape[0]
    deep = taken // chunks
    copies = [
        pltpu.make_async_copy(w_hbm.at[pl.ds(c * deep, deep)], w_ref.at[pl.ds(c * deep, deep)], w_sem.at[c])
        for c in range(chunks)
    ]
    first = pltpu.make_async_copy(text_hbm, text_ref, sem.at[3])
    pairs = (
        (video_hbm, video_ref),
        (conv_hbm, conv_ref),
        (w_hbm.at[pl.ds(taken, depth - taken)], last_ref),
    )
    ahead = [pltpu.make_async_copy(src, dst, sem.at[i]) for i, (src, dst) in enumerate(pairs)]
    first.start()
    for c in copies:
        c.start()
    embed_side(e_ref, mod_ref, lhs_ref, gram_ref, centred_ref)
    first.wait()
    few = 16
    for r in range(0, text_ref.shape[0], few):
        text = text_ref[r : r + few, :].astype(F32)
        centred = text - jnp.mean(text, -1, keepdims=True)
        normed = centred * lax.rsqrt(jnp.mean(centred * centred, -1, keepdims=True) + EPS)
        stream_ref[r : r + few, :] = (normed * (1.0 + mod_ref[3:4, :]) + mod_ref[2:3, :]).astype(BF16)
    flat = w_ref.reshape(taken * parts, width)
    for c in range(chunks):
        copies[c].wait()
        if c == 0:
            for copy in ahead:
                copy.start()
        at = slice(c * deep, (c + 1) * deep)
        add_text(stream_ref[:, at], flat.at[2 * c * deep : 2 * (c + 1) * deep], acc_ref, c == 0)
    for c in ahead:
        c.wait()


def text_side(embed_weight, modulation, text, weight, video, conv_weight):
    depth, parts, width = weight.shape
    count = text.shape[0]
    pi = embed_weight.shape[0]
    taken = depth * 2 // 3
    chunks = 2
    return pl.pallas_call(
        lambda *refs: text_kernel(chunks, *refs),
        out_shape=(
            jax.ShapeDtypeStruct((pi + 16, depth), BF16),
            jax.ShapeDtypeStruct((4 * pi, 2 * pi), BF16),
            jax.ShapeDtypeStruct((parts, count, width), F32),
            jax.ShapeDtypeStruct(text.shape, BF16),
            jax.ShapeDtypeStruct((depth - taken, parts, width), BF16),
            jax.ShapeDtypeStruct(video.shape, BF16),
            jax.ShapeDtypeStruct(conv_weight.shape, BF16),
        ),
        in_specs=[vmem_spec()] * 2 + [hbm_spec()] * 4,
        out_specs=(vmem_spec(),) * 7,
        scratch_shapes=[
            VMEM(text.shape, BF16),
            VMEM((2 * pi, depth), BF16),
            VMEM((taken, parts, width), BF16),
            pltpu.SemaphoreType.DMA((4,)),
            pltpu.SemaphoreType.DMA((chunks,)),
        ],
        compiler_params=params(20),
        cost_estimate=cost(4 * count * depth * parts * width, nbytes(weight, text, video, conv_weight)),
        name="text_side",
    )(embed_weight, modulation, *[far(a) for a in (text, weight, video, conv_weight)])


def fold_kernel(
    lhs_ref,
    gain_ref,
    w0_ref,
    part_ref,
    stream_ref,
    last_ref,
    w_hbm,
    rhs0_ref,
    rhs1_ref,
    shift_ref,
    key_ref,
    value_ref,
    acc_ref,
    sum_ref,
    w1_ref,
    sem,
):
    parts, deep0, width = w0_ref.shape
    depth = lhs_ref.shape[1]
    pi = lhs_ref.shape[0] - 16
    copies = [
        pltpu.make_async_copy(w_hbm.at[p, pl.ds(deep0, depth - deep0)], w1_ref.at[p], sem.at[p])
        for p in range(parts)
    ]
    for c in copies:
        c.start()
    last, _, _ = last_ref.shape
    add_text(stream_ref[:, depth - last :], last_ref.reshape(2 * last, width), sum_ref, True)
    for h in range(width // HS):
        at = slice(h * HS, (h + 1) * HS)
        key_ref[h] = head_norm(part_ref[0, :, at] + sum_ref[0, :, at], gain_ref[1:2, :])
        value_ref[h] = (part_ref[1, :, at] + sum_ref[1, :, at]).astype(BF16)
    for p in range(parts):
        at = slice(p * width, (p + 1) * width)
        acc_ref[:, at] = dot(lhs_ref[:, :deep0], w0_ref[p])
    for p in range(parts):
        at = slice(p * width, (p + 1) * width)
        copies[p].wait()
        acc_ref[:, at] += dot(lhs_ref[:, deep0:], w1_ref[p])
    total = acc_ref[...]
    hi, lo = split(total[:pi])
    none = jnp.zeros_like(hi)
    rhs0_ref[...] = jnp.concatenate([hi, none, lo, none], 0)
    rhs1_ref[...] = jnp.concatenate([none, hi, none, lo], 0)
    shift_ref[...] = total[pi : pi + 1] + total[pi + 1 : pi + 2]


def fold(lhs, gain, weight0, part, stream, last, weight):
    parts, taken, width = weight0.shape
    rows, depth = lhs.shape
    cols = parts * width
    count = stream.shape[0]
    heads = width // HS
    return pl.pallas_call(
        fold_kernel,
        out_shape=(
            jax.ShapeDtypeStruct((4 * (rows - 16), cols), BF16),
            jax.ShapeDtypeStruct((4 * (rows - 16), cols), BF16),
            jax.ShapeDtypeStruct((1, cols), F32),
            jax.ShapeDtypeStruct((heads, count, HS), BF16),
            jax.ShapeDtypeStruct((heads, count, HS), BF16),
        ),
        in_specs=[vmem_spec()] * 6 + [hbm_spec()],
        out_specs=(vmem_spec(),) * 5,
        scratch_shapes=[
            VMEM((rows, cols), F32),
            VMEM(part.shape, F32),
            VMEM((parts, depth - taken, width), BF16),
            pltpu.SemaphoreType.DMA((parts,)),
        ],
        compiler_params=params(20),
        cost_estimate=cost(2 * 144 * depth * cols, nbytes(weight)),
        name="fold",
    )(lhs, gain, weight0, part, stream, last, far(weight))


def conv_kernel(
    chunks,
    video_ref,
    halo_ref,
    weight_ref,
    latent_ref,
    qkv_hbm,
    out_ref,
    qkv_ref,
    wide_ref,
    even_ref,
    odd_ref,
    left_ref,
    spread_ref,
    sem,
):
    deep = qkv_ref.shape[1] // chunks
    ahead = [
        pltpu.make_async_copy(
            qkv_hbm.at[p, pl.ds(c * deep, deep)], qkv_ref.at[p, pl.ds(c * deep, deep)], sem.at[p, c]
        )
        for p in range(qkv_ref.shape[0])
        for c in range(chunks)
    ]
    for copy in ahead:
        copy.start()
    frames, rows, cols, chans = video_ref.shape
    block = cols + 8
    half = cols // 2
    quarter = cols // 4
    for r in range(rows + 1):
        for f in range(frames):
            base = (r * frames + f) * block
            pixels = (halo_ref[f, 0] if r == 0 else video_ref[f, r - 1]).astype(F32)
            if r == 0:
                pixels = jnp.where(lax.axis_index("ctx") == 0, 0.0, pixels)
            wide_ref[base : base + 8, :] = jnp.zeros((8, chans), F32)
            wide_ref[base + 8 : base + block, :] = pixels
            at = [wide_ref[pl.ds(base + 7 + o, quarter, stride=4), :] for o in range(5)]
            even = jnp.concatenate([at[1], at[3]], 0).astype(BF16)
            odd = jnp.concatenate([at[2], at[4]], 0).astype(BF16)
            left = jnp.concatenate([at[0], at[2]], 0).astype(BF16)
            for t in (range(3) if f == 0 else (f + 2,)):
                even_ref[r, t] = even
                odd_ref[r, t] = odd
                left_ref[r, t] = left
    lat, mid = latent_ref.shape
    tall = rows // 2
    spread_ref[...] = jnp.zeros_like(spread_ref)
    for s in range(2 * tall):
        spread_ref[s * lat : (s + 1) * lat, s * mid : (s + 1) * mid] = latent_ref[...]
    pieces = []
    for j in range(tall):
        taps = []
        for kt in range(3):
            for kr in range(3):
                for ref in (left_ref, even_ref, odd_ref):
                    taps.append(ref[2 * j + kr, kt : kt + frames].reshape(frames * half, chans))
        conv = dot(jnp.concatenate(taps, 1), weight_ref[...])
        act = (conv * (1.0 / (1.0 + jnp.exp(-conv)))).astype(BF16)
        for b in range(2):
            pieces.append(
                jnp.concatenate(
                    [act[f * half + b * quarter : f * half + (b + 1) * quarter] for f in range(frames)], 0
                )
            )
    out_ref[...] = dot_nt(jnp.concatenate(pieces, 1), spread_ref[...]).astype(BF16)
    for copy in ahead:
        copy.wait()


def conv_side(video, halo, weight, latent_weight, qkv_weight, taken):
    frames, rows, cols, chans = video.shape
    parts, depth, width = qkv_weight.shape
    mid = weight.shape[-1]
    lat = latent_weight.shape[1]
    latent = latent_weight.T
    half = cols // 2
    tall = rows // 2
    chunks = 1
    return pl.pallas_call(
        lambda *refs: conv_kernel(chunks, *refs),
        out_shape=(
            jax.ShapeDtypeStruct((frames * half // 2, 2 * tall * lat), BF16),
            jax.ShapeDtypeStruct((parts, taken, width), BF16),
        ),
        in_specs=[vmem_spec()] * 4 + [hbm_spec()],
        out_specs=(vmem_spec(),) * 2,
        scratch_shapes=[VMEM(((rows + 1) * frames * (cols + 8), chans), F32)]
        + [VMEM((rows + 1, frames + 2, half, chans), BF16)] * 3
        + [VMEM((2 * tall * lat, 2 * tall * mid), BF16), pltpu.SemaphoreType.DMA((parts, chunks))],
        compiler_params=params(24),
        cost_estimate=cost(
            2 * frames * tall * half * 27 * chans * mid, nbytes(video, halo, weight)
        ),
        name="conv_side",
    )(video, halo, weight, latent, far(qkv_weight))


def token_scales(x, xx, gram_ref):
    quad = dot(xx, gram_ref[...]) * x.astype(F32)
    lane = lax.broadcasted_iota(jnp.int32, quad.shape, 1)
    low = lane < quad.shape[1] // 2
    scales = []
    for i in range(2):
        var = jnp.sum(jnp.where(low if i == 0 else ~low, quad, 0.0), -1, keepdims=True)
        scales.append(lax.rsqrt(jnp.maximum(var, 0.0) + EPS))
    return scales


def block_queries(n, own, x, xx, scales, rhs_refs, shift_ref, gain_ref, query_ref):
    heads = query_ref.shape[0]
    rows = x.shape[1]
    span = rows // n
    grain = span // own
    gain = gain_ref[0:1, :] * (math.log2(math.e) / math.sqrt(HS))
    for i in range(2):
        at = slice(0, heads * HS)
        projected = dot(xx, rhs_refs[i][:, at]) * scales[i] + shift_ref[:, at]
        for h in range(heads):
            v = head_norm(projected[:, h * HS : (h + 1) * HS], gain)
            for j in range(x.shape[0] // rows):
                for s in range(n):
                    for f in range(own):
                        to = 2 * j * rows + f * (n * 2 * grain) + (s * 2 + i) * grain
                        come = j * rows + s * span + f * grain
                        query_ref[h, to : to + grain, :] = v[come : come + grain]


def attention(query_ref, key_ref, value_ref, out_refs):
    heads, total, _ = key_ref.shape
    rows = query_ref.shape[1] // len(out_refs)
    for j in range(0, len(out_refs), 2):
        group = out_refs[j : j + 2]
        for h in range(heads):
            query = query_ref[h, j * rows : (j + len(group)) * rows, :]
            weights = jnp.exp2(dot_nt(query, key_ref[h]))
            norm = weights[:, :HS]
            for c in range(HS, total, HS):
                norm = norm + weights[:, c : c + HS]
            norm = jnp.sum(norm, -1, keepdims=True)
            attended = (dot(weights.astype(BF16), value_ref[h]) / norm).astype(BF16)
            for g, ref in enumerate(group):
                ref[:, h * HS : (h + 1) * HS] = attended[g * rows : (g + 1) * rows]


def first_kernel(order, frames, *refs):
    n = len(order)
    patch_refs = refs[:n]
    rhs0_ref, rhs1_ref, shift_ref, gram_ref, gain_ref, tkey_ref, tvalue_ref = refs[n : n + 7]
    out_ref, x_ref, key_ref, value_ref, patch_scr, query_ref = refs[n + 7 :]
    me = lax.axis_index("ctx")
    rhs_refs = (rhs0_ref, rhs1_ref)
    heads, count, _ = tkey_ref.shape
    rows = patch_refs[0].shape[1]
    for k, ref in zip(order, patch_refs):
        patch_scr[pl.ds(pl.multiple_of((me ^ k) * rows, rows), rows), :] = ref[...]
    key_ref[:, 0:count, :] = tkey_ref[...]
    value_ref[:, 0:count, :] = tvalue_ref[...]
    own = frames // n
    span = rows // n
    for j, k in enumerate(order):
        for s in range(n):
            at = pl.multiple_of((me ^ k) * span, span) + s * rows
            x_ref[j * rows + s * span : j * rows + (s + 1) * span, :] = patch_scr[
                pl.ds(pl.multiple_of(at, span), span), :
            ]
    x = x_ref[...]
    xx = jnp.concatenate([x, x], 1)
    scales = token_scales(x, xx, gram_ref)
    width = heads * HS
    for i in range(2):
        for p in (1, 2):
            for h0 in range(0, heads, 2):
                at = slice(p * width + h0 * HS, p * width + (h0 + 2) * HS)
                pair = dot(xx, rhs_refs[i][:, at]) * scales[i] + shift_ref[:, at]
                for h in (h0, h0 + 1):
                    v = pair[:, (h - h0) * HS : (h - h0 + 1) * HS]
                    to = slice(count + i * n * rows, count + (i + 1) * n * rows)
                    if p == 1:
                        key_ref[h, to, :] = head_norm(v, gain_ref[1:2, :])
                    else:
                        value_ref[h, to, :] = v.astype(BF16)
    block_queries(
        n, own, x[:rows], xx[:rows], [v[:rows] for v in scales], rhs_refs, shift_ref, gain_ref, query_ref
    )
    attention(query_ref, key_ref, value_ref, (out_ref,))


def first_block(order, frames, patches, rhs0, rhs1, shift, gram, gain, tkey, tvalue):
    n = len(order)
    heads, count, _ = tkey.shape
    rows = patches[0].shape[1]
    total = count + 2 * n * rows
    return pl.pallas_call(
        lambda *refs: first_kernel(order, frames, *refs),
        out_shape=(
            jax.ShapeDtypeStruct((2 * rows, heads * HS), BF16),
            jax.ShapeDtypeStruct((n * rows, rows), BF16),
            jax.ShapeDtypeStruct((heads, total, HS), BF16),
            jax.ShapeDtypeStruct((heads, total, HS), BF16),
        ),
        in_specs=[vmem_spec()] * (n + 7),
        out_specs=(vmem_spec(),) * 4,
        scratch_shapes=[VMEM((n * rows, rows), BF16), VMEM((heads, 2 * rows, HS), BF16)],
        compiler_params=params(16),
        cost_estimate=cost(2 * 2 * n * rows * 256 * 3 * heads * HS, 4 * nbytes(rhs0)),
        name="first_block",
    )(*patches, rhs0, rhs1, shift, gram, gain, tkey, tvalue)


def attend_kernel(
    n, own, first, x_ref, rhs0_ref, rhs1_ref, shift_ref, gram_ref, gain_ref, key_ref, value_ref, *refs
):
    out_refs, query_ref = refs[:-1], refs[-1]
    rows = x_ref.shape[1]
    x = x_ref[first * rows : (first + len(out_refs)) * rows, :]
    xx = jnp.concatenate([x, x], 1)
    scales = token_scales(x, xx, gram_ref)
    block_queries(n, own, x, xx, scales, (rhs0_ref, rhs1_ref), shift_ref, gain_ref, query_ref)
    attention(query_ref, key_ref, value_ref, out_refs)


def attend(n, frames, first, count, x, rhs0, rhs1, shift, gram, gain, key, value):
    heads = key.shape[0]
    rows = x.shape[1]
    return pl.pallas_call(
        lambda *refs: attend_kernel(n, frames // n, first, *refs),
        out_shape=(jax.ShapeDtypeStruct((2 * rows, heads * HS), BF16),) * count,
        in_specs=[vmem_spec()] * 8,
        out_specs=(vmem_spec(),) * count,
        scratch_shapes=[VMEM((heads, count * 2 * rows, HS), BF16)],
        compiler_params=params(20),
        cost_estimate=cost(heads * rows * HS, 2 * nbytes(x)),
        name="attend",
    )(x, rhs0, rhs1, shift, gram, gain, key, value)


def place(block, k, out_ref, sem):
    width = block.shape[1]
    at = pl.multiple_of((lax.axis_index("ctx") ^ k) * width, width)
    return pltpu.make_async_copy(block, out_ref.at[:, pl.ds(at, width)], sem)


def own_kernel(
    n,
    own,
    far,
    far_ref,
    x_ref,
    rhs0_ref,
    rhs1_ref,
    shift_ref,
    gram_ref,
    gain_ref,
    key_ref,
    value_ref,
    out_ref,
    query_ref,
    block_ref,
    sem,
):
    first = place(far_ref, far, out_ref, sem.at[0])
    first.start()
    attend_kernel(
        n,
        own,
        n - 1,
        x_ref,
        rhs0_ref,
        rhs1_ref,
        shift_ref,
        gram_ref,
        gain_ref,
        key_ref,
        value_ref,
        block_ref,
        query_ref,
    )
    second = place(block_ref, 0, out_ref, sem.at[1])
    second.start()
    first.wait()
    second.wait()


def own_block(n, frames, far, far_block, x, rhs0, rhs1, shift, gram, gain, key, value):
    heads = key.shape[0]
    rows = x.shape[1]
    width = heads * HS
    return pl.pallas_call(
        lambda *refs: own_kernel(n, frames // n, far, *refs),
        out_shape=jax.ShapeDtypeStruct((2 * rows, n * width), BF16),
        in_specs=[vmem_spec()] * 9,
        out_specs=hbm_spec(),
        scratch_shapes=[
            VMEM((heads, 2 * rows, HS), BF16),
            VMEM((2 * rows, width), BF16),
            pltpu.SemaphoreType.DMA((2,)),
        ],
        compiler_params=params(12),
        cost_estimate=cost(heads * rows * HS, 2 * nbytes(x)),
        name="own_block",
    )(far_block, x, rhs0, rhs1, shift, gram, gain, key, value)


def rest_kernel(order, out_in_ref, *refs):
    n = len(order)
    out_ref, sem = refs[n:]
    copies = [place(refs[j], k, out_ref, sem.at[j]) for j, k in enumerate(order)]
    for c in copies:
        c.start()
    for c in copies:
        c.wait()


def rest(order, out, blocks):
    n = len(order)
    return pl.pallas_call(
        lambda *refs: rest_kernel(order, *refs),
        out_shape=jax.ShapeDtypeStruct(out.shape, BF16),
        in_specs=[hbm_spec()] + [vmem_spec()] * n,
        out_specs=hbm_spec(),
        scratch_shapes=[pltpu.SemaphoreType.DMA((n,))],
        input_output_aliases={0: 0},
        compiler_params=params(4),
        cost_estimate=cost(0, 2 * n * nbytes(blocks[0])),
        name="rest",
    )(out, *blocks)


def shards(video, conv_weight, latent_weight, embed_weight, modulation, qkv_weight, qk_gain, text, text_weight):
    n = lax.axis_size("ctx")
    frames = video.shape[0]

    def swap(x, k):
        return lax.ppermute(x, "ctx", [(i, i ^ k) for i in range(n)])

    weight = qkv_weight.transpose(1, 0, 2)
    edge_row, e_near, mod_near = edge(video, embed_weight, modulation)
    halo = lax.ppermute(edge_row, "ctx", [(i, (i + 1) % n) for i in range(n)])
    lhs, gram, part, stream, last, tile, taps = text_side(
        e_near,
        mod_near,
        text,
        text_weight,
        video,
        conv_weight.reshape(-1, conv_weight.shape[-1]),
    )
    patches, weight_near = conv_side(tile, halo, taps, latent_weight, weight, weight.shape[1] * 2 // 3)
    order = tuple(range(n - 1, -1, -1))
    received = [swap(patches, k) if k else patches for k in order]
    rhs0, rhs1, shift, tkey, tvalue = fold(lhs, qk_gain, weight_near, part, stream, last, weight)
    block, x, key, value = first_block(
        order, frames, received, rhs0, rhs1, shift, gram, qk_gain, tkey, tvalue
    )
    far_block = swap(block, order[0])
    common = (x, rhs0, rhs1, shift, gram, qk_gain, key, value)
    blocks = [swap(b, k) for b, k in zip(attend(n, frames, 1, n - 2, *common), order[1:])]
    out = own_block(n, frames, order[0], far_block, *common)
    return rest(order[1 : n - 1], out, blocks)


def solution(mesh):
    in_specs = (
        P("dp", "ctx", None, None),
        P(),
        P(),
        P(),
        P("dp", None),
        P(None, None, "ctx"),
        P(),
        P("dp", None),
        P(None, None, "ctx"),
    )
    out_specs = P(("dp", "ctx"), None)
    return jax.shard_map(shards, mesh=mesh, in_specs=in_specs, out_specs=out_specs, check_vma=False)
```

```python
import math

import jax
import jax.numpy as jnp
from jax import lax
from jax.experimental import pallas as pl
from jax.experimental.pallas import tpu as pltpu
from jax.sharding import PartitionSpec as P

HS = 128
EPS = 1e-06
F32 = jnp.float32
BF16 = jnp.bfloat16
VMEM = pltpu.VMEM
MIB = 1024 * 1024


def vmem_spec():
    return pl.BlockSpec(memory_space=pltpu.VMEM)


def hbm_spec():
    return pl.BlockSpec(memory_space=pltpu.HBM)


def far(x):
    return pltpu.with_memory_space_constraint(x, pltpu.HBM)


def params(mib):
    return pltpu.CompilerParams(vmem_limit_bytes=mib * MIB)


def cost(flops, bytes_accessed, transcendentals=0):
    return pl.CostEstimate(
        flops=int(flops), bytes_accessed=int(bytes_accessed), transcendentals=int(transcendentals)
    )


def nbytes(*arrays):
    return sum(math.prod(a.shape) * a.dtype.itemsize for a in arrays)


def split(x):
    hi = x.astype(BF16)
    return hi, (x - hi.astype(F32)).astype(BF16)


def dot(a, b):
    return jnp.dot(a, b, preferred_element_type=F32)


def dot_nt(a, b):
    return lax.dot_general(a, b, (((1,), (1,)), ((), ())), preferred_element_type=F32)


def head_norm(v, gain):
    return (v * lax.rsqrt(jnp.mean(v * v, -1, keepdims=True) + EPS) * gain).astype(BF16)


def edge_kernel(video_hbm, e_hbm, mod_hbm, halo_ref, e_ref, mod_ref, sem):
    rows = video_hbm.shape[1]
    pairs = (
        (video_hbm.at[:, pl.ds(rows - 1, 1)], halo_ref),
        (e_hbm, e_ref),
        (mod_hbm, mod_ref),
    )
    copies = [pltpu.make_async_copy(src, dst, sem.at[i]) for i, (src, dst) in enumerate(pairs)]
    for c in copies:
        c.start()
    for c in copies:
        c.wait()


def edge(video, embed_weight, modulation):
    frames, _, cols, chans = video.shape
    return pl.pallas_call(
        edge_kernel,
        out_shape=(
            jax.ShapeDtypeStruct((frames, 1, cols, chans), BF16),
            jax.ShapeDtypeStruct(embed_weight.shape, BF16),
            jax.ShapeDtypeStruct(modulation.shape, F32),
        ),
        in_specs=[hbm_spec()] * 3,
        out_specs=(vmem_spec(),) * 3,
        scratch_shapes=[pltpu.SemaphoreType.DMA((3,))],
        compiler_params=params(4),
        cost_estimate=cost(0, 2 * nbytes(embed_weight, modulation)),
        name="edge",
    )(*[far(a) for a in (video, embed_weight, modulation)])


def add_text(stream, flat, acc_ref, fresh):
    step = 128
    row = lax.broadcasted_iota(jnp.int32, (2 * step, 2 * step), 0)
    col = lax.broadcasted_iota(jnp.int32, (2 * step, 2 * step), 1)
    pick = jnp.where(col == 2 * (row % step) + row // step, 1.0, 0.0).astype(BF16)
    pieces = ([], [])
    for at in range(0, flat.shape[0], 2 * step):
        both = dot(pick, flat[at : at + 2 * step, :]).astype(BF16)
        pieces[0].append(both[:step])
        pieces[1].append(both[step:])
    for p in range(2):
        term = dot(stream, jnp.concatenate(pieces[p], 0))
        if fresh:
            acc_ref[p] = term
        else:
            acc_ref[p] += term


def embed_side(e_ref, mod_ref, lhs_ref, gram_ref, centred_ref):
    pi, depth = e_ref.shape
    few = 16
    for r in range(0, pi, few):
        e = e_ref[r : r + few, :].astype(F32)
        centred = e - jnp.mean(e, -1, keepdims=True)
        lhs_ref[r : r + few, :] = (centred * (1.0 + mod_ref[1:2, :])).astype(BF16)
        centred = centred.astype(BF16)
        centred_ref[r : r + few, :] = centred
        centred_ref[pi + r : pi + r + few, :] = centred
    shift_hi, shift_lo = split(mod_ref[0:1, :])
    lhs_ref[pi:, :] = jnp.concatenate(
        [shift_hi.astype(F32), shift_lo.astype(F32), jnp.zeros((few - 2, depth), F32)], 0
    ).astype(BF16)
    gram = dot_nt(centred_ref[...], centred_ref[...])
    row = lax.broadcasted_iota(jnp.int32, gram.shape, 0) // pi
    col = lax.broadcasted_iota(jnp.int32, gram.shape, 1) // pi
    ghi, glo = split(jnp.where(row == col, gram * (1.0 / depth), 0.0))
    gram_ref[...] = jnp.concatenate([ghi, glo], 0)


def text_kernel(
    chunks,
    e_ref,
    mod_ref,
    text_hbm,
    w_hbm,
    video_hbm,
    conv_hbm,
    lhs_ref,
    gram_ref,
    acc_ref,
    stream_ref,
    last_ref,
    video_ref,
    conv_ref,
    text_ref,
    centred_ref,
    w_ref,
    sem,
    w_sem,
):
    depth, parts, width = w_hbm.shape
    taken = w_ref.shape[0]
    deep = taken // chunks
    copies = [
        pltpu.make_async_copy(w_hbm.at[pl.ds(c * deep, deep)], w_ref.at[pl.ds(c * deep, deep)], w_sem.at[c])
        for c in range(chunks)
    ]
    first = pltpu.make_async_copy(text_hbm, text_ref, sem.at[3])
    pairs = (
        (video_hbm, video_ref),
        (conv_hbm, conv_ref),
        (w_hbm.at[pl.ds(taken, depth - taken)], last_ref),
    )
    ahead = [pltpu.make_async_copy(src, dst, sem.at[i]) for i, (src, dst) in enumerate(pairs)]
    first.start()
    for c in copies:
        c.start()
    embed_side(e_ref, mod_ref, lhs_ref, gram_ref, centred_ref)
    first.wait()
    for copy in ahead:
        copy.start()
    few = 16
    for r in range(0, text_ref.shape[0], few):
        text = text_ref[r : r + few, :].astype(F32)
        centred = text - jnp.mean(text, -1, keepdims=True)
        normed = centred * lax.rsqrt(jnp.mean(centred * centred, -1, keepdims=True) + EPS)
        stream_ref[r : r + few, :] = (normed * (1.0 + mod_ref[3:4, :]) + mod_ref[2:3, :]).astype(BF16)
    flat = w_ref.reshape(taken * parts, width)
    for c in range(chunks):
        copies[c].wait()
        at = slice(c * deep, (c + 1) * deep)
        add_text(stream_ref[:, at], flat.at[2 * c * deep : 2 * (c + 1) * deep], acc_ref, c == 0)
    for c in ahead:
        c.wait()


def text_side(embed_weight, modulation, text, weight, video, conv_weight):
    depth, parts, width = weight.shape
    count = text.shape[0]
    pi = embed_weight.shape[0]
    taken = depth * 2 // 3
    chunks = 2
    return pl.pallas_call(
        lambda *refs: text_kernel(chunks, *refs),
        out_shape=(
            jax.ShapeDtypeStruct((pi + 16, depth), BF16),
            jax.ShapeDtypeStruct((4 * pi, 2 * pi), BF16),
            jax.ShapeDtypeStruct((parts, count, width), F32),
            jax.ShapeDtypeStruct(text.shape, BF16),
            jax.ShapeDtypeStruct((depth - taken, parts, width), BF16),
            jax.ShapeDtypeStruct(video.shape, BF16),
            jax.ShapeDtypeStruct(conv_weight.shape, BF16),
        ),
        in_specs=[vmem_spec()] * 2 + [hbm_spec()] * 4,
        out_specs=(vmem_spec(),) * 7,
        scratch_shapes=[
            VMEM(text.shape, BF16),
            VMEM((2 * pi, depth), BF16),
            VMEM((taken, parts, width), BF16),
            pltpu.SemaphoreType.DMA((4,)),
            pltpu.SemaphoreType.DMA((chunks,)),
        ],
        compiler_params=params(20),
        cost_estimate=cost(4 * count * depth * parts * width, nbytes(weight, text, video, conv_weight)),
        name="text_side",
    )(embed_weight, modulation, *[far(a) for a in (text, weight, video, conv_weight)])


def fold_kernel(
    lhs_ref,
    gain_ref,
    w0_ref,
    part_ref,
    stream_ref,
    last_ref,
    w_hbm,
    rhs0_ref,
    rhs1_ref,
    shift_ref,
    key_ref,
    value_ref,
    acc_ref,
    sum_ref,
    w1_ref,
    sem,
):
    parts, deep0, width = w0_ref.shape
    depth = lhs_ref.shape[1]
    pi = lhs_ref.shape[0] - 16
    copies = [
        pltpu.make_async_copy(w_hbm.at[p, pl.ds(deep0, depth - deep0)], w1_ref.at[p], sem.at[p])
        for p in range(parts)
    ]
    for c in copies:
        c.start()
    last, _, _ = last_ref.shape
    add_text(stream_ref[:, depth - last :], last_ref.reshape(2 * last, width), sum_ref, True)
    for h in range(width // HS):
        at = slice(h * HS, (h + 1) * HS)
        key_ref[h] = head_norm(part_ref[0, :, at] + sum_ref[0, :, at], gain_ref[1:2, :])
        value_ref[h] = (part_ref[1, :, at] + sum_ref[1, :, at]).astype(BF16)
    for p in range(parts):
        at = slice(p * width, (p + 1) * width)
        acc_ref[:, at] = dot(lhs_ref[:, :deep0], w0_ref[p])
    for p in range(parts):
        at = slice(p * width, (p + 1) * width)
        copies[p].wait()
        acc_ref[:, at] += dot(lhs_ref[:, deep0:], w1_ref[p])
    total = acc_ref[...]
    hi, lo = split(total[:pi])
    none = jnp.zeros_like(hi)
    rhs0_ref[...] = jnp.concatenate([hi, none, lo, none], 0)
    rhs1_ref[...] = jnp.concatenate([none, hi, none, lo], 0)
    shift_ref[...] = total[pi : pi + 1] + total[pi + 1 : pi + 2]


def fold(lhs, gain, weight0, part, stream, last, weight):
    parts, taken, width = weight0.shape
    rows, depth = lhs.shape
    cols = parts * width
    count = stream.shape[0]
    heads = width // HS
    return pl.pallas_call(
        fold_kernel,
        out_shape=(
            jax.ShapeDtypeStruct((4 * (rows - 16), cols), BF16),
            jax.ShapeDtypeStruct((4 * (rows - 16), cols), BF16),
            jax.ShapeDtypeStruct((1, cols), F32),
            jax.ShapeDtypeStruct((heads, count, HS), BF16),
            jax.ShapeDtypeStruct((heads, count, HS), BF16),
        ),
        in_specs=[vmem_spec()] * 6 + [hbm_spec()],
        out_specs=(vmem_spec(),) * 5,
        scratch_shapes=[
            VMEM((rows, cols), F32),
            VMEM(part.shape, F32),
            VMEM((parts, depth - taken, width), BF16),
            pltpu.SemaphoreType.DMA((parts,)),
        ],
        compiler_params=params(20),
        cost_estimate=cost(2 * 144 * depth * cols, nbytes(weight)),
        name="fold",
    )(lhs, gain, weight0, part, stream, last, far(weight))


def conv_kernel(
    chunks,
    video_ref,
    halo_ref,
    weight_ref,
    latent_ref,
    qkv_hbm,
    out_ref,
    qkv_ref,
    wide_ref,
    even_ref,
    odd_ref,
    left_ref,
    spread_ref,
    sem,
):
    deep = qkv_ref.shape[1] // chunks
    ahead = [
        pltpu.make_async_copy(
            qkv_hbm.at[p, pl.ds(c * deep, deep)], qkv_ref.at[p, pl.ds(c * deep, deep)], sem.at[p, c]
        )
        for p in range(qkv_ref.shape[0])
        for c in range(chunks)
    ]
    for copy in ahead:
        copy.start()
    frames, rows, cols, chans = video_ref.shape
    block = cols + 8
    half = cols // 2
    quarter = cols // 4
    for r in range(rows + 1):
        for f in range(frames):
            base = (r * frames + f) * block
            pixels = (halo_ref[f, 0] if r == 0 else video_ref[f, r - 1]).astype(F32)
            if r == 0:
                pixels = jnp.where(lax.axis_index("ctx") == 0, 0.0, pixels)
            wide_ref[base : base + 8, :] = jnp.zeros((8, chans), F32)
            wide_ref[base + 8 : base + block, :] = pixels
            at = [wide_ref[pl.ds(base + 7 + o, quarter, stride=4), :] for o in range(5)]
            even = jnp.concatenate([at[1], at[3]], 0).astype(BF16)
            odd = jnp.concatenate([at[2], at[4]], 0).astype(BF16)
            left = jnp.concatenate([at[0], at[2]], 0).astype(BF16)
            for t in (range(3) if f == 0 else (f + 2,)):
                even_ref[r, t] = even
                odd_ref[r, t] = odd
                left_ref[r, t] = left
    lat, mid = latent_ref.shape
    tall = rows // 2
    spread_ref[...] = jnp.zeros_like(spread_ref)
    for s in range(2 * tall):
        spread_ref[s * lat : (s + 1) * lat, s * mid : (s + 1) * mid] = latent_ref[...]
    pieces = []
    for j in range(tall):
        taps = []
        for kt in range(3):
            for kr in range(3):
                for ref in (left_ref, even_ref, odd_ref):
                    taps.append(ref[2 * j + kr, kt : kt + frames].reshape(frames * half, chans))
        conv = dot(jnp.concatenate(taps, 1), weight_ref[...])
        act = (conv * (1.0 / (1.0 + jnp.exp(-conv)))).astype(BF16)
        for b in range(2):
            pieces.append(
                jnp.concatenate(
                    [act[f * half + b * quarter : f * half + (b + 1) * quarter] for f in range(frames)], 0
                )
            )
    out_ref[...] = dot_nt(jnp.concatenate(pieces, 1), spread_ref[...]).astype(BF16)
    for copy in ahead:
        copy.wait()


def conv_side(video, halo, weight, latent_weight, qkv_weight, taken):
    frames, rows, cols, chans = video.shape
    parts, depth, width = qkv_weight.shape
    mid = weight.shape[-1]
    lat = latent_weight.shape[1]
    latent = latent_weight.T
    half = cols // 2
    tall = rows // 2
    chunks = 1
    return pl.pallas_call(
        lambda *refs: conv_kernel(chunks, *refs),
        out_shape=(
            jax.ShapeDtypeStruct((frames * half // 2, 2 * tall * lat), BF16),
            jax.ShapeDtypeStruct((parts, taken, width), BF16),
        ),
        in_specs=[vmem_spec()] * 4 + [hbm_spec()],
        out_specs=(vmem_spec(),) * 2,
        scratch_shapes=[VMEM(((rows + 1) * frames * (cols + 8), chans), F32)]
        + [VMEM((rows + 1, frames + 2, half, chans), BF16)] * 3
        + [VMEM((2 * tall * lat, 2 * tall * mid), BF16), pltpu.SemaphoreType.DMA((parts, chunks))],
        compiler_params=params(24),
        cost_estimate=cost(
            2 * frames * tall * half * 27 * chans * mid, nbytes(video, halo, weight)
        ),
        name="conv_side",
    )(video, halo, weight, latent, far(qkv_weight))


def token_scales(x, xx, gram_ref):
    quad = dot(xx, gram_ref[...]) * x.astype(F32)
    lane = lax.broadcasted_iota(jnp.int32, quad.shape, 1)
    low = lane < quad.shape[1] // 2
    scales = []
    for i in range(2):
        var = jnp.sum(jnp.where(low if i == 0 else ~low, quad, 0.0), -1, keepdims=True)
        scales.append(lax.rsqrt(jnp.maximum(var, 0.0) + EPS))
    return scales


def block_queries(n, own, x, xx, scales, rhs_refs, shift_ref, gain_ref, query_ref):
    heads = query_ref.shape[0]
    rows = x.shape[1]
    span = rows // n
    grain = span // own
    gain = gain_ref[0:1, :] * (math.log2(math.e) / math.sqrt(HS))
    for i in range(2):
        at = slice(0, heads * HS)
        projected = dot(xx, rhs_refs[i][:, at]) * scales[i] + shift_ref[:, at]
        for h in range(heads):
            v = head_norm(projected[:, h * HS : (h + 1) * HS], gain)
            for j in range(x.shape[0] // rows):
                for s in range(n):
                    for f in range(own):
                        to = 2 * j * rows + f * (n * 2 * grain) + (s * 2 + i) * grain
                        come = j * rows + s * span + f * grain
                        query_ref[h, to : to + grain, :] = v[come : come + grain]


def attention(query_ref, key_ref, value_ref, out_refs):
    heads, total, _ = key_ref.shape
    rows = query_ref.shape[1] // len(out_refs)
    for j in range(0, len(out_refs), 2):
        group = out_refs[j : j + 2]
        for h in range(heads):
            query = query_ref[h, j * rows : (j + len(group)) * rows, :]
            weights = jnp.exp2(dot_nt(query, key_ref[h]))
            norm = weights[:, :HS]
            for c in range(HS, total, HS):
                norm = norm + weights[:, c : c + HS]
            norm = jnp.sum(norm, -1, keepdims=True)
            attended = (dot(weights.astype(BF16), value_ref[h]) / norm).astype(BF16)
            for g, ref in enumerate(group):
                ref[:, h * HS : (h + 1) * HS] = attended[g * rows : (g + 1) * rows]


def first_kernel(order, frames, *refs):
    n = len(order)
    patch_refs = refs[:n]
    rhs0_ref, rhs1_ref, shift_ref, gram_ref, gain_ref, tkey_ref, tvalue_ref = refs[n : n + 7]
    out_ref, x_ref, key_ref, value_ref, patch_scr, query_ref = refs[n + 7 :]
    me = lax.axis_index("ctx")
    rhs_refs = (rhs0_ref, rhs1_ref)
    heads, count, _ = tkey_ref.shape
    rows = patch_refs[0].shape[1]
    for k, ref in zip(order, patch_refs):
        patch_scr[pl.ds(pl.multiple_of((me ^ k) * rows, rows), rows), :] = ref[...]
    key_ref[:, 0:count, :] = tkey_ref[...]
    value_ref[:, 0:count, :] = tvalue_ref[...]
    own = frames // n
    span = rows // n
    for j, k in enumerate(order):
        for s in range(n):
            at = pl.multiple_of((me ^ k) * span, span) + s * rows
            x_ref[j * rows + s * span : j * rows + (s + 1) * span, :] = patch_scr[
                pl.ds(pl.multiple_of(at, span), span), :
            ]
    x = x_ref[...]
    xx = jnp.concatenate([x, x], 1)
    scales = token_scales(x, xx, gram_ref)
    width = heads * HS
    for i in range(2):
        for p in (1, 2):
            for h0 in range(0, heads, 2):
                at = slice(p * width + h0 * HS, p * width + (h0 + 2) * HS)
                pair = dot(xx, rhs_refs[i][:, at]) * scales[i] + shift_ref[:, at]
                for h in (h0, h0 + 1):
                    v = pair[:, (h - h0) * HS : (h - h0 + 1) * HS]
                    to = slice(count + i * n * rows, count + (i + 1) * n * rows)
                    if p == 1:
                        key_ref[h, to, :] = head_norm(v, gain_ref[1:2, :])
                    else:
                        value_ref[h, to, :] = v.astype(BF16)
    block_queries(
        n, own, x[:rows], xx[:rows], [v[:rows] for v in scales], rhs_refs, shift_ref, gain_ref, query_ref
    )
    attention(query_ref, key_ref, value_ref, (out_ref,))


def first_block(order, frames, patches, rhs0, rhs1, shift, gram, gain, tkey, tvalue):
    n = len(order)
    heads, count, _ = tkey.shape
    rows = patches[0].shape[1]
    total = count + 2 * n * rows
    return pl.pallas_call(
        lambda *refs: first_kernel(order, frames, *refs),
        out_shape=(
            jax.ShapeDtypeStruct((2 * rows, heads * HS), BF16),
            jax.ShapeDtypeStruct((n * rows, rows), BF16),
            jax.ShapeDtypeStruct((heads, total, HS), BF16),
            jax.ShapeDtypeStruct((heads, total, HS), BF16),
        ),
        in_specs=[vmem_spec()] * (n + 7),
        out_specs=(vmem_spec(),) * 4,
        scratch_shapes=[VMEM((n * rows, rows), BF16), VMEM((heads, 2 * rows, HS), BF16)],
        compiler_params=params(16),
        cost_estimate=cost(2 * 2 * n * rows * 256 * 3 * heads * HS, 4 * nbytes(rhs0)),
        name="first_block",
    )(*patches, rhs0, rhs1, shift, gram, gain, tkey, tvalue)


def attend_kernel(
    n, own, first, x_ref, rhs0_ref, rhs1_ref, shift_ref, gram_ref, gain_ref, key_ref, value_ref, *refs
):
    out_refs, query_ref = refs[:-1], refs[-1]
    rows = x_ref.shape[1]
    x = x_ref[first * rows : (first + len(out_refs)) * rows, :]
    xx = jnp.concatenate([x, x], 1)
    scales = token_scales(x, xx, gram_ref)
    block_queries(n, own, x, xx, scales, (rhs0_ref, rhs1_ref), shift_ref, gain_ref, query_ref)
    attention(query_ref, key_ref, value_ref, out_refs)


def attend(n, frames, first, count, x, rhs0, rhs1, shift, gram, gain, key, value):
    heads = key.shape[0]
    rows = x.shape[1]
    return pl.pallas_call(
        lambda *refs: attend_kernel(n, frames // n, first, *refs),
        out_shape=(jax.ShapeDtypeStruct((2 * rows, heads * HS), BF16),) * count,
        in_specs=[vmem_spec()] * 8,
        out_specs=(vmem_spec(),) * count,
        scratch_shapes=[VMEM((heads, count * 2 * rows, HS), BF16)],
        compiler_params=params(20),
        cost_estimate=cost(heads * rows * HS, 2 * nbytes(x)),
        name="attend",
    )(x, rhs0, rhs1, shift, gram, gain, key, value)


def place(block, k, out_ref, sem):
    width = block.shape[1]
    at = pl.multiple_of((lax.axis_index("ctx") ^ k) * width, width)
    return pltpu.make_async_copy(block, out_ref.at[:, pl.ds(at, width)], sem)


def own_kernel(
    n,
    own,
    far,
    far_ref,
    x_ref,
    rhs0_ref,
    rhs1_ref,
    shift_ref,
    gram_ref,
    gain_ref,
    key_ref,
    value_ref,
    out_ref,
    query_ref,
    block_ref,
    sem,
):
    first = place(far_ref, far, out_ref, sem.at[0])
    first.start()
    attend_kernel(
        n,
        own,
        n - 1,
        x_ref,
        rhs0_ref,
        rhs1_ref,
        shift_ref,
        gram_ref,
        gain_ref,
        key_ref,
        value_ref,
        block_ref,
        query_ref,
    )
    second = place(block_ref, 0, out_ref, sem.at[1])
    second.start()
    first.wait()
    second.wait()


def own_block(n, frames, far, far_block, x, rhs0, rhs1, shift, gram, gain, key, value):
    heads = key.shape[0]
    rows = x.shape[1]
    width = heads * HS
    return pl.pallas_call(
        lambda *refs: own_kernel(n, frames // n, far, *refs),
        out_shape=jax.ShapeDtypeStruct((2 * rows, n * width), BF16),
        in_specs=[vmem_spec()] * 9,
        out_specs=hbm_spec(),
        scratch_shapes=[
            VMEM((heads, 2 * rows, HS), BF16),
            VMEM((2 * rows, width), BF16),
            pltpu.SemaphoreType.DMA((2,)),
        ],
        compiler_params=params(12),
        cost_estimate=cost(heads * rows * HS, 2 * nbytes(x)),
        name="own_block",
    )(far_block, x, rhs0, rhs1, shift, gram, gain, key, value)


def rest_kernel(order, out_in_ref, *refs):
    n = len(order)
    out_ref, sem = refs[n:]
    copies = [place(refs[j], k, out_ref, sem.at[j]) for j, k in enumerate(order)]
    for c in copies:
        c.start()
    for c in copies:
        c.wait()


def rest(order, out, blocks):
    n = len(order)
    return pl.pallas_call(
        lambda *refs: rest_kernel(order, *refs),
        out_shape=jax.ShapeDtypeStruct(out.shape, BF16),
        in_specs=[hbm_spec()] + [vmem_spec()] * n,
        out_specs=hbm_spec(),
        scratch_shapes=[pltpu.SemaphoreType.DMA((n,))],
        input_output_aliases={0: 0},
        compiler_params=params(4),
        cost_estimate=cost(0, 2 * n * nbytes(blocks[0])),
        name="rest",
    )(out, *blocks)


def shards(video, conv_weight, latent_weight, embed_weight, modulation, qkv_weight, qk_gain, text, text_weight):
    n = lax.axis_size("ctx")
    frames = video.shape[0]

    def swap(x, k):
        return lax.ppermute(x, "ctx", [(i, i ^ k) for i in range(n)])

    weight = qkv_weight.transpose(1, 0, 2)
    edge_row, e_near, mod_near = edge(video, embed_weight, modulation)
    halo = lax.ppermute(edge_row, "ctx", [(i, (i + 1) % n) for i in range(n)])
    lhs, gram, part, stream, last, tile, taps = text_side(
        e_near,
        mod_near,
        text,
        text_weight,
        video,
        conv_weight.reshape(-1, conv_weight.shape[-1]),
    )
    patches, weight_near = conv_side(tile, halo, taps, latent_weight, weight, weight.shape[1] // 2)
    order = tuple(range(n - 1, -1, -1))
    received = [swap(patches, k) if k else patches for k in order]
    rhs0, rhs1, shift, tkey, tvalue = fold(lhs, qk_gain, weight_near, part, stream, last, weight)
    block, x, key, value = first_block(
        order, frames, received, rhs0, rhs1, shift, gram, qk_gain, tkey, tvalue
    )
    far_block = swap(block, order[0])
    common = (x, rhs0, rhs1, shift, gram, qk_gain, key, value)
    blocks = [swap(b, k) for b, k in zip(attend(n, frames, 1, n - 2, *common), order[1:])]
    out = own_block(n, frames, order[0], far_block, *common)
    return rest(order[1 : n - 1], out, blocks)


def solution(mesh):
    in_specs = (
        P("dp", "ctx", None, None),
        P(),
        P(),
        P(),
        P("dp", None),
        P(None, None, "ctx"),
        P(),
        P("dp", None),
        P(None, None, "ctx"),
    )
    out_specs = P(("dp", "ctx"), None)
    return jax.shard_map(shards, mesh=mesh, in_specs=in_specs, out_specs=out_specs, check_vma=False)
```

```python
import math

import jax
import jax.numpy as jnp
from jax import lax
from jax.experimental import pallas as pl
from jax.experimental.pallas import tpu as pltpu
from jax.sharding import PartitionSpec as P

HS = 128
EPS = 1e-06
F32 = jnp.float32
BF16 = jnp.bfloat16
VMEM = pltpu.VMEM
MIB = 1024 * 1024


def vmem_spec():
    return pl.BlockSpec(memory_space=pltpu.VMEM)


def hbm_spec():
    return pl.BlockSpec(memory_space=pltpu.HBM)


def far(x):
    return pltpu.with_memory_space_constraint(x, pltpu.HBM)


def params(mib):
    return pltpu.CompilerParams(vmem_limit_bytes=mib * MIB)


def cost(flops, bytes_accessed, transcendentals=0):
    return pl.CostEstimate(
        flops=int(flops), bytes_accessed=int(bytes_accessed), transcendentals=int(transcendentals)
    )


def nbytes(*arrays):
    return sum(math.prod(a.shape) * a.dtype.itemsize for a in arrays)


def split(x):
    hi = x.astype(BF16)
    return hi, (x - hi.astype(F32)).astype(BF16)


def dot(a, b):
    return jnp.dot(a, b, preferred_element_type=F32)


def dot_nt(a, b):
    return lax.dot_general(a, b, (((1,), (1,)), ((), ())), preferred_element_type=F32)


def head_norm(v, gain):
    return (v * lax.rsqrt(jnp.mean(v * v, -1, keepdims=True) + EPS) * gain).astype(BF16)


def edge_kernel(video_hbm, e_hbm, mod_hbm, halo_ref, e_ref, mod_ref, sem):
    rows = video_hbm.shape[1]
    pairs = (
        (video_hbm.at[:, pl.ds(rows - 1, 1)], halo_ref),
        (e_hbm, e_ref),
        (mod_hbm, mod_ref),
    )
    copies = [pltpu.make_async_copy(src, dst, sem.at[i]) for i, (src, dst) in enumerate(pairs)]
    for c in copies:
        c.start()
    for c in copies:
        c.wait()


def edge(video, embed_weight, modulation):
    frames, _, cols, chans = video.shape
    return pl.pallas_call(
        edge_kernel,
        out_shape=(
            jax.ShapeDtypeStruct((frames, 1, cols, chans), BF16),
            jax.ShapeDtypeStruct(embed_weight.shape, BF16),
            jax.ShapeDtypeStruct(modulation.shape, F32),
        ),
        in_specs=[hbm_spec()] * 3,
        out_specs=(vmem_spec(),) * 3,
        scratch_shapes=[pltpu.SemaphoreType.DMA((3,))],
        compiler_params=params(4),
        cost_estimate=cost(0, 2 * nbytes(embed_weight, modulation)),
        name="edge",
    )(*[far(a) for a in (video, embed_weight, modulation)])


def add_text(stream, flat, acc_ref, fresh):
    step = 128
    row = lax.broadcasted_iota(jnp.int32, (2 * step, 2 * step), 0)
    col = lax.broadcasted_iota(jnp.int32, (2 * step, 2 * step), 1)
    pick = jnp.where(col == 2 * (row % step) + row // step, 1.0, 0.0).astype(BF16)
    pieces = ([], [])
    for at in range(0, flat.shape[0], 2 * step):
        both = dot(pick, flat[at : at + 2 * step, :]).astype(BF16)
        pieces[0].append(both[:step])
        pieces[1].append(both[step:])
    for p in range(2):
        term = dot(stream, jnp.concatenate(pieces[p], 0))
        if fresh:
            acc_ref[p] = term
        else:
            acc_ref[p] += term


def embed_side(e_ref, mod_ref, lhs_ref, gram_ref, centred_ref):
    pi, depth = e_ref.shape
    few = 16
    for r in range(0, pi, few):
        e = e_ref[r : r + few, :].astype(F32)
        centred = e - jnp.mean(e, -1, keepdims=True)
        lhs_ref[r : r + few, :] = (centred * (1.0 + mod_ref[1:2, :])).astype(BF16)
        centred = centred.astype(BF16)
        centred_ref[r : r + few, :] = centred
        centred_ref[pi + r : pi + r + few, :] = centred
    shift_hi, shift_lo = split(mod_ref[0:1, :])
    lhs_ref[pi:, :] = jnp.concatenate(
        [shift_hi.astype(F32), shift_lo.astype(F32), jnp.zeros((few - 2, depth), F32)], 0
    ).astype(BF16)
    gram = dot_nt(centred_ref[...], centred_ref[...])
    row = lax.broadcasted_iota(jnp.int32, gram.shape, 0) // pi
    col = lax.broadcasted_iota(jnp.int32, gram.shape, 1) // pi
    ghi, glo = split(jnp.where(row == col, gram * (1.0 / depth), 0.0))
    gram_ref[...] = jnp.concatenate([ghi, glo], 0)


def text_kernel(
    chunks,
    e_ref,
    mod_ref,
    text_hbm,
    w_hbm,
    video_hbm,
    conv_hbm,
    lhs_ref,
    gram_ref,
    acc_ref,
    stream_ref,
    last_ref,
    video_ref,
    conv_ref,
    text_ref,
    centred_ref,
    w_ref,
    sem,
    w_sem,
):
    depth, parts, width = w_hbm.shape
    taken = w_ref.shape[0]
    deep = taken // chunks
    copies = [
        pltpu.make_async_copy(w_hbm.at[pl.ds(c * deep, deep)], w_ref.at[pl.ds(c * deep, deep)], w_sem.at[c])
        for c in range(chunks)
    ]
    first = pltpu.make_async_copy(text_hbm, text_ref, sem.at[3])
    pairs = (
        (video_hbm, video_ref),
        (conv_hbm, conv_ref),
        (w_hbm.at[pl.ds(taken, depth - taken)], last_ref),
    )
    ahead = [pltpu.make_async_copy(src, dst, sem.at[i]) for i, (src, dst) in enumerate(pairs)]
    first.start()
    for c in copies:
        c.start()
    embed_side(e_ref, mod_ref, lhs_ref, gram_ref, centred_ref)
    first.wait()
    for copy in ahead:
        copy.start()
    few = 16
    for r in range(0, text_ref.shape[0], few):
        text = text_ref[r : r + few, :].astype(F32)
        centred = text - jnp.mean(text, -1, keepdims=True)
        normed = centred * lax.rsqrt(jnp.mean(centred * centred, -1, keepdims=True) + EPS)
        stream_ref[r : r + few, :] = (normed * (1.0 + mod_ref[3:4, :]) + mod_ref[2:3, :]).astype(BF16)
    flat = w_ref.reshape(taken * parts, width)
    for c in range(chunks):
        copies[c].wait()
        at = slice(c * deep, (c + 1) * deep)
        add_text(stream_ref[:, at], flat.at[2 * c * deep : 2 * (c + 1) * deep], acc_ref, c == 0)
    for c in ahead:
        c.wait()


def text_side(embed_weight, modulation, text, weight, video, conv_weight):
    depth, parts, width = weight.shape
    count = text.shape[0]
    pi = embed_weight.shape[0]
    taken = depth * 2 // 3
    chunks = 2
    return pl.pallas_call(
        lambda *refs: text_kernel(chunks, *refs),
        out_shape=(
            jax.ShapeDtypeStruct((pi + 16, depth), BF16),
            jax.ShapeDtypeStruct((4 * pi, 2 * pi), BF16),
            jax.ShapeDtypeStruct((parts, count, width), F32),
            jax.ShapeDtypeStruct(text.shape, BF16),
            jax.ShapeDtypeStruct((depth - taken, parts, width), BF16),
            jax.ShapeDtypeStruct(video.shape, BF16),
            jax.ShapeDtypeStruct(conv_weight.shape, BF16),
        ),
        in_specs=[vmem_spec()] * 2 + [hbm_spec()] * 4,
        out_specs=(vmem_spec(),) * 7,
        scratch_shapes=[
            VMEM(text.shape, BF16),
            VMEM((2 * pi, depth), BF16),
            VMEM((taken, parts, width), BF16),
            pltpu.SemaphoreType.DMA((4,)),
            pltpu.SemaphoreType.DMA((chunks,)),
        ],
        compiler_params=params(20),
        cost_estimate=cost(4 * count * depth * parts * width, nbytes(weight, text, video, conv_weight)),
        name="text_side",
    )(embed_weight, modulation, *[far(a) for a in (text, weight, video, conv_weight)])


def fold_kernel(
    lhs_ref,
    gain_ref,
    w0_ref,
    part_ref,
    stream_ref,
    last_ref,
    w_hbm,
    rhs0_ref,
    rhs1_ref,
    shift_ref,
    key_ref,
    value_ref,
    acc_ref,
    sum_ref,
    w1_ref,
    sem,
):
    parts, deep0, width = w0_ref.shape
    depth = lhs_ref.shape[1]
    pi = lhs_ref.shape[0] - 16
    copies = [
        pltpu.make_async_copy(w_hbm.at[p, pl.ds(deep0, depth - deep0)], w1_ref.at[p], sem.at[p])
        for p in range(parts)
    ]
    for c in copies:
        c.start()
    last, _, _ = last_ref.shape
    add_text(stream_ref[:, depth - last :], last_ref.reshape(2 * last, width), sum_ref, True)
    for h in range(width // HS):
        at = slice(h * HS, (h + 1) * HS)
        key_ref[h] = head_norm(part_ref[0, :, at] + sum_ref[0, :, at], gain_ref[1:2, :])
        value_ref[h] = (part_ref[1, :, at] + sum_ref[1, :, at]).astype(BF16)
    for p in range(parts):
        at = slice(p * width, (p + 1) * width)
        acc_ref[:, at] = dot(lhs_ref[:, :deep0], w0_ref[p])
    for p in range(parts):
        at = slice(p * width, (p + 1) * width)
        copies[p].wait()
        acc_ref[:, at] += dot(lhs_ref[:, deep0:], w1_ref[p])
    total = acc_ref[...]
    hi, lo = split(total[:pi])
    none = jnp.zeros_like(hi)
    rhs0_ref[...] = jnp.concatenate([hi, none, lo, none], 0)
    rhs1_ref[...] = jnp.concatenate([none, hi, none, lo], 0)
    shift_ref[...] = total[pi : pi + 1] + total[pi + 1 : pi + 2]


def fold(lhs, gain, weight0, part, stream, last, weight):
    parts, taken, width = weight0.shape
    rows, depth = lhs.shape
    cols = parts * width
    count = stream.shape[0]
    heads = width // HS
    return pl.pallas_call(
        fold_kernel,
        out_shape=(
            jax.ShapeDtypeStruct((4 * (rows - 16), cols), BF16),
            jax.ShapeDtypeStruct((4 * (rows - 16), cols), BF16),
            jax.ShapeDtypeStruct((1, cols), F32),
            jax.ShapeDtypeStruct((heads, count, HS), BF16),
            jax.ShapeDtypeStruct((heads, count, HS), BF16),
        ),
        in_specs=[vmem_spec()] * 6 + [hbm_spec()],
        out_specs=(vmem_spec(),) * 5,
        scratch_shapes=[
            VMEM((rows, cols), F32),
            VMEM(part.shape, F32),
            VMEM((parts, depth - taken, width), BF16),
            pltpu.SemaphoreType.DMA((parts,)),
        ],
        compiler_params=params(20),
        cost_estimate=cost(2 * 144 * depth * cols, nbytes(weight)),
        name="fold",
    )(lhs, gain, weight0, part, stream, last, far(weight))


def conv_kernel(
    chunks,
    video_ref,
    halo_ref,
    weight_ref,
    latent_ref,
    qkv_hbm,
    out_ref,
    qkv_ref,
    wide_ref,
    even_ref,
    odd_ref,
    left_ref,
    spread_ref,
    sem,
):
    deep = qkv_ref.shape[1] // chunks
    ahead = [
        pltpu.make_async_copy(
            qkv_hbm.at[p, pl.ds(c * deep, deep)], qkv_ref.at[p, pl.ds(c * deep, deep)], sem.at[p, c]
        )
        for p in range(qkv_ref.shape[0])
        for c in range(chunks)
    ]
    for copy in ahead:
        copy.start()
    frames, rows, cols, chans = video_ref.shape
    block = cols + 8
    half = cols // 2
    quarter = cols // 4
    for r in range(rows + 1):
        for f in range(frames):
            base = (r * frames + f) * block
            pixels = (halo_ref[f, 0] if r == 0 else video_ref[f, r - 1]).astype(F32)
            if r == 0:
                pixels = jnp.where(lax.axis_index("ctx") == 0, 0.0, pixels)
            wide_ref[base : base + 8, :] = jnp.zeros((8, chans), F32)
            wide_ref[base + 8 : base + block, :] = pixels
            at = [wide_ref[pl.ds(base + 7 + o, quarter, stride=4), :] for o in range(5)]
            even = jnp.concatenate([at[1], at[3]], 0).astype(BF16)
            odd = jnp.concatenate([at[2], at[4]], 0).astype(BF16)
            left = jnp.concatenate([at[0], at[2]], 0).astype(BF16)
            for t in (range(3) if f == 0 else (f + 2,)):
                even_ref[r, t] = even
                odd_ref[r, t] = odd
                left_ref[r, t] = left
    lat, mid = latent_ref.shape
    tall = rows // 2
    spread_ref[...] = jnp.zeros_like(spread_ref)
    for s in range(2 * tall):
        spread_ref[s * lat : (s + 1) * lat, s * mid : (s + 1) * mid] = latent_ref[...]
    pieces = []
    for j in range(tall):
        taps = []
        for kt in range(3):
            for kr in range(3):
                for ref in (left_ref, even_ref, odd_ref):
                    taps.append(ref[2 * j + kr, kt : kt + frames].reshape(frames * half, chans))
        conv = dot(jnp.concatenate(taps, 1), weight_ref[...])
        act = (conv * (1.0 / (1.0 + jnp.exp(-conv)))).astype(BF16)
        for b in range(2):
            pieces.append(
                jnp.concatenate(
                    [act[f * half + b * quarter : f * half + (b + 1) * quarter] for f in range(frames)], 0
                )
            )
    out_ref[...] = dot_nt(jnp.concatenate(pieces, 1), spread_ref[...]).astype(BF16)
    for copy in ahead:
        copy.wait()


def conv_side(video, halo, weight, latent_weight, qkv_weight, taken):
    frames, rows, cols, chans = video.shape
    parts, depth, width = qkv_weight.shape
    mid = weight.shape[-1]
    lat = latent_weight.shape[1]
    latent = latent_weight.T
    half = cols // 2
    tall = rows // 2
    chunks = 1
    return pl.pallas_call(
        lambda *refs: conv_kernel(chunks, *refs),
        out_shape=(
            jax.ShapeDtypeStruct((frames * half // 2, 2 * tall * lat), BF16),
            jax.ShapeDtypeStruct((parts, taken, width), BF16),
        ),
        in_specs=[vmem_spec()] * 4 + [hbm_spec()],
        out_specs=(vmem_spec(),) * 2,
        scratch_shapes=[VMEM(((rows + 1) * frames * (cols + 8), chans), F32)]
        + [VMEM((rows + 1, frames + 2, half, chans), BF16)] * 3
        + [VMEM((2 * tall * lat, 2 * tall * mid), BF16), pltpu.SemaphoreType.DMA((parts, chunks))],
        compiler_params=params(24),
        cost_estimate=cost(
            2 * frames * tall * half * 27 * chans * mid, nbytes(video, halo, weight)
        ),
        name="conv_side",
    )(video, halo, weight, latent, far(qkv_weight))


def token_scales(x, xx, gram_ref):
    quad = dot(xx, gram_ref[...]) * x.astype(F32)
    lane = lax.broadcasted_iota(jnp.int32, quad.shape, 1)
    low = lane < quad.shape[1] // 2
    scales = []
    for i in range(2):
        var = jnp.sum(jnp.where(low if i == 0 else ~low, quad, 0.0), -1, keepdims=True)
        scales.append(lax.rsqrt(jnp.maximum(var, 0.0) + EPS))
    return scales


def block_queries(n, own, x, xx, scales, rhs_refs, shift_ref, gain_ref, query_ref):
    heads = query_ref.shape[0]
    rows = x.shape[1]
    span = rows // n
    grain = span // own
    gain = gain_ref[0:1, :] * (math.log2(math.e) / math.sqrt(HS))
    for i in range(2):
        at = slice(0, heads * HS)
        projected = dot(xx, rhs_refs[i][:, at]) * scales[i] + shift_ref[:, at]
        for h in range(heads):
            v = head_norm(projected[:, h * HS : (h + 1) * HS], gain)
            for j in range(x.shape[0] // rows):
                for s in range(n):
                    for f in range(own):
                        to = 2 * j * rows + f * (n * 2 * grain) + (s * 2 + i) * grain
                        come = j * rows + s * span + f * grain
                        query_ref[h, to : to + grain, :] = v[come : come + grain]


def attention(query_ref, key_ref, value_ref, out_refs):
    heads, total, _ = key_ref.shape
    rows = query_ref.shape[1] // len(out_refs)
    for j in range(0, len(out_refs), 2):
        group = out_refs[j : j + 2]
        for h in range(heads):
            query = query_ref[h, j * rows : (j + len(group)) * rows, :]
            weights = jnp.exp2(dot_nt(query, key_ref[h]))
            norm = weights[:, :HS]
            for c in range(HS, total, HS):
                norm = norm + weights[:, c : c + HS]
            norm = jnp.sum(norm, -1, keepdims=True)
            attended = (dot(weights.astype(BF16), value_ref[h]) * (1.0 / norm)).astype(BF16)
            for g, ref in enumerate(group):
                ref[:, h * HS : (h + 1) * HS] = attended[g * rows : (g + 1) * rows]


def first_kernel(order, frames, *refs):
    n = len(order)
    patch_refs = refs[:n]
    rhs0_ref, rhs1_ref, shift_ref, gram_ref, gain_ref, tkey_ref, tvalue_ref = refs[n : n + 7]
    out_ref, x_ref, key_ref, value_ref, patch_scr, query_ref = refs[n + 7 :]
    me = lax.axis_index("ctx")
    rhs_refs = (rhs0_ref, rhs1_ref)
    heads, count, _ = tkey_ref.shape
    rows = patch_refs[0].shape[1]
    for k, ref in zip(order, patch_refs):
        patch_scr[pl.ds(pl.multiple_of((me ^ k) * rows, rows), rows), :] = ref[...]
    key_ref[:, 0:count, :] = tkey_ref[...]
    value_ref[:, 0:count, :] = tvalue_ref[...]
    own = frames // n
    span = rows // n
    for j, k in enumerate(order):
        for s in range(n):
            at = pl.multiple_of((me ^ k) * span, span) + s * rows
            x_ref[j * rows + s * span : j * rows + (s + 1) * span, :] = patch_scr[
                pl.ds(pl.multiple_of(at, span), span), :
            ]
    x = x_ref[...]
    xx = jnp.concatenate([x, x], 1)
    scales = token_scales(x, xx, gram_ref)
    width = heads * HS
    for i in range(2):
        for p in (1, 2):
            for h0 in range(0, heads, 2):
                at = slice(p * width + h0 * HS, p * width + (h0 + 2) * HS)
                pair = dot(xx, rhs_refs[i][:, at]) * scales[i] + shift_ref[:, at]
                for h in (h0, h0 + 1):
                    v = pair[:, (h - h0) * HS : (h - h0 + 1) * HS]
                    to = slice(count + i * n * rows, count + (i + 1) * n * rows)
                    if p == 1:
                        key_ref[h, to, :] = head_norm(v, gain_ref[1:2, :])
                    else:
                        value_ref[h, to, :] = v.astype(BF16)
    block_queries(
        n, own, x[:rows], xx[:rows], [v[:rows] for v in scales], rhs_refs, shift_ref, gain_ref, query_ref
    )
    attention(query_ref, key_ref, value_ref, (out_ref,))


def first_block(order, frames, patches, rhs0, rhs1, shift, gram, gain, tkey, tvalue):
    n = len(order)
    heads, count, _ = tkey.shape
    rows = patches[0].shape[1]
    total = count + 2 * n * rows
    return pl.pallas_call(
        lambda *refs: first_kernel(order, frames, *refs),
        out_shape=(
            jax.ShapeDtypeStruct((2 * rows, heads * HS), BF16),
            jax.ShapeDtypeStruct((n * rows, rows), BF16),
            jax.ShapeDtypeStruct((heads, total, HS), BF16),
            jax.ShapeDtypeStruct((heads, total, HS), BF16),
        ),
        in_specs=[vmem_spec()] * (n + 7),
        out_specs=(vmem_spec(),) * 4,
        scratch_shapes=[VMEM((n * rows, rows), BF16), VMEM((heads, 2 * rows, HS), BF16)],
        compiler_params=params(16),
        cost_estimate=cost(2 * 2 * n * rows * 256 * 3 * heads * HS, 4 * nbytes(rhs0)),
        name="first_block",
    )(*patches, rhs0, rhs1, shift, gram, gain, tkey, tvalue)


def attend_kernel(
    n, own, first, x_ref, rhs0_ref, rhs1_ref, shift_ref, gram_ref, gain_ref, key_ref, value_ref, *refs
):
    out_refs, query_ref = refs[:-1], refs[-1]
    rows = x_ref.shape[1]
    x = x_ref[first * rows : (first + len(out_refs)) * rows, :]
    xx = jnp.concatenate([x, x], 1)
    scales = token_scales(x, xx, gram_ref)
    block_queries(n, own, x, xx, scales, (rhs0_ref, rhs1_ref), shift_ref, gain_ref, query_ref)
    attention(query_ref, key_ref, value_ref, out_refs)


def attend(n, frames, first, count, x, rhs0, rhs1, shift, gram, gain, key, value):
    heads = key.shape[0]
    rows = x.shape[1]
    return pl.pallas_call(
        lambda *refs: attend_kernel(n, frames // n, first, *refs),
        out_shape=(jax.ShapeDtypeStruct((2 * rows, heads * HS), BF16),) * count,
        in_specs=[vmem_spec()] * 8,
        out_specs=(vmem_spec(),) * count,
        scratch_shapes=[VMEM((heads, count * 2 * rows, HS), BF16)],
        compiler_params=params(20),
        cost_estimate=cost(heads * rows * HS, 2 * nbytes(x)),
        name="attend",
    )(x, rhs0, rhs1, shift, gram, gain, key, value)


def place(block, k, out_ref, sem):
    width = block.shape[1]
    at = pl.multiple_of((lax.axis_index("ctx") ^ k) * width, width)
    return pltpu.make_async_copy(block, out_ref.at[:, pl.ds(at, width)], sem)


def own_kernel(
    n,
    own,
    far,
    far_ref,
    x_ref,
    rhs0_ref,
    rhs1_ref,
    shift_ref,
    gram_ref,
    gain_ref,
    key_ref,
    value_ref,
    out_ref,
    query_ref,
    block_ref,
    sem,
):
    first = place(far_ref, far, out_ref, sem.at[0])
    first.start()
    attend_kernel(
        n,
        own,
        n - 1,
        x_ref,
        rhs0_ref,
        rhs1_ref,
        shift_ref,
        gram_ref,
        gain_ref,
        key_ref,
        value_ref,
        block_ref,
        query_ref,
    )
    second = place(block_ref, 0, out_ref, sem.at[1])
    second.start()
    first.wait()
    second.wait()


def own_block(n, frames, far, far_block, x, rhs0, rhs1, shift, gram, gain, key, value):
    heads = key.shape[0]
    rows = x.shape[1]
    width = heads * HS
    return pl.pallas_call(
        lambda *refs: own_kernel(n, frames // n, far, *refs),
        out_shape=jax.ShapeDtypeStruct((2 * rows, n * width), BF16),
        in_specs=[vmem_spec()] * 9,
        out_specs=hbm_spec(),
        scratch_shapes=[
            VMEM((heads, 2 * rows, HS), BF16),
            VMEM((2 * rows, width), BF16),
            pltpu.SemaphoreType.DMA((2,)),
        ],
        compiler_params=params(12),
        cost_estimate=cost(heads * rows * HS, 2 * nbytes(x)),
        name="own_block",
    )(far_block, x, rhs0, rhs1, shift, gram, gain, key, value)


def rest_kernel(order, out_in_ref, *refs):
    n = len(order)
    out_ref, sem = refs[n:]
    copies = [place(refs[j], k, out_ref, sem.at[j]) for j, k in enumerate(order)]
    for c in copies:
        c.start()
    for c in copies:
        c.wait()


def rest(order, out, blocks):
    n = len(order)
    return pl.pallas_call(
        lambda *refs: rest_kernel(order, *refs),
        out_shape=jax.ShapeDtypeStruct(out.shape, BF16),
        in_specs=[hbm_spec()] + [vmem_spec()] * n,
        out_specs=hbm_spec(),
        scratch_shapes=[pltpu.SemaphoreType.DMA((n,))],
        input_output_aliases={0: 0},
        compiler_params=params(4),
        cost_estimate=cost(0, 2 * n * nbytes(blocks[0])),
        name="rest",
    )(out, *blocks)


def shards(video, conv_weight, latent_weight, embed_weight, modulation, qkv_weight, qk_gain, text, text_weight):
    n = lax.axis_size("ctx")
    frames = video.shape[0]

    def swap(x, k):
        return lax.ppermute(x, "ctx", [(i, i ^ k) for i in range(n)])

    weight = qkv_weight.transpose(1, 0, 2)
    edge_row, e_near, mod_near = edge(video, embed_weight, modulation)
    halo = lax.ppermute(edge_row, "ctx", [(i, (i + 1) % n) for i in range(n)])
    lhs, gram, part, stream, last, tile, taps = text_side(
        e_near,
        mod_near,
        text,
        text_weight,
        video,
        conv_weight.reshape(-1, conv_weight.shape[-1]),
    )
    patches, weight_near = conv_side(tile, halo, taps, latent_weight, weight, weight.shape[1] // 2)
    order = tuple(range(n - 1, -1, -1))
    received = [swap(patches, k) if k else patches for k in order]
    rhs0, rhs1, shift, tkey, tvalue = fold(lhs, qk_gain, weight_near, part, stream, last, weight)
    block, x, key, value = first_block(
        order, frames, received, rhs0, rhs1, shift, gram, qk_gain, tkey, tvalue
    )
    far_block = swap(block, order[0])
    common = (x, rhs0, rhs1, shift, gram, qk_gain, key, value)
    blocks = [swap(b, k) for b, k in zip(attend(n, frames, 1, n - 2, *common), order[1:])]
    out = own_block(n, frames, order[0], far_block, *common)
    return rest(order[1 : n - 1], out, blocks)


def solution(mesh):
    in_specs = (
        P("dp", "ctx", None, None),
        P(),
        P(),
        P(),
        P("dp", None),
        P(None, None, "ctx"),
        P(),
        P("dp", None),
        P(None, None, "ctx"),
    )
    out_specs = P(("dp", "ctx"), None)
    return jax.shard_map(shards, mesh=mesh, in_specs=in_specs, out_specs=out_specs, check_vma=False)
```

```python
import math

import jax
import jax.numpy as jnp
from jax import lax
from jax.experimental import pallas as pl
from jax.experimental.pallas import tpu as pltpu
from jax.sharding import PartitionSpec as P

HS = 128
EPS = 1e-06
F32 = jnp.float32
BF16 = jnp.bfloat16
VMEM = pltpu.VMEM
MIB = 1024 * 1024


def vmem_spec():
    return pl.BlockSpec(memory_space=pltpu.VMEM)


def hbm_spec():
    return pl.BlockSpec(memory_space=pltpu.HBM)


def far(x):
    return pltpu.with_memory_space_constraint(x, pltpu.HBM)


def params(mib):
    return pltpu.CompilerParams(vmem_limit_bytes=mib * MIB)


def cost(flops, bytes_accessed, transcendentals=0):
    return pl.CostEstimate(
        flops=int(flops), bytes_accessed=int(bytes_accessed), transcendentals=int(transcendentals)
    )


def nbytes(*arrays):
    return sum(math.prod(a.shape) * a.dtype.itemsize for a in arrays)


def split(x):
    hi = x.astype(BF16)
    return hi, (x - hi.astype(F32)).astype(BF16)


def dot(a, b):
    return jnp.dot(a, b, preferred_element_type=F32)


def dot_nt(a, b):
    return lax.dot_general(a, b, (((1,), (1,)), ((), ())), preferred_element_type=F32)


def head_norm(v, gain):
    return (v * lax.rsqrt(jnp.mean(v * v, -1, keepdims=True) + EPS) * gain).astype(BF16)


def edge_kernel(video_hbm, e_hbm, mod_hbm, halo_ref, e_ref, mod_ref, sem):
    rows = video_hbm.shape[1]
    pairs = (
        (video_hbm.at[:, pl.ds(rows - 1, 1)], halo_ref),
        (e_hbm, e_ref),
        (mod_hbm, mod_ref),
    )
    copies = [pltpu.make_async_copy(src, dst, sem.at[i]) for i, (src, dst) in enumerate(pairs)]
    for c in copies:
        c.start()
    for c in copies:
        c.wait()


def edge(video, embed_weight, modulation):
    frames, _, cols, chans = video.shape
    return pl.pallas_call(
        edge_kernel,
        out_shape=(
            jax.ShapeDtypeStruct((frames, 1, cols, chans), BF16),
            jax.ShapeDtypeStruct(embed_weight.shape, BF16),
            jax.ShapeDtypeStruct(modulation.shape, F32),
        ),
        in_specs=[hbm_spec()] * 3,
        out_specs=(vmem_spec(),) * 3,
        scratch_shapes=[pltpu.SemaphoreType.DMA((3,))],
        compiler_params=params(4),
        cost_estimate=cost(0, 2 * nbytes(embed_weight, modulation)),
        name="edge",
    )(*[far(a) for a in (video, embed_weight, modulation)])


def add_text(stream, flat, acc_ref, fresh):
    step = 128
    row = lax.broadcasted_iota(jnp.int32, (2 * step, 2 * step), 0)
    col = lax.broadcasted_iota(jnp.int32, (2 * step, 2 * step), 1)
    pick = jnp.where(col == 2 * (row % step) + row // step, 1.0, 0.0).astype(BF16)
    pieces = ([], [])
    for at in range(0, flat.shape[0], 2 * step):
        both = dot(pick, flat[at : at + 2 * step, :]).astype(BF16)
        pieces[0].append(both[:step])
        pieces[1].append(both[step:])
    for p in range(2):
        term = dot(stream, jnp.concatenate(pieces[p], 0))
        if fresh:
            acc_ref[p] = term
        else:
            acc_ref[p] += term


def embed_side(e_ref, mod_ref, lhs_ref, gram_ref, centred_ref):
    pi, depth = e_ref.shape
    few = 16
    for r in range(0, pi, few):
        e = e_ref[r : r + few, :].astype(F32)
        centred = e - jnp.mean(e, -1, keepdims=True)
        lhs_ref[r : r + few, :] = (centred * (1.0 + mod_ref[1:2, :])).astype(BF16)
        centred = centred.astype(BF16)
        centred_ref[r : r + few, :] = centred
        centred_ref[pi + r : pi + r + few, :] = centred
    shift_hi, shift_lo = split(mod_ref[0:1, :])
    lhs_ref[pi:, :] = jnp.concatenate(
        [shift_hi.astype(F32), shift_lo.astype(F32), jnp.zeros((few - 2, depth), F32)], 0
    ).astype(BF16)
    gram = dot_nt(centred_ref[...], centred_ref[...])
    row = lax.broadcasted_iota(jnp.int32, gram.shape, 0) // pi
    col = lax.broadcasted_iota(jnp.int32, gram.shape, 1) // pi
    ghi, glo = split(jnp.where(row == col, gram * (1.0 / depth), 0.0))
    gram_ref[...] = jnp.concatenate([ghi, glo], 0)


def text_kernel(
    chunks,
    e_ref,
    mod_ref,
    text_hbm,
    w_hbm,
    video_hbm,
    conv_hbm,
    lhs_ref,
    gram_ref,
    acc_ref,
    stream_ref,
    last_ref,
    video_ref,
    conv_ref,
    text_ref,
    centred_ref,
    w_ref,
    sem,
    w_sem,
):
    depth, parts, width = w_hbm.shape
    taken = w_ref.shape[0]
    deep = taken // chunks
    copies = [
        pltpu.make_async_copy(w_hbm.at[pl.ds(c * deep, deep)], w_ref.at[pl.ds(c * deep, deep)], w_sem.at[c])
        for c in range(chunks)
    ]
    first = pltpu.make_async_copy(text_hbm, text_ref, sem.at[3])
    pairs = (
        (video_hbm, video_ref),
        (conv_hbm, conv_ref),
        (w_hbm.at[pl.ds(taken, depth - taken)], last_ref),
    )
    ahead = [pltpu.make_async_copy(src, dst, sem.at[i]) for i, (src, dst) in enumerate(pairs)]
    first.start()
    for c in copies:
        c.start()
    embed_side(e_ref, mod_ref, lhs_ref, gram_ref, centred_ref)
    first.wait()
    for copy in ahead:
        copy.start()
    few = 32
    for r in range(0, text_ref.shape[0], few):
        text = text_ref[r : r + few, :].astype(F32)
        centred = text - jnp.mean(text, -1, keepdims=True)
        normed = centred * lax.rsqrt(jnp.mean(centred * centred, -1, keepdims=True) + EPS)
        stream_ref[r : r + few, :] = (normed * (1.0 + mod_ref[3:4, :]) + mod_ref[2:3, :]).astype(BF16)
    flat = w_ref.reshape(taken * parts, width)
    for c in range(chunks):
        copies[c].wait()
        at = slice(c * deep, (c + 1) * deep)
        add_text(stream_ref[:, at], flat.at[2 * c * deep : 2 * (c + 1) * deep], acc_ref, c == 0)
    for c in ahead:
        c.wait()


def text_side(embed_weight, modulation, text, weight, video, conv_weight):
    depth, parts, width = weight.shape
    count = text.shape[0]
    pi = embed_weight.shape[0]
    taken = depth * 2 // 3
    chunks = 2
    return pl.pallas_call(
        lambda *refs: text_kernel(chunks, *refs),
        out_shape=(
            jax.ShapeDtypeStruct((pi + 16, depth), BF16),
            jax.ShapeDtypeStruct((4 * pi, 2 * pi), BF16),
            jax.ShapeDtypeStruct((parts, count, width), F32),
            jax.ShapeDtypeStruct(text.shape, BF16),
            jax.ShapeDtypeStruct((depth - taken, parts, width), BF16),
            jax.ShapeDtypeStruct(video.shape, BF16),
            jax.ShapeDtypeStruct(conv_weight.shape, BF16),
        ),
        in_specs=[vmem_spec()] * 2 + [hbm_spec()] * 4,
        out_specs=(vmem_spec(),) * 7,
        scratch_shapes=[
            VMEM(text.shape, BF16),
            VMEM((2 * pi, depth), BF16),
            VMEM((taken, parts, width), BF16),
            pltpu.SemaphoreType.DMA((4,)),
            pltpu.SemaphoreType.DMA((chunks,)),
        ],
        compiler_params=params(20),
        cost_estimate=cost(4 * count * depth * parts * width, nbytes(weight, text, video, conv_weight)),
        name="text_side",
    )(embed_weight, modulation, *[far(a) for a in (text, weight, video, conv_weight)])


def fold_kernel(
    lhs_ref,
    gain_ref,
    w0_ref,
    part_ref,
    stream_ref,
    last_ref,
    w_hbm,
    rhs0_ref,
    rhs1_ref,
    shift_ref,
    key_ref,
    value_ref,
    acc_ref,
    sum_ref,
    w1_ref,
    sem,
):
    parts, deep0, width = w0_ref.shape
    depth = lhs_ref.shape[1]
    pi = lhs_ref.shape[0] - 16
    copies = [
        pltpu.make_async_copy(w_hbm.at[p, pl.ds(deep0, depth - deep0)], w1_ref.at[p], sem.at[p])
        for p in range(parts)
    ]
    for c in copies:
        c.start()
    last, _, _ = last_ref.shape
    add_text(stream_ref[:, depth - last :], last_ref.reshape(2 * last, width), sum_ref, True)
    for h in range(width // HS):
        at = slice(h * HS, (h + 1) * HS)
        key_ref[h] = head_norm(part_ref[0, :, at] + sum_ref[0, :, at], gain_ref[1:2, :])
        value_ref[h] = (part_ref[1, :, at] + sum_ref[1, :, at]).astype(BF16)
    for p in range(parts):
        at = slice(p * width, (p + 1) * width)
        acc_ref[:, at] = dot(lhs_ref[:, :deep0], w0_ref[p])
    for p in range(parts):
        at = slice(p * width, (p + 1) * width)
        copies[p].wait()
        acc_ref[:, at] += dot(lhs_ref[:, deep0:], w1_ref[p])
    total = acc_ref[...]
    hi, lo = split(total[:pi])
    none = jnp.zeros_like(hi)
    rhs0_ref[...] = jnp.concatenate([hi, none, lo, none], 0)
    rhs1_ref[...] = jnp.concatenate([none, hi, none, lo], 0)
    shift_ref[...] = total[pi : pi + 1] + total[pi + 1 : pi + 2]


def fold(lhs, gain, weight0, part, stream, last, weight):
    parts, taken, width = weight0.shape
    rows, depth = lhs.shape
    cols = parts * width
    count = stream.shape[0]
    heads = width // HS
    return pl.pallas_call(
        fold_kernel,
        out_shape=(
            jax.ShapeDtypeStruct((4 * (rows - 16), cols), BF16),
            jax.ShapeDtypeStruct((4 * (rows - 16), cols), BF16),
            jax.ShapeDtypeStruct((1, cols), F32),
            jax.ShapeDtypeStruct((heads, count, HS), BF16),
            jax.ShapeDtypeStruct((heads, count, HS), BF16),
        ),
        in_specs=[vmem_spec()] * 6 + [hbm_spec()],
        out_specs=(vmem_spec(),) * 5,
        scratch_shapes=[
            VMEM((rows, cols), F32),
            VMEM(part.shape, F32),
            VMEM((parts, depth - taken, width), BF16),
            pltpu.SemaphoreType.DMA((parts,)),
        ],
        compiler_params=params(20),
        cost_estimate=cost(2 * 144 * depth * cols, nbytes(weight)),
        name="fold",
    )(lhs, gain, weight0, part, stream, last, far(weight))


def conv_kernel(
    chunks,
    video_ref,
    halo_ref,
    weight_ref,
    latent_ref,
    qkv_hbm,
    out_ref,
    qkv_ref,
    wide_ref,
    even_ref,
    odd_ref,
    left_ref,
    spread_ref,
    sem,
):
    deep = qkv_ref.shape[1] // chunks
    ahead = [
        pltpu.make_async_copy(
            qkv_hbm.at[p, pl.ds(c * deep, deep)], qkv_ref.at[p, pl.ds(c * deep, deep)], sem.at[p, c]
        )
        for p in range(qkv_ref.shape[0])
        for c in range(chunks)
    ]
    for copy in ahead:
        copy.start()
    frames, rows, cols, chans = video_ref.shape
    block = cols + 8
    half = cols // 2
    quarter = cols // 4
    for r in range(rows + 1):
        for f in range(frames):
            base = (r * frames + f) * block
            pixels = (halo_ref[f, 0] if r == 0 else video_ref[f, r - 1]).astype(F32)
            if r == 0:
                pixels = jnp.where(lax.axis_index("ctx") == 0, 0.0, pixels)
            wide_ref[base : base + 8, :] = jnp.zeros((8, chans), F32)
            wide_ref[base + 8 : base + block, :] = pixels
            at = [wide_ref[pl.ds(base + 7 + o, quarter, stride=4), :] for o in range(5)]
            even = jnp.concatenate([at[1], at[3]], 0).astype(BF16)
            odd = jnp.concatenate([at[2], at[4]], 0).astype(BF16)
            left = jnp.concatenate([at[0], at[2]], 0).astype(BF16)
            for t in (range(3) if f == 0 else (f + 2,)):
                even_ref[r, t] = even
                odd_ref[r, t] = odd
                left_ref[r, t] = left
    lat, mid = latent_ref.shape
    tall = rows // 2
    spread_ref[...] = jnp.zeros_like(spread_ref)
    for s in range(2 * tall):
        spread_ref[s * lat : (s + 1) * lat, s * mid : (s + 1) * mid] = latent_ref[...]
    pieces = []
    for j in range(tall):
        taps = []
        for kt in range(3):
            for kr in range(3):
                for ref in (left_ref, even_ref, odd_ref):
                    taps.append(ref[2 * j + kr, kt : kt + frames].reshape(frames * half, chans))
        conv = dot(jnp.concatenate(taps, 1), weight_ref[...])
        act = (conv * (1.0 / (1.0 + jnp.exp(-conv)))).astype(BF16)
        for b in range(2):
            pieces.append(
                jnp.concatenate(
                    [act[f * half + b * quarter : f * half + (b + 1) * quarter] for f in range(frames)], 0
                )
            )
    out_ref[...] = dot_nt(jnp.concatenate(pieces, 1), spread_ref[...]).astype(BF16)
    for copy in ahead:
        copy.wait()


def conv_side(video, halo, weight, latent_weight, qkv_weight, taken):
    frames, rows, cols, chans = video.shape
    parts, depth, width = qkv_weight.shape
    mid = weight.shape[-1]
    lat = latent_weight.shape[1]
    latent = latent_weight.T
    half = cols // 2
    tall = rows // 2
    chunks = 1
    return pl.pallas_call(
        lambda *refs: conv_kernel(chunks, *refs),
        out_shape=(
            jax.ShapeDtypeStruct((frames * half // 2, 2 * tall * lat), BF16),
            jax.ShapeDtypeStruct((parts, taken, width), BF16),
        ),
        in_specs=[vmem_spec()] * 4 + [hbm_spec()],
        out_specs=(vmem_spec(),) * 2,
        scratch_shapes=[VMEM(((rows + 1) * frames * (cols + 8), chans), F32)]
        + [VMEM((rows + 1, frames + 2, half, chans), BF16)] * 3
        + [VMEM((2 * tall * lat, 2 * tall * mid), BF16), pltpu.SemaphoreType.DMA((parts, chunks))],
        compiler_params=params(24),
        cost_estimate=cost(
            2 * frames * tall * half * 27 * chans * mid, nbytes(video, halo, weight)
        ),
        name="conv_side",
    )(video, halo, weight, latent, far(qkv_weight))


def token_scales(x, xx, gram_ref):
    quad = dot(xx, gram_ref[...]) * x.astype(F32)
    lane = lax.broadcasted_iota(jnp.int32, quad.shape, 1)
    low = lane < quad.shape[1] // 2
    scales = []
    for i in range(2):
        var = jnp.sum(jnp.where(low if i == 0 else ~low, quad, 0.0), -1, keepdims=True)
        scales.append(lax.rsqrt(jnp.maximum(var, 0.0) + EPS))
    return scales


def block_queries(n, own, x, xx, scales, rhs_refs, shift_ref, gain_ref, query_ref):
    heads = query_ref.shape[0]
    rows = x.shape[1]
    span = rows // n
    grain = span // own
    gain = gain_ref[0:1, :] * (math.log2(math.e) / math.sqrt(HS))
    for i in range(2):
        at = slice(0, heads * HS)
        projected = dot(xx, rhs_refs[i][:, at]) * scales[i] + shift_ref[:, at]
        for h in range(heads):
            v = head_norm(projected[:, h * HS : (h + 1) * HS], gain)
            for j in range(x.shape[0] // rows):
                for s in range(n):
                    for f in range(own):
                        to = 2 * j * rows + f * (n * 2 * grain) + (s * 2 + i) * grain
                        come = j * rows + s * span + f * grain
                        query_ref[h, to : to + grain, :] = v[come : come + grain]


def attention(query_ref, key_ref, value_ref, out_refs):
    heads, total, _ = key_ref.shape
    rows = query_ref.shape[1] // len(out_refs)
    for j in range(0, len(out_refs), 2):
        group = out_refs[j : j + 2]
        for h in range(heads):
            query = query_ref[h, j * rows : (j + len(group)) * rows, :]
            weights = jnp.exp2(dot_nt(query, key_ref[h]))
            norm = weights[:, :HS]
            for c in range(HS, total, HS):
                norm = norm + weights[:, c : c + HS]
            norm = jnp.sum(norm, -1, keepdims=True)
            attended = (dot(weights.astype(BF16), value_ref[h]) * (1.0 / norm)).astype(BF16)
            for g, ref in enumerate(group):
                ref[:, h * HS : (h + 1) * HS] = attended[g * rows : (g + 1) * rows]


def first_kernel(order, frames, *refs):
    n = len(order)
    patch_refs = refs[:n]
    rhs0_ref, rhs1_ref, shift_ref, gram_ref, gain_ref, tkey_ref, tvalue_ref = refs[n : n + 7]
    out_ref, x_ref, key_ref, value_ref, patch_scr, query_ref = refs[n + 7 :]
    me = lax.axis_index("ctx")
    rhs_refs = (rhs0_ref, rhs1_ref)
    heads, count, _ = tkey_ref.shape
    rows = patch_refs[0].shape[1]
    for k, ref in zip(order, patch_refs):
        patch_scr[pl.ds(pl.multiple_of((me ^ k) * rows, rows), rows), :] = ref[...]
    key_ref[:, 0:count, :] = tkey_ref[...]
    value_ref[:, 0:count, :] = tvalue_ref[...]
    own = frames // n
    span = rows // n
    for j, k in enumerate(order):
        for s in range(n):
            at = pl.multiple_of((me ^ k) * span, span) + s * rows
            x_ref[j * rows + s * span : j * rows + (s + 1) * span, :] = patch_scr[
                pl.ds(pl.multiple_of(at, span), span), :
            ]
    x = x_ref[...]
    xx = jnp.concatenate([x, x], 1)
    scales = token_scales(x, xx, gram_ref)
    width = heads * HS
    for i in range(2):
        for p in (1, 2):
            for h0 in range(0, heads, 2):
                at = slice(p * width + h0 * HS, p * width + (h0 + 2) * HS)
                pair = dot(xx, rhs_refs[i][:, at]) * scales[i] + shift_ref[:, at]
                for h in (h0, h0 + 1):
                    v = pair[:, (h - h0) * HS : (h - h0 + 1) * HS]
                    to = slice(count + i * n * rows, count + (i + 1) * n * rows)
                    if p == 1:
                        key_ref[h, to, :] = head_norm(v, gain_ref[1:2, :])
                    else:
                        value_ref[h, to, :] = v.astype(BF16)
    block_queries(
        n, own, x[:rows], xx[:rows], [v[:rows] for v in scales], rhs_refs, shift_ref, gain_ref, query_ref
    )
    attention(query_ref, key_ref, value_ref, (out_ref,))


def first_block(order, frames, patches, rhs0, rhs1, shift, gram, gain, tkey, tvalue):
    n = len(order)
    heads, count, _ = tkey.shape
    rows = patches[0].shape[1]
    total = count + 2 * n * rows
    return pl.pallas_call(
        lambda *refs: first_kernel(order, frames, *refs),
        out_shape=(
            jax.ShapeDtypeStruct((2 * rows, heads * HS), BF16),
            jax.ShapeDtypeStruct((n * rows, rows), BF16),
            jax.ShapeDtypeStruct((heads, total, HS), BF16),
            jax.ShapeDtypeStruct((heads, total, HS), BF16),
        ),
        in_specs=[vmem_spec()] * (n + 7),
        out_specs=(vmem_spec(),) * 4,
        scratch_shapes=[VMEM((n * rows, rows), BF16), VMEM((heads, 2 * rows, HS), BF16)],
        compiler_params=params(16),
        cost_estimate=cost(2 * 2 * n * rows * 256 * 3 * heads * HS, 4 * nbytes(rhs0)),
        name="first_block",
    )(*patches, rhs0, rhs1, shift, gram, gain, tkey, tvalue)


def attend_kernel(
    n, own, first, x_ref, rhs0_ref, rhs1_ref, shift_ref, gram_ref, gain_ref, key_ref, value_ref, *refs
):
    out_refs, query_ref = refs[:-1], refs[-1]
    rows = x_ref.shape[1]
    x = x_ref[first * rows : (first + len(out_refs)) * rows, :]
    xx = jnp.concatenate([x, x], 1)
    scales = token_scales(x, xx, gram_ref)
    block_queries(n, own, x, xx, scales, (rhs0_ref, rhs1_ref), shift_ref, gain_ref, query_ref)
    attention(query_ref, key_ref, value_ref, out_refs)


def attend(n, frames, first, count, x, rhs0, rhs1, shift, gram, gain, key, value):
    heads = key.shape[0]
    rows = x.shape[1]
    return pl.pallas_call(
        lambda *refs: attend_kernel(n, frames // n, first, *refs),
        out_shape=(jax.ShapeDtypeStruct((2 * rows, heads * HS), BF16),) * count,
        in_specs=[vmem_spec()] * 8,
        out_specs=(vmem_spec(),) * count,
        scratch_shapes=[VMEM((heads, count * 2 * rows, HS), BF16)],
        compiler_params=params(20),
        cost_estimate=cost(heads * rows * HS, 2 * nbytes(x)),
        name="attend",
    )(x, rhs0, rhs1, shift, gram, gain, key, value)


def place(block, k, out_ref, sem):
    width = block.shape[1]
    at = pl.multiple_of((lax.axis_index("ctx") ^ k) * width, width)
    return pltpu.make_async_copy(block, out_ref.at[:, pl.ds(at, width)], sem)


def own_kernel(
    n,
    own,
    far,
    far_ref,
    x_ref,
    rhs0_ref,
    rhs1_ref,
    shift_ref,
    gram_ref,
    gain_ref,
    key_ref,
    value_ref,
    out_ref,
    query_ref,
    block_ref,
    sem,
):
    first = place(far_ref, far, out_ref, sem.at[0])
    first.start()
    attend_kernel(
        n,
        own,
        n - 1,
        x_ref,
        rhs0_ref,
        rhs1_ref,
        shift_ref,
        gram_ref,
        gain_ref,
        key_ref,
        value_ref,
        block_ref,
        query_ref,
    )
    second = place(block_ref, 0, out_ref, sem.at[1])
    second.start()
    first.wait()
    second.wait()


def own_block(n, frames, far, far_block, x, rhs0, rhs1, shift, gram, gain, key, value):
    heads = key.shape[0]
    rows = x.shape[1]
    width = heads * HS
    return pl.pallas_call(
        lambda *refs: own_kernel(n, frames // n, far, *refs),
        out_shape=jax.ShapeDtypeStruct((2 * rows, n * width), BF16),
        in_specs=[vmem_spec()] * 9,
        out_specs=hbm_spec(),
        scratch_shapes=[
            VMEM((heads, 2 * rows, HS), BF16),
            VMEM((2 * rows, width), BF16),
            pltpu.SemaphoreType.DMA((2,)),
        ],
        compiler_params=params(12),
        cost_estimate=cost(heads * rows * HS, 2 * nbytes(x)),
        name="own_block",
    )(far_block, x, rhs0, rhs1, shift, gram, gain, key, value)


def rest_kernel(order, out_in_ref, *refs):
    n = len(order)
    out_ref, sem = refs[n:]
    copies = [place(refs[j], k, out_ref, sem.at[j]) for j, k in enumerate(order)]
    for c in copies:
        c.start()
    for c in copies:
        c.wait()


def rest(order, out, blocks):
    n = len(order)
    return pl.pallas_call(
        lambda *refs: rest_kernel(order, *refs),
        out_shape=jax.ShapeDtypeStruct(out.shape, BF16),
        in_specs=[hbm_spec()] + [vmem_spec()] * n,
        out_specs=hbm_spec(),
        scratch_shapes=[pltpu.SemaphoreType.DMA((n,))],
        input_output_aliases={0: 0},
        compiler_params=params(4),
        cost_estimate=cost(0, 2 * n * nbytes(blocks[0])),
        name="rest",
    )(out, *blocks)


def shards(video, conv_weight, latent_weight, embed_weight, modulation, qkv_weight, qk_gain, text, text_weight):
    n = lax.axis_size("ctx")
    frames = video.shape[0]

    def swap(x, k):
        return lax.ppermute(x, "ctx", [(i, i ^ k) for i in range(n)])

    weight = qkv_weight.transpose(1, 0, 2)
    edge_row, e_near, mod_near = edge(video, embed_weight, modulation)
    halo = lax.ppermute(edge_row, "ctx", [(i, (i + 1) % n) for i in range(n)])
    lhs, gram, part, stream, last, tile, taps = text_side(
        e_near,
        mod_near,
        text,
        text_weight,
        video,
        conv_weight.reshape(-1, conv_weight.shape[-1]),
    )
    patches, weight_near = conv_side(tile, halo, taps, latent_weight, weight, weight.shape[1] // 2)
    order = tuple(range(n - 1, -1, -1))
    received = [swap(patches, k) if k else patches for k in order]
    rhs0, rhs1, shift, tkey, tvalue = fold(lhs, qk_gain, weight_near, part, stream, last, weight)
    block, x, key, value = first_block(
        order, frames, received, rhs0, rhs1, shift, gram, qk_gain, tkey, tvalue
    )
    far_block = swap(block, order[0])
    common = (x, rhs0, rhs1, shift, gram, qk_gain, key, value)
    blocks = [swap(b, k) for b, k in zip(attend(n, frames, 1, n - 2, *common), order[1:])]
    out = own_block(n, frames, order[0], far_block, *common)
    return rest(order[1 : n - 1], out, blocks)


def solution(mesh):
    in_specs = (
        P("dp", "ctx", None, None),
        P(),
        P(),
        P(),
        P("dp", None),
        P(None, None, "ctx"),
        P(),
        P("dp", None),
        P(None, None, "ctx"),
    )
    out_specs = P(("dp", "ctx"), None)
    return jax.shard_map(shards, mesh=mesh, in_specs=in_specs, out_specs=out_specs, check_vma=False)
```
